256 devices in a mesh: grp: 2 (over core), dom: 64 (over y_lo, z, x), sub: 2 (over y_hi).
Axes of the slice: x: 4, y: 4 (y_hi: 2, y_lo: 2; y = y_hi * 2 + y_lo), z: 8, core: 2. Of those that a mesh axis runs over, the one named last changes fastest.
Arguments:
- positions: float32 [3, 65536], P(None, ('grp', 'dom', 'sub')), may hold values from 0 to 4
- charges: float32 [65536], P(('grp', 'dom', 'sub')), may hold values from -3 to 3
- polar: float32 [65536], P(('grp', 'dom', 'sub')), may hold values from 0.1 to 0.6
- features: bfloat16 [65536, 256], P(('grp', 'dom', 'sub')), may hold values from -6 to 6
- neighbours: int32 [65536, 32], P(('grp', 'dom', 'sub')), may hold values from 0 to 512, as said below
- send_rows: int32 [2, 32768], P(None, ('grp', 'dom', 'sub')), may hold values from 0 to 255
- blocks: int32 [1024], P(('grp', 'dom', 'sub')), may hold values from 0 to 255
- radial_in: bfloat16 [2, 8, 64], replicated, may hold values from -2 to 2
- radial_mid: bfloat16 [2, 2, 64, 64], replicated, may hold values from -0.75 to 0.75
- radial_out: bfloat16 [2, 64, 256], replicated, may hold values from -0.75 to 0.75
- node_in: bfloat16 [2, 256, 256], replicated, may hold values from -0.375 to 0.375
- node_out: bfloat16 [2, 256, 256], replicated, may hold values from -0.375 to 0.375
- field_gain: float32 [256], replicated, may hold values from -3 to 3
- readout: bfloat16 [256, 2], replicated, may hold values from -0.375 to 0.375
Outputs:
- site_result: float32 [3, 65536], P(None, ('grp', 'dom', 'sub'))
- response: float32 [3, 65536], P(None, ('grp', 'dom', 'sub'))
The draws below stay inside these ranges and needn't reach their ends.
Inputs may be any that keep to these rules, and one draw needn't show every extreme that they name: `neighbours`: entries below 256 name the block's own sites, entries from 256 to 511 its lent sites, 512 an empty slot; empty slots follow the used ones. `blocks`: repeats may occur.
All inputs are finite; a program needn't handle non-finite values.
Results may differ from the reference program's by a relative error of at most 0.0022.
The reference program's roundings to bfloat16 on the way count: a program that leaves them out, or rounds other values in their place, can miss the bound.
Values may be sent and summed in bfloat16 or wider, within the bound.
No kernel may reach another device: no remote copies, remote signals or barrier semaphores. Data moves between devices by JAX's collectives and lax.ppermute only.
A program may use at most 64 MiB of HBM per device.

```python
import math
import jax
import jax.numpy as jnp
from jax import lax

CHANNELS = 256
RADIAL = 64
BASIS = 8
NEIGHBOURS = 32
LAYERS = 2
SWEEPS = 4
ROWS = 256
HALO = 128
BLOCK = 128
LISTED = 4
SITES = 65536
RIMS = 32768
LISTS = 1024
NBLOCKS = 256
N_DOM = 64
N_SUB = 2


def draw_neighbours(key, part):
    pick_key, count_key, rim_key, side_key = jax.random.split(jax.random.fold_in(key, 17), 4)
    own_pick = jax.random.randint(pick_key, (SITES, NEIGHBOURS), 0, ROWS)
    rim_pick = ROWS + jax.random.randint(rim_key, (SITES, NEIGHBOURS), 0, 2 * HALO)
    coin = jax.random.randint(side_key, (SITES, NEIGHBOURS), 0, 4)
    picked = jnp.where(coin < 3, rim_pick, own_pick)
    counts = jax.random.randint(count_key, (SITES, 1), NEIGHBOURS // 2, NEIGHBOURS + 1)
    slot_index = lax.broadcasted_iota(jnp.int32, (SITES, NEIGHBOURS), 1)
    return jnp.where(slot_index < counts, picked, ROWS + 2 * HALO).astype(jnp.int32)


def with_ends(result, stream_key, low, high):
    longest = result.shape.index(max(result.shape))
    spots = []
    for shift in (0, 1):
        where = [jax.random.randint(jax.random.fold_in(stream_key, axis), (), 0, length) for axis, length in enumerate(result.shape)]
        where[longest] = (where[longest] + shift) % result.shape[longest]
        spots.append(tuple(where))
    return result.at[spots[0]].set(low).at[spots[1]].set(high)


def block_scale(own_key, extent, pieces, smallest, top_value):
    level, own = 1.0, jax.random.fold_in(own_key, 6)
    for position, blocks in pieces:
        heights = jnp.exp(jax.random.uniform(jax.random.fold_in(own, position), (blocks,), jnp.float32, smallest / len(pieces), top_value / len(pieces)))
        level = level * jnp.repeat(heights, extent[position] // blocks).reshape([-1 if axis == position else 1 for axis in range(len(extent))])
    return level


def normal_values(own_key, extent, deviation, reach, pieces=(), kind=jnp.bfloat16):
    values = deviation * jax.random.normal(own_key, extent, jnp.float32)
    if pieces:
        values = values * block_scale(own_key, extent, pieces, -0.22, 0.18)
    return jnp.clip(values, -reach, reach).astype(kind)


def setup_inputs(seed: int = 0) -> dict:
    keys = jax.random.split(jax.random.key(seed), 15)
    return {
        "positions": jnp.clip(4.0 * jax.random.uniform(keys[0], (3, SITES), jnp.float32) ** block_scale(keys[0], (3, SITES), ((1, 256),), -0.2, 0.2), 0.0, 4.0),
        "charges": normal_values(keys[1], (SITES,), 0.5, 3.0, ((0, 256),), jnp.float32),
        "polar": jnp.clip(jnp.exp(math.log(0.6) - 1.7917595 * jax.random.uniform(keys[2], (SITES,), jnp.float32) ** block_scale(keys[2], (SITES,), ((0, 256),), -0.2, 0.2)), 0.1, 0.6),
        "features": normal_values(keys[3], (SITES, CHANNELS), 1.0, 6.0, ((0, 256),)),
        "neighbours": draw_neighbours(jax.random.fold_in(keys[14], 71), 0),
        "send_rows": with_ends(jax.random.randint(keys[5], (2, RIMS), 0, ROWS), jax.random.fold_in(keys[5], 1), 0, ROWS - 1).astype(jnp.int32),
        "blocks": with_ends(jax.random.randint(keys[6], (LISTS,), 0, NBLOCKS), jax.random.fold_in(keys[6], 1), 0, NBLOCKS - 1).astype(jnp.int32),
        "radial_in": normal_values(keys[7], (LAYERS, BASIS, RADIAL), BASIS ** -0.5, 2.0),
        "radial_mid": normal_values(keys[8], (LAYERS, 2, RADIAL, RADIAL), RADIAL ** -0.5, 0.75),
        "radial_out": normal_values(keys[9], (LAYERS, RADIAL, CHANNELS), RADIAL ** -0.5, 0.75),
        "node_in": normal_values(keys[10], (LAYERS, CHANNELS, CHANNELS), CHANNELS ** -0.5, 0.375),
        "node_out": normal_values(keys[11], (LAYERS, CHANNELS, CHANNELS), CHANNELS ** -0.5, 0.375),
        "field_gain": normal_values(keys[12], (CHANNELS,), 0.5, 3.0, (), jnp.float32),
        "readout": normal_values(keys[13], (CHANNELS, 2), CHANNELS ** -0.5, 0.375),
    }


SMOOTH = 1.0
GAMMA = 1.0
SPACING = 0.75

def field_at(target, source, charge, dipole):
    tile_count = target.shape[1] // BLOCK
    tiles = target.reshape(3, tile_count, BLOCK).transpose(1, 0, 2)

    def one_tile(target_tile):
        offset = target_tile[:, :, None] - source[:, None, :]
        dist_sq = lax.optimization_barrier(jnp.sum(offset * offset, axis=0)) + SMOOTH
        inverse = lax.rsqrt(dist_sq)
        inverse_cube = inverse * inverse * inverse
        inverse_fifth = inverse_cube * inverse * inverse
        projected = lax.optimization_barrier(jnp.sum(offset * dipole[:, None, :], axis=0))
        source_scale = charge[None, :] * inverse_cube + 3.0 * projected * inverse_fifth
        return lax.optimization_barrier(jnp.sum(offset * source_scale[None] - dipole[:, None, :] * inverse_cube[None], axis=2))
    return lax.map(one_tile, tiles).transpose(1, 0, 2).reshape(3, -1)

def edge_geometry(local_data, site_table, neighbour_list):
    source = site_table[:3][:, neighbour_list]
    offset = local_data[:3][:, :, None] - source
    dist_sq = lax.optimization_barrier(jnp.sum(offset * offset, axis=0)) + SMOOTH
    return (offset, dist_sq)

def pair_field(offset, dist_sq, source_charge, source_dipole):
    inverse = lax.rsqrt(dist_sq)
    inverse_cube = inverse * inverse * inverse
    inverse_fifth = inverse_cube * inverse * inverse
    projected = lax.optimization_barrier(jnp.sum(offset * source_dipole, axis=0))
    source_scale = source_charge * inverse_cube + 3.0 * projected * inverse_fifth
    return lax.optimization_barrier(jnp.sum(offset * source_scale[None] - source_dipole * inverse_cube[None], axis=2))

def message_update(hidden, lifted_table, radial_basis, neighbour_list, w_first, w_middle, w_last, w_node):
    row_count, channel_count = hidden.shape
    slot_count = neighbour_list.shape[1]
    tile_count = row_count // BLOCK
    basis_tiles = radial_basis.reshape(tile_count, BLOCK * slot_count, radial_basis.shape[2])
    index_tiles = neighbour_list.reshape(tile_count, BLOCK * slot_count)

    def one_tile(operands):
        basis_tile, index_tile = operands
        first_hidden = jax.nn.silu(jnp.dot(basis_tile, w_first, preferred_element_type=jnp.float32)).astype(jnp.bfloat16)
        second_hidden = jax.nn.silu(jnp.dot(first_hidden, w_middle[0], preferred_element_type=jnp.float32)).astype(jnp.bfloat16)
        third_hidden = jax.nn.silu(jnp.dot(second_hidden, w_middle[1], preferred_element_type=jnp.float32)).astype(jnp.bfloat16)
        edge_weight = jnp.dot(third_hidden, w_last, preferred_element_type=jnp.float32)
        source = lifted_table[index_tile].astype(jnp.float32)
        summed = lax.optimization_barrier(jnp.sum((edge_weight * source).reshape(BLOCK, slot_count, channel_count), axis=1))
        return summed / slot_count
    message = lax.map(one_tile, (basis_tiles, index_tiles)).reshape(row_count, channel_count).astype(jnp.bfloat16)
    update = jax.nn.silu(jnp.dot(message, w_node, preferred_element_type=jnp.float32))
    return (hidden.astype(jnp.float32) + update).astype(jnp.bfloat16)

def rim_cols(values, rim_lists):
    to_next = jax.vmap(lambda v, s: v[:, s[0]])(values, rim_lists)
    to_prev = jax.vmap(lambda v, s: v[:, s[1]])(values, rim_lists)
    missing = jnp.zeros_like(to_next[:1])
    lower = jnp.concatenate([missing, to_next[:-1]], 0)
    upper = jnp.concatenate([to_prev[1:], missing], 0)
    empty_entry = jnp.zeros(values.shape[:-1] + (1,), values.dtype)
    return jnp.concatenate([values, lower, upper, empty_entry], -1)

def rim_rows(values, rim_lists):
    to_next = jax.vmap(lambda v, s: v[s[0]])(values, rim_lists)
    to_prev = jax.vmap(lambda v, s: v[s[1]])(values, rim_lists)
    missing = jnp.zeros_like(to_next[:1])
    lower = jnp.concatenate([missing, to_next[:-1]], 0)
    upper = jnp.concatenate([to_prev[1:], missing], 0)
    empty_entry = jnp.zeros((values.shape[0], 1) + values.shape[2:], values.dtype)
    return jnp.concatenate([values, lower, upper, empty_entry], 1)

def reference(positions, charges, polar, features, neighbours, send_rows, blocks, radial_in, radial_mid, radial_out, node_in, node_out, field_gain, readout):
    groups = N_DOM * N_SUB
    local_data = jnp.concatenate([positions, charges[None], polar[None]], 0).reshape(5, 2 * groups, ROWS).transpose(1, 0, 2)
    neighbour_lists = neighbours.reshape(2 * groups, ROWS, NEIGHBOURS)
    rim_lists = send_rows.reshape(2, 2 * groups, HALO).transpose(1, 0, 2)
    block_lists = blocks.reshape(2 * groups, LISTED)
    by_group = local_data.reshape(2, groups, 5, ROWS).transpose(0, 2, 1, 3).reshape(2, 5, groups * ROWS)

    def pick(other, listed):
        return jnp.take(other.reshape(5, -1, BLOCK), listed, axis=1).reshape(5, -1)
    near_learned = jax.vmap(lambda l: pick(by_group[1], l))(block_lists[:groups])
    near_solvent = jax.vmap(lambda l: pick(by_group[0], l))(block_lists[groups:])
    near_sites = jnp.concatenate([near_learned, near_solvent], 0)
    outside = lax.map(lambda a: field_at(a[0][:3], a[1][:3], a[1][3], jnp.zeros_like(a[1][:3])), (local_data, near_sites))
    site_tables = jnp.concatenate([rim_cols(local_data[:groups], rim_lists[:groups]), rim_cols(local_data[groups:], rim_lists[groups:])], 0)
    strength = jnp.sqrt(1.0 + lax.optimization_barrier(jnp.sum(outside * outside, axis=1)))
    learned_offset, learned_dist = jax.vmap(edge_geometry)(local_data[:groups], site_tables[:groups], neighbour_lists[:groups])
    centres = jnp.arange(BASIS, dtype=jnp.float32) * SPACING
    radial_basis = jnp.exp(-GAMMA * (jnp.sqrt(learned_dist)[..., None] - centres) ** 2).astype(jnp.bfloat16)
    initial = features.reshape(2 * groups, ROWS, CHANNELS)[:groups].astype(jnp.float32)
    hidden = (initial + strength[:groups, :, None] * field_gain[None, None, :]).astype(jnp.bfloat16)
    for layer_index in range(LAYERS):
        lifted = lax.map(lambda h: jnp.dot(h, node_in[layer_index], preferred_element_type=jnp.float32).astype(jnp.bfloat16), hidden)
        lifted_tables = rim_rows(lifted, rim_lists[:groups])
        hidden = lax.map(lambda a: message_update(a[0], a[1], a[2], a[3], radial_in[layer_index], radial_mid[layer_index], radial_out[layer_index], node_out[layer_index]), (hidden, lifted_tables, radial_basis, neighbour_lists[:groups]))
    readouts = lax.map(lambda h: jnp.dot(h, readout, preferred_element_type=jnp.float32), hidden)
    solvent_offset, solvent_dist = jax.vmap(edge_geometry)(local_data[groups:], site_tables[groups:], neighbour_lists[groups:])
    source_charge = jax.vmap(lambda t, n: t[3][n])(site_tables[groups:], neighbour_lists[groups:])
    fixed_field = outside[groups:] + jax.vmap(pair_field)(solvent_offset, solvent_dist, source_charge, jnp.zeros_like(solvent_offset))
    polar_rows = local_data[groups:, 4]
    dipole = polar_rows[:, None, :] * fixed_field
    for sweep_index in range(SWEEPS):
        dipole_tables = rim_cols(dipole, rim_lists[groups:])
        gathered = jax.vmap(lambda t, n: t[:, n])(dipole_tables, neighbour_lists[groups:])
        induced = jax.vmap(pair_field)(solvent_offset, solvent_dist, jnp.zeros_like(solvent_dist), gathered)
        dipole = polar_rows[:, None, :] * (fixed_field + induced)
    learned_charge = readouts[:, :, 0]
    source_q = jnp.concatenate([learned_charge, jnp.zeros_like(learned_charge)], 0)
    source_d = jnp.concatenate([jnp.zeros_like(dipole), dipole], 0)
    terms = lax.map(lambda a: field_at(a[0][:3], a[1][:3], a[2], a[3]), (near_sites, local_data, source_q, source_d))

    def collect(part_terms, part_lists):
        flat_terms = part_terms.reshape(groups, 3, LISTED, BLOCK).transpose(1, 0, 2, 3).reshape(3, groups * LISTED, BLOCK)
        summed = jnp.zeros((3, NBLOCKS, BLOCK), jnp.float32).at[:, part_lists.reshape(-1)].add(flat_terms)
        return summed.reshape(3, -1)
    from_learned = collect(terms[:groups], block_lists[:groups])
    from_solvent = collect(terms[groups:], block_lists[groups:])
    response = jnp.concatenate([from_solvent, from_learned], 1)
    learned_rows = jnp.stack([readouts[:, :, 0], readouts[:, :, 1], strength[:groups]], 1)
    site_result = jnp.concatenate([learned_rows, dipole], 0).transpose(1, 0, 2).reshape(3, -1)
    return (site_result, response)
```

```python
import jax
import jax.numpy as jnp
from jax import lax
from jax.experimental import pallas as pl
from jax.experimental.pallas import tpu as pltpu
from jax.sharding import PartitionSpec as P

BASIS = 8
LAYERS = 2
SMOOTH = 1.0
SPACING = 0.75
DOM = ("dom", "sub")
EVERY = ("grp", "dom", "sub")
F32 = jnp.float32
BF16 = jnp.bfloat16
VMEM = pl.BlockSpec(memory_space=pltpu.VMEM)
SMEM = pl.BlockSpec(memory_space=pltpu.SMEM)
CHUNK = 16


def call(body, outs, args, smem_count, scratch=()):
    return pl.pallas_call(
        body,
        out_shape=[jax.ShapeDtypeStruct(s, d) for s, d in outs],
        in_specs=[SMEM] * smem_count + [VMEM] * (len(args) - smem_count),
        out_specs=[VMEM] * len(outs),
        scratch_shapes=list(scratch),
        compiler_params=pltpu.CompilerParams(vmem_limit_bytes=40 * 2**20),
    )(*args)


def dot(a, b):
    return jnp.dot(a, b, preferred_element_type=F32)


def silu(x):
    return x * jax.nn.sigmoid(x)


def flip(x):
    return x.astype(F32).T


def split3(x):
    high = x.astype(BF16)
    rest = x - high.astype(F32)
    mid = rest.astype(BF16)
    low = (rest - mid.astype(F32)).astype(BF16)
    return jnp.concatenate([high, mid, low], axis=0)


def join3(x):
    return x[0:8] + x[8:16] + x[16:24]


def one_hot(row, depth):
    ids = lax.broadcasted_iota(jnp.int32, (depth, row.shape[1]), 0)
    return jnp.where(ids == row, 1.0, 0.0).astype(BF16)


def rows_kernel(meta, pos, charge, polar, neighbours, send, site, mine, lent_a, lent_b, slots, picks):
    odd = meta[1] == 1
    width = pos.shape[1]
    site[...] = jnp.zeros_like(site)
    site[0:3, :] = pos[...]
    site[3:4, :] = charge[...]
    site[4:5, :] = polar[...]
    for half in range(2):
        mine[half] = site[0:4, half * 128 : half * 128 + 128]
    first, second = send[0:1, :], send[1:2, :]
    swap = jnp.full(first.shape, meta[1], jnp.int32) == 1
    picks[0:1, :] = jnp.where(swap, second, first)
    picks[1:2, :] = jnp.where(swap, first, second)
    pieces = split3(site[...])
    lent_a[...] = join3(dot(pieces, one_hot(picks[0:1, :], width)))
    lent_b[...] = join3(dot(pieces, one_hot(picks[1:2, :], width)))
    table = flip(neighbours[...]).astype(jnp.int32)
    other = jnp.where((table >= 256) & (table < 512), jnp.bitwise_xor(table, 128), table)
    keep = jnp.full(table.shape, meta[1], jnp.int32) == 1
    slots[...] = jnp.where(keep, table, other)


def static_kernel(
    meta, site, rim_a, rim_b, slots, features, w_in, w_mid, w_out, node_in, node_out, gain,
    third, feat_t, out_t, in_t, node_t, gain_col, w3, w5, fixed, entry,
):
    learned = meta[0] == 0
    width = site.shape[1]
    depth = 2 * width
    slot_count = slots.shape[0]

    @pl.when(learned)
    def _():
        table = jnp.concatenate([site[...], rim_a[...], rim_b[...]], axis=1)
        pieces = split3(table)
        feat_t[...] = flip(features[...]).astype(BF16)
        gain_col[...] = jnp.broadcast_to(gain[...], (8, width)).T
        for layer in range(LAYERS):
            in_t[layer] = flip(node_in[layer]).astype(BF16)
            node_t[layer] = flip(node_out[layer]).astype(BF16)
            out_t[layer] = flip(w_out[layer]).astype(BF16)
        first_w = jnp.concatenate([flip(w_in[0]), flip(w_in[1])], axis=0).astype(BF16)
        zero = jnp.zeros((64, 64), F32)

        def both(depth_index):
            top = jnp.concatenate([flip(w_mid[0, depth_index]), zero], axis=1)
            bottom = jnp.concatenate([zero, flip(w_mid[1, depth_index])], axis=1)
            return jnp.concatenate([top, bottom], axis=0).astype(BF16)

        second_w, third_w = both(0), both(1)
        centres = lax.broadcasted_iota(jnp.int32, (BASIS, width), 0).astype(F32) * SPACING

        def one_slot(k, carry):
            found = join3(dot(pieces, one_hot(slots[pl.ds(k, 1), :], depth)))
            offset = site[...] - found
            squares = offset * offset
            dist_sq = squares[0:1] + squares[1:2] + squares[2:3] + SMOOTH
            gap = jnp.sqrt(dist_sq) - centres
            basis = jnp.exp(-(gap * gap)).astype(BF16)
            hidden = silu(dot(first_w, basis)).astype(BF16)
            hidden = silu(dot(second_w, hidden)).astype(BF16)
            hidden = silu(dot(third_w, hidden)).astype(BF16)
            third[k] = hidden
            return carry

        lax.fori_loop(0, slot_count, one_slot, 0, unroll=4)

    @pl.when(jnp.logical_not(learned))
    def _():
        table = jnp.concatenate([site[...], rim_a[...], rim_b[...]], axis=1)
        entry[...] = table.T
        tx, ty, tz = site[0:1, :], site[1:2, :], site[2:3, :]

        def some_rows(j, acc):
            start = pl.multiple_of(j * CHUNK, CHUNK)
            ids = lax.broadcasted_iota(jnp.int32, (CHUNK, width), 0) + start
            count = jnp.zeros((CHUNK, width), F32)
            for k in range(slot_count):
                count = count + jnp.where(ids == slots[k : k + 1, :], 1.0, 0.0)
            cols = entry[pl.ds(start, CHUNK), :]
            rx, ry, rz = tx - cols[:, 0:1], ty - cols[:, 1:2], tz - cols[:, 2:3]
            inverse = lax.rsqrt(rx * rx + ry * ry + rz * rz + SMOOTH)
            squared = inverse * inverse
            cube = count * (squared * inverse)
            w3[pl.ds(start, CHUNK), :] = cube
            w5[pl.ds(start, CHUNK), :] = 3.0 * (cube * squared)
            scale = cols[:, 3:4] * cube
            return acc[0] + rx * scale, acc[1] + ry * scale, acc[2] + rz * scale

        nil = jnp.zeros((CHUNK, width), F32)
        sums = lax.fori_loop(0, depth // CHUNK, some_rows, (nil, nil, nil))
        fixed[...] = jnp.zeros_like(fixed)
        for axis in range(3):
            fixed[axis : axis + 1, :] = jnp.sum(sums[axis], axis=0, keepdims=True)


def lend_dipoles(dipole, picks, lent_a, lent_b, whole):
    pieces = split3(dipole)
    for row, out in ((0, lent_a), (1, lent_b)):
        found = dot(pieces, one_hot(picks[row : row + 1, :], dipole.shape[1]))
        if whole:
            out[...] = join3(found)
        else:
            out[0:32, :] = jnp.concatenate([found, jnp.zeros((8, found.shape[1]), F32)], 0).astype(BF16)


def lend_lifted(lifted, picks, lent_a, lent_b):
    for row, out in ((0, lent_a), (1, lent_b)):
        out[...] = dot(lifted, one_hot(picks[row : row + 1, :], lifted.shape[1])).astype(BF16)


def sweep(site, w3, w5, fixed, dipole, side_a, side_b, entry, moment):
    width = site.shape[1]
    moment[...] = jnp.concatenate([dipole, side_a, side_b], axis=1).T
    tx, ty, tz = site[0:1, :], site[1:2, :], site[2:3, :]

    def some_rows(j, acc):
        start = pl.multiple_of(j * CHUNK, CHUNK)
        cols, d = entry[pl.ds(start, CHUNK), :], moment[pl.ds(start, CHUNK), :]
        rx, ry, rz = tx - cols[:, 0:1], ty - cols[:, 1:2], tz - cols[:, 2:3]
        dx, dy, dz = d[:, 0:1], d[:, 1:2], d[:, 2:3]
        cube = w3[pl.ds(start, CHUNK), :]
        scale = (rx * dx + ry * dy + rz * dz) * w5[pl.ds(start, CHUNK), :]
        return (
            acc[0] + (rx * scale - dx * cube),
            acc[1] + (ry * scale - dy * cube),
            acc[2] + (rz * scale - dz * cube),
        )

    nil = jnp.zeros((CHUNK, width), F32)
    sums = lax.fori_loop(0, w3.shape[0] // CHUNK, some_rows, (nil, nil, nil), unroll=2)
    induced = jnp.concatenate(
        [jnp.sum(s, axis=0, keepdims=True) for s in sums] + [jnp.zeros((5, width), F32)], axis=0
    )
    return site[4:5, :] * (fixed + induced)


def outside_kernel(
    meta, blocks, near, site, picks, feat_t, in_t, gain_col, fixed,
    outside_row, hidden, lifted, dipole, fixed_all, lent_a, lent_b, cols,
):
    learned = meta[0] == 0
    width = site.shape[1]
    listed = blocks.shape[0]
    for l in range(listed):
        tile = near[blocks[l]]
        cols[l * 128 : l * 128 + 128, :] = jnp.concatenate([tile, tile], axis=0).T
    tx, ty, tz = site[0:1, :], site[1:2, :], site[2:3, :]

    def some_rows(j, acc):
        c = cols[pl.ds(pl.multiple_of(j * CHUNK, CHUNK), CHUNK), :]
        rx, ry, rz = tx - c[:, 0:1], ty - c[:, 1:2], tz - c[:, 2:3]
        inverse = lax.rsqrt(rx * rx + ry * ry + rz * rz + SMOOTH)
        scale = c[:, 3:4] * (inverse * inverse * inverse)
        return acc[0] + rx * scale, acc[1] + ry * scale, acc[2] + rz * scale

    nil = jnp.zeros((CHUNK, width), F32)
    sums = lax.fori_loop(0, listed * 128 // CHUNK, some_rows, (nil, nil, nil), unroll=2)
    field = [jnp.sum(s, axis=0, keepdims=True) for s in sums]
    strength = jnp.sqrt(1.0 + (field[0] * field[0] + field[1] * field[1] + field[2] * field[2]))
    outside_row[...] = jnp.broadcast_to(strength, (8, width))

    @pl.when(learned)
    def _():
        start = (feat_t[...].astype(F32) + gain_col[:, 0:1] * strength).astype(BF16)
        hidden[...] = start
        raised = dot(in_t[0], start).astype(BF16)
        lifted[...] = raised
        lend_lifted(raised, picks, lent_a, lent_b)

    @pl.when(jnp.logical_not(learned))
    def _():
        total = fixed[...] + jnp.concatenate(field + [jnp.zeros((5, width), F32)], axis=0)
        fixed_all[...] = total
        moment = site[4:5, :] * total
        dipole[...] = moment
        lent_a[...] = jnp.zeros_like(lent_a)
        lent_b[...] = jnp.zeros_like(lent_b)
        lend_dipoles(moment, picks, lent_a, lent_b, False)


def message(layer, hidden, lifted, side_a, side_b, third, out_t, node_t, slots, total):
    slot_count, width = slots.shape
    table = jnp.concatenate([lifted[...], side_a[...], side_b[...]], axis=1)
    total[...] = jnp.zeros_like(total)

    def one_slot(k, carry):
        picked = dot(table, one_hot(slots[pl.ds(k, 1), :], table.shape[1]))
        weight = dot(out_t[layer], third[k, layer * 64 : layer * 64 + 64, :])
        total[...] += weight * picked
        return carry

    lax.fori_loop(0, slot_count, one_slot, 0, unroll=4)
    mean = (total[...] * (1.0 / slot_count)).astype(BF16)
    return (hidden[...].astype(F32) + silu(dot(node_t[layer], mean))).astype(BF16)


def round_one_kernel(
    meta, hidden, lifted, side_a, side_b, third, out_t, in_t, node_t, slots, picks,
    site, w3, w5, fixed, dipole, entry,
    hidden_out, lifted_out, lent_a, lent_b, dipole_out, small_a, small_b, total, moment,
):
    learned = meta[0] == 0

    @pl.when(learned)
    def _():
        new = message(0, hidden, lifted, side_a, side_b, third, out_t, node_t, slots, total)
        hidden_out[...] = new
        raised = dot(in_t[1], new).astype(BF16)
        lifted_out[...] = raised
        lend_lifted(raised, picks, lent_a, lent_b)

    @pl.when(jnp.logical_not(learned))
    def _():
        a, b = join3(side_a[0:24, :].astype(F32)), join3(side_b[0:24, :].astype(F32))
        new = sweep(site, w3, w5, fixed[...], dipole[...], a, b, entry, moment)
        dipole_out[...] = new
        lend_dipoles(new, picks, small_a, small_b, True)


def round_two_kernel(
    meta, got_a, got_b, side_a, side_b, site, w3, w5, fixed, dipole, entry, picks,
    lent_a, lent_b, dipole_out, moment,
):
    learned = meta[0] == 0

    @pl.when(learned)
    def _():
        lent_a[...] = got_a[...]
        lent_b[...] = got_b[...]

    @pl.when(jnp.logical_not(learned))
    def _():
        new = sweep(site, w3, w5, fixed[...], dipole[...], side_a[...], side_b[...], entry, moment)
        dipole_out[...] = new
        lent_a[...] = jnp.zeros_like(lent_a)
        lent_b[...] = jnp.zeros_like(lent_b)
        lend_dipoles(new, picks, lent_a, lent_b, False)


def round_three_kernel(
    meta, hidden, lifted, side_a, side_b, third, out_t, node_t, slots, picks, readout,
    site, w3, w5, fixed, dipole, entry,
    charge, dipole_out, small_a, small_b, total, moment,
):
    learned = meta[0] == 0

    @pl.when(learned)
    def _():
        new = message(1, hidden, lifted, side_a, side_b, third, out_t, node_t, slots, total)
        columns = flip(readout[...])
        padded = jnp.concatenate([columns, jnp.zeros((6, columns.shape[1]), F32)], axis=0)
        charge[...] = dot(padded.astype(BF16), new)

    @pl.when(jnp.logical_not(learned))
    def _():
        a, b = join3(side_a[0:24, :].astype(F32)), join3(side_b[0:24, :].astype(F32))
        new = sweep(site, w3, w5, fixed[...], dipole[...], a, b, entry, moment)
        dipole_out[...] = new
        lend_dipoles(new, picks, small_a, small_b, True)


def response_kernel(
    meta, blocks, near, site, charge, outside_row, side_a, side_b, w3, w5, fixed, dipole, entry,
    result, spread, cols, moment, term,
):
    learned = meta[0] == 0
    width = site.shape[1]
    listed = blocks.shape[0]
    spread[...] = jnp.zeros_like(spread)

    def terms(dipoles):
        for l in range(listed):
            tile = near[blocks[l]]
            tx, ty, tz = tile[0:1, :], tile[1:2, :], tile[2:3, :]

            def some_rows(j, acc):
                start = pl.multiple_of(j * 2 * CHUNK, 2 * CHUNK)
                c = cols[pl.ds(start, 2 * CHUNK), :]
                rx, ry, rz = tx - c[:, 0:1], ty - c[:, 1:2], tz - c[:, 2:3]
                inverse = lax.rsqrt(rx * rx + ry * ry + rz * rz + SMOOTH)
                squared = inverse * inverse
                cube = squared * inverse
                if dipoles:
                    dx, dy, dz = c[:, 4:5], c[:, 5:6], c[:, 6:7]
                    scale = (rx * dx + ry * dy + rz * dz) * (3.0 * (cube * squared))
                    return (
                        acc[0] + (rx * scale - dx * cube),
                        acc[1] + (ry * scale - dy * cube),
                        acc[2] + (rz * scale - dz * cube),
                    )
                scale = c[:, 3:4] * cube
                return acc[0] + rx * scale, acc[1] + ry * scale, acc[2] + rz * scale

            nil = jnp.zeros((2 * CHUNK, 128), F32)
            sums = lax.fori_loop(0, width // (2 * CHUNK), some_rows, (nil, nil, nil), unroll=2)
            for axis in range(3):
                term[l, axis : axis + 1, :] = jnp.sum(sums[axis], axis=0, keepdims=True)
        for l in range(listed):
            spread[blocks[l]] += term[l]

    term[...] = jnp.zeros_like(term)

    @pl.when(learned)
    def _():
        q = charge[...]
        result[...] = jnp.concatenate([q[0:2], outside_row[0:1, :], jnp.zeros((5, width), F32)], axis=0)
        cols[...] = jnp.concatenate([site[0:3, :], q[0:1], jnp.zeros((4, width), F32)], axis=0).T
        terms(False)

    @pl.when(jnp.logical_not(learned))
    def _():
        new = sweep(site, w3, w5, fixed[...], dipole[...], side_a[...], side_b[...], entry, moment)
        result[...] = new
        cols[...] = jnp.concatenate([site[0:4, :], new[0:3], jnp.zeros((1, width), F32)], axis=0).T
        terms(True)


def local(
    positions, charges, polar, features, neighbours, send_rows, blocks,
    radial_in, radial_mid, radial_out, node_in, node_out, field_gain, readout,
):
    width = positions.shape[1]
    slot_count = neighbours.shape[1]
    depth = 2 * width
    half = send_rows.shape[1]
    channels = features.shape[1]
    members = lax.axis_size(DOM)
    group = lax.axis_index("grp")
    index = lax.axis_index(DOM)
    meta = jnp.stack([group, index % 2]).astype(jnp.int32)
    near_pairs = [(i, i ^ 1) for i in range(members)]
    far_pairs = [(i, ((i - 1) ^ 1) + 1) for i in range(1, members - 1)]

    def both_groups(pairs):
        return pairs + [(a + members, b + members) for a, b in pairs]

    def trade(a, b, solvent_only=False):
        shift = [[(x + members, y + members) for x, y in pairs] for pairs in (near_pairs, far_pairs)]
        full = [both_groups(near_pairs), both_groups(far_pairs)]
        used = shift if solvent_only else full
        return lax.ppermute(a, EVERY, used[0]), lax.ppermute(b, EVERY, used[1])

    site, mine, lent_a, lent_b, slots, picks = call(
        rows_kernel,
        [((8, width), F32), ((2, 4, half), F32), ((8, half), F32), ((8, half), F32),
         ((slot_count, width), jnp.int32), ((2, half), jnp.int32)],
        (meta, positions, charges[None], polar[None], neighbours, send_rows), 1,
    )
    partner = lax.ppermute(mine, "grp", [(0, 1), (1, 0)])
    copies = jnp.broadcast_to(partner[None], (members,) + partner.shape)
    near = lax.all_to_all(copies, DOM, 0, 0, tiled=True).reshape(2 * members, 4, half)
    rim_a, rim_b = trade(lent_a, lent_b)
    third, feat_t, out_t, in_t, node_t, gain_col, w3, w5, fixed, entry = call(
        static_kernel,
        [((slot_count, 128, width), BF16), ((channels, width), BF16), ((LAYERS, channels, 64), BF16),
         ((LAYERS, channels, channels), BF16), ((LAYERS, channels, channels), BF16), ((channels, 8), F32),
         ((depth, width), F32), ((depth, width), F32), ((8, width), F32), ((depth, 8), F32)],
        (meta, site, rim_a, rim_b, slots, features, radial_in, radial_mid, radial_out, node_in, node_out,
         field_gain[None]), 1,
    )
    wide = [((channels, half), BF16)] * 2
    small = [((8, half), F32)] * 2
    outside_row, hidden, lifted, dipole, fixed_all, lent_a, lent_b = call(
        outside_kernel,
        [((8, width), F32), ((channels, width), BF16), ((channels, width), BF16), ((8, width), F32),
         ((8, width), F32)] + wide,
        (meta, blocks, near, site, picks, feat_t, in_t, gain_col, fixed), 2,
        [pltpu.VMEM((4 * half, 8), F32)],
    )
    side_a, side_b = trade(lent_a, lent_b)
    moment = pltpu.VMEM((depth, 8), F32)
    total = pltpu.VMEM((channels, width), F32)
    hidden, lifted, lent_a, lent_b, dipole, small_a, small_b = call(
        round_one_kernel,
        [((channels, width), BF16), ((channels, width), BF16)] + wide + [((8, width), F32)] + small,
        (meta, hidden, lifted, side_a, side_b, third, out_t, in_t, node_t, slots, picks,
         site, w3, w5, fixed_all, dipole, entry), 1, [total, moment],
    )
    side_a, side_b = trade(small_a, small_b, True)
    lent_a, lent_b, dipole = call(
        round_two_kernel, wide + [((8, width), F32)],
        (meta, lent_a, lent_b, side_a, side_b, site, w3, w5, fixed_all, dipole, entry, picks), 1, [moment],
    )
    side_a, side_b = trade(lent_a, lent_b)
    charge, dipole, small_a, small_b = call(
        round_three_kernel, [((8, width), F32), ((8, width), F32)] + small,
        (meta, hidden, lifted, side_a, side_b, third, out_t, node_t, slots, picks, readout,
         site, w3, w5, fixed_all, dipole, entry), 1, [total, moment],
    )
    side_a, side_b = trade(small_a, small_b, True)
    result, spread = call(
        response_kernel, [((8, width), F32), ((2 * members, 4, half), F32)],
        (meta, blocks, near, site, charge, outside_row, side_a, side_b, w3, w5, fixed_all, dipole, entry), 2,
        [pltpu.VMEM((width, 8), F32), moment, pltpu.VMEM((4, 4, half), F32)],
    )
    pieces = lax.all_to_all(spread.reshape(members, 2, 4, half), DOM, 0, 0, tiled=True)
    share = lax.ppermute(jnp.sum(pieces, axis=0), "grp", [(0, 1), (1, 0)])
    response = jnp.concatenate([share[0, :3], share[1, :3]], axis=1)
    return result[:3], response


def solution(mesh):
    sites = P(None, EVERY)
    in_specs = (sites, P(EVERY), P(EVERY), P(EVERY, None), P(EVERY, None), sites, P(EVERY)) + (P(),) * 7
    return jax.shard_map(local, mesh=mesh, in_specs=in_specs, out_specs=(sites, sites), check_vma=False)
```

```python
import jax
import jax.numpy as jnp
from jax import lax
from jax.experimental import pallas as pl
from jax.experimental.pallas import tpu as pltpu
from jax.sharding import PartitionSpec as P

BASIS = 8
LAYERS = 2
SMOOTH = 1.0
SPACING = 0.75
DOM = ("dom", "sub")
EVERY = ("grp", "dom", "sub")
F32 = jnp.float32
BF16 = jnp.bfloat16
VMEM = pl.BlockSpec(memory_space=pltpu.VMEM)
ANY = pl.BlockSpec(memory_space=pl.ANY)
CHUNK = 16


def call(body, outs, held, far=(), scratch=(), copies=0, far_outs=0, loose=0):
    return pl.pallas_call(
        body,
        out_shape=[jax.ShapeDtypeStruct(s, d) for s, d in outs[: len(outs) - far_outs]]
        + [pltpu.HBM(s, d) for s, d in outs[len(outs) - far_outs :]],
        in_specs=[VMEM] * len(held) + [ANY] * len(far),
        out_specs=[VMEM] * (len(outs) - far_outs) + [ANY] * far_outs,
        scratch_shapes=list(scratch) + ([pltpu.SemaphoreType.DMA((copies,))] if copies else []),
        compiler_params=pltpu.CompilerParams(vmem_limit_bytes=24 * 2**20),
    )(*held, *far[:loose], *[pltpu.with_memory_space_constraint(a, pltpu.HBM) for a in far[loose:]])


def fetch(pairs, done, first=0):
    copies = [pltpu.make_async_copy(a, b, done.at[first + i]) for i, (a, b) in enumerate(pairs)]
    for c in copies:
        c.start()

    def wait():
        for c in copies:
            c.wait()

    return wait


def learned():
    return lax.axis_index("grp") == 0


def dot(a, b):
    return jnp.dot(a, b, preferred_element_type=F32)


def silu(x):
    half = 0.5 * x
    return half + half * jnp.tanh(half)


def flip(x):
    return x.astype(F32).T


def split3(x):
    high = x.astype(BF16)
    rest = x - high.astype(F32)
    mid = rest.astype(BF16)
    low = (rest - mid.astype(F32)).astype(BF16)
    return jnp.concatenate([high, mid, low], axis=0)


def join3(x):
    return x[0:8] + x[8:16] + x[16:24]


def one_hot(row, depth):
    ids = lax.broadcasted_iota(jnp.int32, (depth, row.shape[1]), 0)
    return jnp.where(ids == row, 1.0, 0.0).astype(BF16)


def rows(parts, count=8):
    have = sum(p.shape[0] for p in parts)
    return jnp.concatenate(list(parts) + [jnp.zeros((count - have, parts[0].shape[1]), F32)], axis=0)


def rows_kernel(
    pos_far, charge_far, polar_far, table_far, send_far, blocks_far,
    site, mine, lent_a, lent_b, slots, picks,
    pos, charge, polar, table, send, blocks, done,
):
    pairs = ((pos_far, pos), (charge_far, charge), (polar_far, polar), (table_far, table), (send_far, send))
    wait = fetch(pairs + ((blocks_far, blocks),), done)
    odd = lax.axis_index("sub")
    width = pos.shape[1]
    wait()
    sites = rows([pos[...], charge[...], polar[...]])
    site[...] = sites
    for half in range(2):
        mine[half] = sites[0:4, half * 128 : half * 128 + 128]
    first, second = send[0:1, :], send[1:2, :]
    swap = jnp.full(first.shape, odd, jnp.int32) == 1
    picks[0:1, :] = jnp.where(swap, second, first)
    picks[1:2, :] = jnp.where(swap, first, second)
    lane = lax.broadcasted_iota(jnp.int32, (1, 128), 1)
    listed = jnp.zeros((1, 128), jnp.int32)
    for l in range(blocks.shape[0]):
        listed = jnp.where(lane == l, blocks[l], listed)
    pieces = split3(sites)
    for row, out in ((0, lent_a), (1, lent_b)):
        found = join3(dot(pieces, one_hot(picks[row : row + 1, :], width)))
        out[...] = rows([found[0:5], listed.astype(F32), jnp.ones((1, 128), F32)])
    raw = table[...]
    other = jnp.where((raw >= 256) & (raw < 512), jnp.bitwise_xor(raw, 128), raw)
    keep = jnp.full(raw.shape, odd, jnp.int32) == 1
    slots[...] = jnp.where(keep, raw, other)


def static_kernel(
    site, rim_a, rim_b, slots, picks, features_far,
    feat_t, w3, w5, fixed, entry, lent_a, lent_b, features, done,
):
    width = site.shape[1]
    depth = 2 * width
    slot_count = slots.shape[0]

    @pl.when(learned())
    def _():
        fetch(((features_far, features),), done)()
        flipped = flip(features[...]).astype(BF16)
        feat_t[...] = flipped
        lend_channels(flipped, picks, lent_a, lent_b)

    @pl.when(jnp.logical_not(learned()))
    def _():
        table = jnp.concatenate([site[...], rim_a[...], rim_b[...]], axis=1)
        entry[...] = table.T
        tx, ty, tz = site[0:1, :], site[1:2, :], site[2:3, :]

        def some_rows(j, acc):
            start = pl.multiple_of(j * CHUNK, CHUNK)
            ids = lax.broadcasted_iota(jnp.int32, (CHUNK, width), 0) + start
            count = jnp.zeros((CHUNK, width), F32)
            for k in range(slot_count):
                count = count + jnp.where(ids == slots[k : k + 1, :], 1.0, 0.0)
            cols = entry[pl.ds(start, CHUNK), :]
            rx, ry, rz = tx - cols[:, 0:1], ty - cols[:, 1:2], tz - cols[:, 2:3]
            inverse = lax.rsqrt(rx * rx + ry * ry + rz * rz + SMOOTH)
            squared = inverse * inverse
            cube = count * (squared * inverse)
            w3[pl.ds(start, CHUNK), :] = cube
            w5[pl.ds(start, CHUNK), :] = 3.0 * (cube * squared)
            scale = cols[:, 3:4] * cube
            return acc[0] + rx * scale, acc[1] + ry * scale, acc[2] + rz * scale

        nil = jnp.zeros((CHUNK, width), F32)
        sums = lax.fori_loop(0, depth // CHUNK, some_rows, (nil, nil, nil))
        total = rows([jnp.sum(s, axis=0, keepdims=True) for s in sums])
        fixed[...] = total
        lend_pieces(total, picks, lent_a, lent_b)


def radial_kernel(
    site, rim_a, rim_b, slots, w_in_far, w_mid_far,
    third_far, w_in, w_mid, third, done,
):
    width = site.shape[1]
    depth = 2 * width
    slot_count = slots.shape[0]

    @pl.when(learned())
    def _():
        wait = fetch(((w_in_far, w_in), (w_mid_far, w_mid)), done)
        pieces = split3(jnp.concatenate([site[...], rim_a[...], rim_b[...]], axis=1))
        centres = lax.broadcasted_iota(jnp.int32, (BASIS, width), 0).astype(F32) * SPACING
        wait()
        first_w = jnp.concatenate([flip(w_in[0]), flip(w_in[1])], axis=0).astype(BF16)
        zero = jnp.zeros((64, 64), F32)

        def both(level):
            top = jnp.concatenate([flip(w_mid[0, level]), zero], axis=1)
            bottom = jnp.concatenate([zero, flip(w_mid[1, level])], axis=1)
            return jnp.concatenate([top, bottom], axis=0).astype(BF16)

        second_w, third_w = both(0), both(1)

        def one_slot(k, carry):
            found = join3(dot(pieces, one_hot(slots[pl.ds(k, 1), :], depth)))
            offset = site[...] - found
            squares = offset * offset
            dist_sq = squares[0:1] + squares[1:2] + squares[2:3] + SMOOTH
            gap = jnp.sqrt(dist_sq) - centres
            basis = jnp.exp(-(gap * gap)).astype(BF16)
            hidden = silu(dot(first_w, basis)).astype(BF16)
            hidden = silu(dot(second_w, hidden)).astype(BF16)
            third[k] = silu(dot(third_w, hidden)).astype(BF16)
            return carry

        lax.fori_loop(0, slot_count, one_slot, 0, unroll=4)
        fetch(((third, third_far),), done, 2)()


def lend_pieces(values, picks, lent_a, lent_b):
    pieces = split3(values)
    for row, out in ((0, lent_a), (1, lent_b)):
        found = dot(pieces, one_hot(picks[row : row + 1, :], values.shape[1]))
        out[...] = jnp.zeros_like(out)
        out[0:32, :] = rows([found], 32).astype(BF16)


def lend_whole(values, picks, lent_a, lent_b):
    pieces = split3(values)
    for row, out in ((0, lent_a), (1, lent_b)):
        out[...] = join3(dot(pieces, one_hot(picks[row : row + 1, :], values.shape[1])))


def lend_channels(values, picks, lent_a, lent_b):
    for row, out in ((0, lent_a), (1, lent_b)):
        out[...] = dot(values, one_hot(picks[row : row + 1, :], values.shape[1])).astype(BF16)


def sweep(site, w3, w5, fixed, dipoles, entry, moment):
    width = site.shape[1]
    moment[...] = dipoles.T
    tx, ty, tz = site[0:1, :], site[1:2, :], site[2:3, :]

    def some_rows(j, acc):
        start = pl.multiple_of(j * CHUNK, CHUNK)
        cols, d = entry[pl.ds(start, CHUNK), :], moment[pl.ds(start, CHUNK), :]
        rx, ry, rz = tx - cols[:, 0:1], ty - cols[:, 1:2], tz - cols[:, 2:3]
        dx, dy, dz = d[:, 0:1], d[:, 1:2], d[:, 2:3]
        cube = w3[pl.ds(start, CHUNK), :]
        scale = (rx * dx + ry * dy + rz * dz) * w5[pl.ds(start, CHUNK), :]
        return (
            acc[0] + (rx * scale - dx * cube),
            acc[1] + (ry * scale - dy * cube),
            acc[2] + (rz * scale - dz * cube),
        )

    nil = jnp.zeros((CHUNK, width), F32)
    sums = lax.fori_loop(0, w3.shape[0] // CHUNK, some_rows, (nil, nil, nil), unroll=2)
    return site[4:5, :] * (fixed + rows([jnp.sum(s, axis=0, keepdims=True) for s in sums]))


def message(layer, hidden, table, third, out_t, node_t, slots, total):
    slot_count = slots.shape[0]
    total[...] = jnp.zeros_like(total)

    def one_slot(k, carry):
        picked = dot(table, one_hot(slots[pl.ds(k, 1), :], table.shape[1]))
        weight = dot(out_t, third[k, layer * 64 : layer * 64 + 64, :])
        total[...] += weight * picked
        return carry

    lax.fori_loop(0, slot_count, one_slot, 0, unroll=4)
    mean = (total[...] * (1.0 / slot_count)).astype(BF16)
    return (hidden.astype(F32) + silu(dot(node_t, mean))).astype(BF16)


def charge_field(target, cols, first, count):
    tx, ty, tz = target[0:1, :], target[1:2, :], target[2:3, :]

    def some_rows(j, acc):
        c = cols[pl.ds(pl.multiple_of(first + j * CHUNK, CHUNK), CHUNK), :]
        rx, ry, rz = tx - c[:, 0:1], ty - c[:, 1:2], tz - c[:, 2:3]
        inverse = lax.rsqrt(rx * rx + ry * ry + rz * rz + SMOOTH)
        scale = c[:, 3:4] * (inverse * inverse * inverse)
        return acc[0] + rx * scale, acc[1] + ry * scale, acc[2] + rz * scale

    nil = jnp.zeros((CHUNK, target.shape[1]), F32)
    sums = lax.fori_loop(0, count // CHUNK, some_rows, (nil, nil, nil), unroll=2)
    return jnp.concatenate([jnp.sum(s, axis=0, keepdims=True) for s in sums], axis=0)


def first_kernel(
    site, rim_a, rim_b, slots, picks, feat_t, side_a, side_b, w3, w5, fixed, entry,
    near_far, blocks_far, third_far, node_in_far, node_out_far, w_out_far, gain_far,
    outside_row, near_own, hidden_out, lifted_out, fixed_out, dipole_out, lent_a, lent_b,
    blocks, near, cols, third, node_in, node_out, w_out, gain, total, moment, done,
):
    width = site.shape[1]
    listed = blocks.shape[0]
    wait_blocks = fetch(((blocks_far, blocks),), done)
    weights = (
        (third_far, third), (node_in_far, node_in), (node_out_far.at[0], node_out),
        (w_out_far.at[0], w_out), (gain_far, gain),
    )

    @pl.when(learned())
    def _():
        fetch(weights, done, 1)

    lane = lax.broadcasted_iota(jnp.int32, (1, 128), 1)

    def lent_block(rim, l):
        return jnp.sum(jnp.where(lane == l, rim[5:6, :], 0.0)).astype(jnp.int32)

    numbers = [lent_block(rim, l) for rim in (rim_a, rim_b) for l in range(listed)]
    wait_blocks()
    numbers = [blocks[l] for l in range(listed)] + numbers
    fetch([(near_far.at[b], near.at[i]) for i, b in enumerate(numbers)], done, 6)()
    near_own[...] = near[0:listed]
    for i in range(3 * listed):
        tile = near[i]
        cols[i * 128 : i * 128 + 128, :] = jnp.concatenate([tile, tile], axis=0).T
    reach = listed * 128
    own_field = charge_field(site[...], cols, 0, reach)
    field = jnp.concatenate(
        [own_field, charge_field(rim_a[...], cols, reach, reach), charge_field(rim_b[...], cols, 2 * reach, reach)],
        axis=1,
    )
    strength = jnp.sqrt(1.0 + (field[0:1] * field[0:1] + field[1:2] * field[1:2] + field[2:3] * field[2:3]))
    outside_row[...] = jnp.broadcast_to(strength[:, :width], outside_row.shape)

    @pl.when(learned())
    def _():
        for i, (a, b) in enumerate(weights):
            pltpu.make_async_copy(a, b, done.at[1 + i]).wait()
        gain_col = jnp.broadcast_to(gain[...], (8, width)).T
        features = jnp.concatenate([feat_t[...], side_a[...], side_b[...]], axis=1)
        start = (features.astype(F32) + gain_col[:, 0:1] * strength).astype(BF16)
        present = jnp.concatenate([jnp.ones((1, width), F32), rim_a[6:7, :], rim_b[6:7, :]], axis=1)
        raised = dot(flip(node_in[0]).astype(BF16), start)
        table = jnp.where(present > 0.5, raised, 0.0).astype(BF16)
        out_t, node_t = flip(w_out[...]).astype(BF16), flip(node_out[...]).astype(BF16)
        new = message(0, start[:, :width], table, third, out_t, node_t, slots, total)
        hidden_out[...] = new
        raised = dot(flip(node_in[1]).astype(BF16), new).astype(BF16)
        lifted_out[...] = raised
        lend_channels(raised, picks, lent_a, lent_b)

    @pl.when(jnp.logical_not(learned()))
    def _():
        known = [fixed[...], join3(side_a[0:24, :].astype(F32)), join3(side_b[0:24, :].astype(F32))]
        whole = jnp.concatenate(known, axis=1) + rows([field])
        fixed_out[...] = whole[:, :width]
        polar = jnp.concatenate([site[4:5, :], rim_a[4:5, :], rim_b[4:5, :]], axis=1)
        new = sweep(site, w3, w5, whole[:, :width], polar * whole, entry, moment)
        dipole_out[...] = new
        lend_pieces(new, picks, lent_a, lent_b)


def second_kernel(
    hidden, lifted, side_a, side_b, slots, picks, site, w3, w5, fixed, dipole, entry,
    third_far, node_out_far, w_out_far, readout_far,
    charge, dipole_out, small_a, small_b,
    third, node_out, w_out, readout, total, moment, done,
):
    width = site.shape[1]

    @pl.when(learned())
    def _():
        fetch(
            ((third_far, third), (node_out_far.at[1], node_out), (w_out_far.at[1], w_out), (readout_far, readout)), done
        )()
        table = jnp.concatenate([lifted[...], side_a[...], side_b[...]], axis=1)
        out_t, node_t = flip(w_out[...]).astype(BF16), flip(node_out[...]).astype(BF16)
        new = message(1, hidden[...], table, third, out_t, node_t, slots, total)
        charge[...] = dot(rows([readout[...].astype(F32)]).astype(BF16), new)

    @pl.when(jnp.logical_not(learned()))
    def _():
        sides = [join3(side_a[0:24, :].astype(F32)), join3(side_b[0:24, :].astype(F32))]
        table = jnp.concatenate([dipole[...]] + sides, axis=1)
        new = sweep(site, w3, w5, fixed[...], table, entry, moment)
        dipole_out[...] = new
        lend_whole(new, picks, small_a, small_b)


def third_kernel(side_a, side_b, picks, site, w3, w5, fixed, dipole, entry, dipole_out, small_a, small_b, moment):
    @pl.when(jnp.logical_not(learned()))
    def _():
        table = jnp.concatenate([dipole[...], side_a[...], side_b[...]], axis=1)
        new = sweep(site, w3, w5, fixed[...], table, entry, moment)
        dipole_out[...] = new
        lend_whole(new, picks, small_a, small_b)


def response_kernel(
    near, site, charge, outside_row, side_a, side_b, w3, w5, fixed, dipole, entry, blocks_far,
    result, spread, blocks, cols, moment, term, done,
):
    width = site.shape[1]
    listed = blocks.shape[0]
    wait = fetch(((blocks_far, blocks),), done)
    spread[...] = jnp.zeros_like(spread)
    term[...] = jnp.zeros_like(term)

    def terms(dipoles):
        for l in range(listed):
            tile = near[l]
            tx, ty, tz = tile[0:1, :], tile[1:2, :], tile[2:3, :]

            def some_rows(j, acc):
                start = pl.multiple_of(j * 2 * CHUNK, 2 * CHUNK)
                c = cols[pl.ds(start, 2 * CHUNK), :]
                rx, ry, rz = tx - c[:, 0:1], ty - c[:, 1:2], tz - c[:, 2:3]
                inverse = lax.rsqrt(rx * rx + ry * ry + rz * rz + SMOOTH)
                squared = inverse * inverse
                cube = squared * inverse
                if dipoles:
                    dx, dy, dz = c[:, 4:5], c[:, 5:6], c[:, 6:7]
                    scale = (rx * dx + ry * dy + rz * dz) * (3.0 * (cube * squared))
                    return (
                        acc[0] + (rx * scale - dx * cube),
                        acc[1] + (ry * scale - dy * cube),
                        acc[2] + (rz * scale - dz * cube),
                    )
                scale = c[:, 3:4] * cube
                return acc[0] + rx * scale, acc[1] + ry * scale, acc[2] + rz * scale

            nil = jnp.zeros((2 * CHUNK, 128), F32)
            sums = lax.fori_loop(0, width // (2 * CHUNK), some_rows, (nil, nil, nil), unroll=2)
            for axis in range(3):
                term[l, axis : axis + 1, :] = jnp.sum(sums[axis], axis=0, keepdims=True)

    @pl.when(learned())
    def _():
        q = charge[...]
        result[...] = jnp.concatenate([q[0:2], outside_row[0:1, :]], axis=0)
        cols[...] = rows([site[0:3, :], q[0:1]]).T
        terms(False)

    @pl.when(jnp.logical_not(learned()))
    def _():
        table = jnp.concatenate([dipole[...], side_a[...], side_b[...]], axis=1)
        new = sweep(site, w3, w5, fixed[...], table, entry, moment)
        result[...] = new[0:3]
        cols[...] = rows([site[0:4, :], new[0:3]]).T
        terms(True)

    wait()
    for l in range(listed):
        spread[blocks[l]] += term[l]


def gather_kernel(pieces, share):
    total = jnp.sum(pieces[...], axis=0)
    share[...] = jnp.concatenate([total[0, 0:3], total[1, 0:3]], axis=1)


def local(
    positions, charges, polar, features, neighbours, send_rows, blocks,
    radial_in, radial_mid, radial_out, node_in, node_out, field_gain, readout,
):
    width = positions.shape[1]
    slot_count = neighbours.shape[1]
    depth = 2 * width
    half = send_rows.shape[1]
    channels = features.shape[1]
    listed = blocks.shape[0]
    members = lax.axis_size(DOM)
    near_pairs = [(i, i ^ 1) for i in range(members)]
    far_pairs = [(i, ((i - 1) ^ 1) + 1) for i in range(1, members - 1)]

    def trade(a, b, solvent_only=False):
        used = []
        for pairs in (near_pairs, far_pairs):
            shifted = [(x + members, y + members) for x, y in pairs]
            used.append(shifted if solvent_only else pairs + shifted)
        return lax.ppermute(a, EVERY, used[0]), lax.ppermute(b, EVERY, used[1])

    row8, table8 = ((8, width), F32), ((8, half), F32)
    wide = ((channels, half), BF16)
    by_site = ((channels, width), BF16)
    ints = jnp.int32
    site, mine, lent_a, lent_b, slots, picks = call(
        rows_kernel,
        [row8, ((2, 4, half), F32), table8, table8, ((slot_count, width), ints), ((2, half), ints)],
        (), (positions, charges[None], polar[None], neighbours.T, send_rows, blocks),
        [pltpu.VMEM((3, width), F32), pltpu.VMEM((1, width), F32), pltpu.VMEM((1, width), F32),
         pltpu.VMEM((slot_count, width), ints), pltpu.VMEM((2, half), ints), pltpu.SMEM((listed,), ints)], 6,
    )
    rim_a, rim_b = trade(lent_a, lent_b)
    partner = lax.ppermute(mine, "grp", [(0, 1), (1, 0)])
    partner, rim_a, rim_b = lax.optimization_barrier((partner, rim_a, rim_b))
    copies = jnp.broadcast_to(partner[None], (members,) + partner.shape)
    near = lax.all_to_all(copies, DOM, 0, 0, tiled=True).reshape(2 * members, 4, half)
    feat_t, w3, w5, fixed, entry, lent_a, lent_b = call(
        static_kernel, [by_site, ((depth, width), F32), ((depth, width), F32), row8, ((depth, 8), F32), wide, wide],
        (site, rim_a, rim_b, slots, picks), (features,), [pltpu.VMEM((width, channels), BF16)], 1,
    )
    side_a, side_b = trade(lent_a, lent_b)
    third_shape = (slot_count, LAYERS * radial_in.shape[2], width)
    (third,) = call(
        radial_kernel, [(third_shape, BF16)], (site, rim_a, rim_b, slots), (radial_in, radial_mid),
        [pltpu.VMEM(radial_in.shape, BF16), pltpu.VMEM(radial_mid.shape, BF16), pltpu.VMEM(third_shape, BF16)], 3, 1,
    )
    moment = pltpu.VMEM((depth, 8), F32)
    total = pltpu.VMEM((channels, width), F32)
    square = pltpu.VMEM(node_out.shape[1:], BF16)
    last = pltpu.VMEM(radial_out.shape[1:], BF16)
    outside_row, near_own, hidden, lifted, fixed_all, dipole, lent_a, lent_b = call(
        first_kernel, [row8, ((listed, 4, half), F32), by_site, by_site, row8, row8, wide, wide],
        (site, rim_a, rim_b, slots, picks, feat_t, side_a, side_b, w3, w5, fixed, entry),
        (near, blocks, third, node_in, node_out, radial_out, field_gain[None]),
        [pltpu.SMEM((listed,), ints), pltpu.VMEM((3 * listed, 4, half), F32), pltpu.VMEM((3 * listed * half, 8), F32),
         pltpu.VMEM(third_shape, BF16), pltpu.VMEM(node_in.shape, BF16), square, last,
         pltpu.VMEM((1, channels), F32), total, moment], 6 + 3 * listed, loose=1,
    )
    side_a, side_b = trade(lent_a, lent_b)
    charge, dipole, small_a, small_b = call(
        second_kernel, [row8, row8, table8, table8],
        (hidden, lifted, side_a, side_b, slots, picks, site, w3, w5, fixed_all, dipole, entry),
        (third, node_out, radial_out, readout.T),
        [pltpu.VMEM(third_shape, BF16), square, last, pltpu.VMEM((2, channels), BF16), total, moment], 4,
    )
    side_a, side_b = trade(small_a, small_b, True)
    dipole, small_a, small_b = call(
        third_kernel, [row8, table8, table8], (side_a, side_b, picks, site, w3, w5, fixed_all, dipole, entry),
        (), [moment],
    )
    side_a, side_b = trade(small_a, small_b, True)
    result, spread = call(
        response_kernel, [((3, width), F32), ((2 * members, 4, half), F32)],
        (near_own, site, charge, outside_row, side_a, side_b, w3, w5, fixed_all, dipole, entry), (blocks,),
        [pltpu.SMEM((listed,), ints), pltpu.VMEM((width, 8), F32), moment, pltpu.VMEM((listed, 4, half), F32)], 1,
    )
    pieces = lax.all_to_all(spread.reshape(members, 2, 4, half), DOM, 0, 0, tiled=True)
    (share,) = call(gather_kernel, [((3, width), F32)], (pieces,))
    return result, lax.ppermute(share, "grp", [(0, 1), (1, 0)])


def solution(mesh):
    sites = P(None, EVERY)
    in_specs = (sites, P(EVERY), P(EVERY), P(EVERY, None), P(EVERY, None), sites, P(EVERY)) + (P(),) * 7
    return jax.shard_map(local, mesh=mesh, in_specs=in_specs, out_specs=(sites, sites), check_vma=False)
```

```python
import jax
import jax.numpy as jnp
from jax import lax
from jax.experimental import pallas as pl
from jax.experimental.pallas import tpu as pltpu
from jax.sharding import PartitionSpec as P

BASIS = 8
LAYERS = 2
SMOOTH = 1.0
SPACING = 0.75
DOM = ("dom", "sub")
EVERY = ("grp", "dom", "sub")
F32 = jnp.float32
BF16 = jnp.bfloat16
VMEM = pl.BlockSpec(memory_space=pltpu.VMEM)
ANY = pl.BlockSpec(memory_space=pl.ANY)
SWEEP_CHUNK, SWEEP_UNROLL = 32, 4
FIELD_CHUNK, FIELD_UNROLL = 32, 4
TERM_CHUNK, TERM_UNROLL = 64, 4
STATIC_CHUNK = 32
RADIAL_SLOTS = 8
MESSAGE_SLOTS = 8


def call(body, outs, held, far=(), scratch=(), copies=0, far_outs=0, loose=0):
    return pl.pallas_call(
        body,
        out_shape=[jax.ShapeDtypeStruct(s, d) for s, d in outs[: len(outs) - far_outs]]
        + [pltpu.HBM(s, d) for s, d in outs[len(outs) - far_outs :]],
        in_specs=[VMEM] * len(held) + [ANY] * len(far),
        out_specs=[VMEM] * (len(outs) - far_outs) + [ANY] * far_outs,
        scratch_shapes=list(scratch) + ([pltpu.SemaphoreType.DMA((copies,))] if copies else []),
        compiler_params=pltpu.CompilerParams(vmem_limit_bytes=24 * 2**20),
    )(*held, *far[:loose], *[pltpu.with_memory_space_constraint(a, pltpu.HBM) for a in far[loose:]])


def fetch(pairs, done, first=0):
    copies = [pltpu.make_async_copy(a, b, done.at[first + i]) for i, (a, b) in enumerate(pairs)]
    for c in copies:
        c.start()

    def wait():
        for c in copies:
            c.wait()

    return wait


def learned():
    return lax.axis_index("grp") == 0


def dot(a, b):
    return jnp.dot(a, b, preferred_element_type=F32)


def silu(x):
    half = 0.5 * x
    return half + half * jnp.tanh(half)


def flip(x):
    return x.astype(F32).T


def split3(x):
    high = x.astype(BF16)
    rest = x - high.astype(F32)
    mid = rest.astype(BF16)
    low = (rest - mid.astype(F32)).astype(BF16)
    return jnp.concatenate([high, mid, low], axis=0)


def join3(x):
    return x[0:8] + x[8:16] + x[16:24]


def one_hot(row, depth):
    ids = lax.broadcasted_iota(jnp.int32, (depth, row.shape[1]), 0)
    return jnp.where(ids == row, 1.0, 0.0).astype(BF16)


def slot_row(slots, first, count):
    return jnp.concatenate([slots[pl.ds(first + i, 1), :] for i in range(count)], axis=1)


def rows(parts, count=8):
    have = sum(p.shape[0] for p in parts)
    return jnp.concatenate(list(parts) + [jnp.zeros((count - have, parts[0].shape[1]), F32)], axis=0)


def rows_kernel(
    pos_far, charge_far, polar_far, table_far, send_far, blocks_far,
    site, mine, lent_a, lent_b, slots, picks,
    pos, charge, polar, table, send, blocks, done,
):
    pairs = ((pos_far, pos), (charge_far, charge), (polar_far, polar), (table_far, table), (send_far, send))
    wait = fetch(pairs + ((blocks_far, blocks),), done)
    odd = lax.axis_index("sub")
    width = pos.shape[1]
    wait()
    sites = rows([pos[...], charge[...], polar[...]])
    site[...] = sites
    for half in range(2):
        mine[half] = sites[0:4, half * 128 : half * 128 + 128]
    first, second = send[0:1, :], send[1:2, :]
    swap = jnp.full(first.shape, odd, jnp.int32) == 1
    picks[0:1, :] = jnp.where(swap, second, first)
    picks[1:2, :] = jnp.where(swap, first, second)
    lane = lax.broadcasted_iota(jnp.int32, (1, 128), 1)
    listed = jnp.zeros((1, 128), jnp.int32)
    for l in range(blocks.shape[0]):
        listed = jnp.where(lane == l, blocks[l], listed)
    pieces = split3(sites)
    for row, out in ((0, lent_a), (1, lent_b)):
        found = join3(dot(pieces, one_hot(picks[row : row + 1, :], width)))
        out[...] = rows([found[0:5], listed.astype(F32), jnp.ones((1, 128), F32)])
    raw = table[...]
    other = jnp.where((raw >= 256) & (raw < 512), jnp.bitwise_xor(raw, 128), raw)
    keep = jnp.full(raw.shape, odd, jnp.int32) == 1
    slots[...] = jnp.where(keep, raw, other)


def static_kernel(
    site, rim_a, rim_b, slots, picks, features_far,
    feat_t, w3, w5, fixed, entry, lent_a, lent_b, features, done,
):
    width = site.shape[1]
    depth = 2 * width
    slot_count = slots.shape[0]

    @pl.when(learned())
    def _():
        fetch(((features_far, features),), done)()
        flipped = flip(features[...]).astype(BF16)
        feat_t[...] = flipped
        lend_channels(flipped, picks, lent_a, lent_b)

    @pl.when(jnp.logical_not(learned()))
    def _():
        table = jnp.concatenate([site[...], rim_a[...], rim_b[...]], axis=1)
        entry[...] = table.T
        tx, ty, tz = site[0:1, :], site[1:2, :], site[2:3, :]

        def some_rows(j, acc):
            start = pl.multiple_of(j * STATIC_CHUNK, STATIC_CHUNK)
            ids = lax.broadcasted_iota(jnp.int32, (STATIC_CHUNK, width), 0) + start
            count = jnp.zeros((STATIC_CHUNK, width), F32)
            for k in range(slot_count):
                count = count + jnp.where(ids == slots[k : k + 1, :], 1.0, 0.0)
            cols = entry[pl.ds(start, STATIC_CHUNK), :]
            rx, ry, rz = tx - cols[:, 0:1], ty - cols[:, 1:2], tz - cols[:, 2:3]
            inverse = lax.rsqrt(rx * rx + ry * ry + rz * rz + SMOOTH)
            squared = inverse * inverse
            cube = count * (squared * inverse)
            w3[pl.ds(start, STATIC_CHUNK), :] = cube
            w5[pl.ds(start, STATIC_CHUNK), :] = 3.0 * (cube * squared)
            scale = cols[:, 3:4] * cube
            return acc[0] + rx * scale, acc[1] + ry * scale, acc[2] + rz * scale

        nil = jnp.zeros((STATIC_CHUNK, width), F32)
        sums = lax.fori_loop(0, depth // STATIC_CHUNK, some_rows, (nil, nil, nil))
        total = rows([jnp.sum(s, axis=0, keepdims=True) for s in sums])
        fixed[...] = total
        lend_pieces(total, picks, lent_a, lent_b)


def radial_kernel(
    site, rim_a, rim_b, slots, w_in_far, w_mid_far,
    third_far, w_in, w_mid, third, done,
):
    width = site.shape[1]
    depth = 2 * width
    slot_count = slots.shape[0]

    @pl.when(learned())
    def _():
        wait = fetch(((w_in_far, w_in), (w_mid_far, w_mid)), done)
        pieces = split3(jnp.concatenate([site[...], rim_a[...], rim_b[...]], axis=1))
        step = RADIAL_SLOTS * width
        here = jnp.concatenate([site[...]] * RADIAL_SLOTS, axis=1)
        centres = lax.broadcasted_iota(jnp.int32, (BASIS, step), 0).astype(F32) * SPACING
        wait()
        first_w = jnp.concatenate([flip(w_in[0]), flip(w_in[1])], axis=0).astype(BF16)
        zero = jnp.zeros((64, 64), F32)

        def both(level):
            top = jnp.concatenate([flip(w_mid[0, level]), zero], axis=1)
            bottom = jnp.concatenate([zero, flip(w_mid[1, level])], axis=1)
            return jnp.concatenate([top, bottom], axis=0).astype(BF16)

        second_w, third_w = both(0), both(1)

        def some_slots(k, carry):
            found = join3(dot(pieces, one_hot(slot_row(slots, k * RADIAL_SLOTS, RADIAL_SLOTS), depth)))
            offset = here - found
            squares = offset * offset
            dist_sq = squares[0:1] + squares[1:2] + squares[2:3] + SMOOTH
            gap = jnp.sqrt(dist_sq) - centres
            basis = jnp.exp(-(gap * gap)).astype(BF16)
            hidden = silu(dot(first_w, basis)).astype(BF16)
            hidden = silu(dot(second_w, hidden)).astype(BF16)
            start = pl.multiple_of(k * step, step)
            third[:, pl.ds(start, step)] = silu(dot(third_w, hidden)).astype(BF16)
            return carry

        lax.fori_loop(0, slot_count // RADIAL_SLOTS, some_slots, 0)
        fetch(((third, third_far),), done, 2)()


def lend_pieces(values, picks, lent_a, lent_b):
    pieces = split3(values)
    for row, out in ((0, lent_a), (1, lent_b)):
        found = dot(pieces, one_hot(picks[row : row + 1, :], values.shape[1]))
        out[...] = jnp.zeros_like(out)
        out[0:32, :] = rows([found], 32).astype(BF16)


def lend_whole(values, picks, lent_a, lent_b):
    pieces = split3(values)
    for row, out in ((0, lent_a), (1, lent_b)):
        out[...] = join3(dot(pieces, one_hot(picks[row : row + 1, :], values.shape[1])))


def lend_channels(values, picks, lent_a, lent_b):
    for row, out in ((0, lent_a), (1, lent_b)):
        out[...] = dot(values, one_hot(picks[row : row + 1, :], values.shape[1])).astype(BF16)


def sweep(site, w3, w5, fixed, dipoles, entry, moment):
    width = site.shape[1]
    moment[...] = dipoles.T
    tx, ty, tz = site[0:1, :], site[1:2, :], site[2:3, :]

    def some_rows(j, acc):
        start = pl.multiple_of(j * SWEEP_CHUNK, SWEEP_CHUNK)
        cols, d = entry[pl.ds(start, SWEEP_CHUNK), :], moment[pl.ds(start, SWEEP_CHUNK), :]
        rx, ry, rz = tx - cols[:, 0:1], ty - cols[:, 1:2], tz - cols[:, 2:3]
        dx, dy, dz = d[:, 0:1], d[:, 1:2], d[:, 2:3]
        cube = w3[pl.ds(start, SWEEP_CHUNK), :]
        scale = (rx * dx + ry * dy + rz * dz) * w5[pl.ds(start, SWEEP_CHUNK), :]
        return (
            acc[0] + (rx * scale - dx * cube),
            acc[1] + (ry * scale - dy * cube),
            acc[2] + (rz * scale - dz * cube),
        )

    nil = jnp.zeros((SWEEP_CHUNK, width), F32)
    sums = lax.fori_loop(0, w3.shape[0] // SWEEP_CHUNK, some_rows, (nil, nil, nil), unroll=SWEEP_UNROLL)
    return site[4:5, :] * (fixed + rows([jnp.sum(s, axis=0, keepdims=True) for s in sums]))


def message(layer, hidden, table, third, out_t, node_t, slots, total):
    slot_count = slots.shape[0]
    width = slots.shape[1]
    step = MESSAGE_SLOTS * width
    total[...] = jnp.zeros_like(total)

    def some_slots(k, carry):
        row = slot_row(slots, k * MESSAGE_SLOTS, MESSAGE_SLOTS)
        picked = dot(table, one_hot(row, table.shape[1]))
        start = pl.multiple_of(k * step, step)
        weight = dot(out_t, third[layer * 64 : layer * 64 + 64, pl.ds(start, step)])
        product = weight * picked
        part = product[:, 0:width]
        for i in range(1, MESSAGE_SLOTS):
            part = part + product[:, i * width : (i + 1) * width]
        total[...] += part
        return carry

    lax.fori_loop(0, slot_count // MESSAGE_SLOTS, some_slots, 0)
    mean = (total[...] * (1.0 / slot_count)).astype(BF16)
    return (hidden.astype(F32) + silu(dot(node_t, mean))).astype(BF16)


def charge_field(target, cols, first, count):
    tx, ty, tz = target[0:1, :], target[1:2, :], target[2:3, :]

    def some_rows(j, acc):
        c = cols[pl.ds(pl.multiple_of(first + j * FIELD_CHUNK, FIELD_CHUNK), FIELD_CHUNK), :]
        rx, ry, rz = tx - c[:, 0:1], ty - c[:, 1:2], tz - c[:, 2:3]
        inverse = lax.rsqrt(rx * rx + ry * ry + rz * rz + SMOOTH)
        scale = c[:, 3:4] * (inverse * inverse * inverse)
        return acc[0] + rx * scale, acc[1] + ry * scale, acc[2] + rz * scale

    nil = jnp.zeros((FIELD_CHUNK, target.shape[1]), F32)
    sums = lax.fori_loop(0, count // FIELD_CHUNK, some_rows, (nil, nil, nil), unroll=FIELD_UNROLL)
    return jnp.concatenate([jnp.sum(s, axis=0, keepdims=True) for s in sums], axis=0)


def first_kernel(
    site, rim_a, rim_b, slots, picks, feat_t, side_a, side_b, w3, w5, fixed, entry,
    near_far, blocks_far, third_far, node_in_far, node_out_far, w_out_far, gain_far,
    outside_row, near_own, hidden_out, lifted_out, fixed_out, dipole_out, lent_a, lent_b,
    blocks, near, cols, third, node_in, node_out, w_out, gain, total, moment, done,
):
    width = site.shape[1]
    listed = blocks.shape[0]
    wait_blocks = fetch(((blocks_far, blocks),), done)
    weights = (
        (third_far, third), (node_in_far, node_in), (node_out_far.at[0], node_out),
        (w_out_far.at[0], w_out), (gain_far, gain),
    )

    @pl.when(learned())
    def _():
        fetch(weights, done, 1)

    lane = lax.broadcasted_iota(jnp.int32, (1, 128), 1)

    def lent_block(rim, l):
        return jnp.sum(jnp.where(lane == l, rim[5:6, :], 0.0)).astype(jnp.int32)

    numbers = [lent_block(rim, l) for rim in (rim_a, rim_b) for l in range(listed)]
    wait_blocks()
    numbers = [blocks[l] for l in range(listed)] + numbers
    fetch([(near_far.at[b], near.at[i]) for i, b in enumerate(numbers)], done, 6)()
    near_own[...] = near[0:listed]
    for i in range(3 * listed):
        tile = near[i]
        cols[i * 128 : i * 128 + 128, :] = jnp.concatenate([tile, tile], axis=0).T
    reach = listed * 128
    own_field = charge_field(site[...], cols, 0, reach)
    field = jnp.concatenate(
        [own_field, charge_field(rim_a[...], cols, reach, reach), charge_field(rim_b[...], cols, 2 * reach, reach)],
        axis=1,
    )
    strength = jnp.sqrt(1.0 + (field[0:1] * field[0:1] + field[1:2] * field[1:2] + field[2:3] * field[2:3]))
    outside_row[...] = jnp.broadcast_to(strength[:, :width], outside_row.shape)

    @pl.when(learned())
    def _():
        for i, (a, b) in enumerate(weights):
            pltpu.make_async_copy(a, b, done.at[1 + i]).wait()
        gain_col = jnp.broadcast_to(gain[...], (8, width)).T
        features = jnp.concatenate([feat_t[...], side_a[...], side_b[...]], axis=1)
        start = (features.astype(F32) + gain_col[:, 0:1] * strength).astype(BF16)
        present = jnp.concatenate([jnp.ones((1, width), F32), rim_a[6:7, :], rim_b[6:7, :]], axis=1)
        raised = dot(flip(node_in[0]).astype(BF16), start)
        table = jnp.where(present > 0.5, raised, 0.0).astype(BF16)
        out_t, node_t = flip(w_out[...]).astype(BF16), flip(node_out[...]).astype(BF16)
        new = message(0, start[:, :width], table, third, out_t, node_t, slots, total)
        hidden_out[...] = new
        raised = dot(flip(node_in[1]).astype(BF16), new).astype(BF16)
        lifted_out[...] = raised
        lend_channels(raised, picks, lent_a, lent_b)

    @pl.when(jnp.logical_not(learned()))
    def _():
        known = [fixed[...], join3(side_a[0:24, :].astype(F32)), join3(side_b[0:24, :].astype(F32))]
        whole = jnp.concatenate(known, axis=1) + rows([field])
        fixed_out[...] = whole[:, :width]
        polar = jnp.concatenate([site[4:5, :], rim_a[4:5, :], rim_b[4:5, :]], axis=1)
        new = sweep(site, w3, w5, whole[:, :width], polar * whole, entry, moment)
        dipole_out[...] = new
        lend_pieces(new, picks, lent_a, lent_b)


def second_kernel(
    hidden, lifted, side_a, side_b, slots, picks, site, w3, w5, fixed, dipole, entry,
    third_far, node_out_far, w_out_far, readout_far,
    charge, dipole_out, small_a, small_b,
    third, node_out, w_out, readout, total, moment, done,
):
    width = site.shape[1]

    @pl.when(learned())
    def _():
        fetch(
            ((third_far, third), (node_out_far.at[1], node_out), (w_out_far.at[1], w_out), (readout_far, readout)), done
        )()
        table = jnp.concatenate([lifted[...], side_a[...], side_b[...]], axis=1)
        out_t, node_t = flip(w_out[...]).astype(BF16), flip(node_out[...]).astype(BF16)
        new = message(1, hidden[...], table, third, out_t, node_t, slots, total)
        charge[...] = dot(rows([readout[...].astype(F32)]).astype(BF16), new)

    @pl.when(jnp.logical_not(learned()))
    def _():
        sides = [join3(side_a[0:24, :].astype(F32)), join3(side_b[0:24, :].astype(F32))]
        table = jnp.concatenate([dipole[...]] + sides, axis=1)
        new = sweep(site, w3, w5, fixed[...], table, entry, moment)
        dipole_out[...] = new
        lend_whole(new, picks, small_a, small_b)


def third_kernel(side_a, side_b, picks, site, w3, w5, fixed, dipole, entry, dipole_out, small_a, small_b, moment):
    @pl.when(jnp.logical_not(learned()))
    def _():
        table = jnp.concatenate([dipole[...], side_a[...], side_b[...]], axis=1)
        new = sweep(site, w3, w5, fixed[...], table, entry, moment)
        dipole_out[...] = new
        lend_whole(new, picks, small_a, small_b)


def response_kernel(
    near, site, charge, outside_row, side_a, side_b, w3, w5, fixed, dipole, entry, blocks_far,
    result, spread, blocks, cols, moment, term, done,
):
    width = site.shape[1]
    listed = blocks.shape[0]
    wait = fetch(((blocks_far, blocks),), done)
    spread[...] = jnp.zeros_like(spread)
    term[...] = jnp.zeros_like(term)

    def terms(dipoles):
        for l in range(listed):
            tile = near[l]
            tx, ty, tz = tile[0:1, :], tile[1:2, :], tile[2:3, :]

            def some_rows(j, acc):
                start = pl.multiple_of(j * TERM_CHUNK, TERM_CHUNK)
                c = cols[pl.ds(start, TERM_CHUNK), :]
                rx, ry, rz = tx - c[:, 0:1], ty - c[:, 1:2], tz - c[:, 2:3]
                inverse = lax.rsqrt(rx * rx + ry * ry + rz * rz + SMOOTH)
                squared = inverse * inverse
                cube = squared * inverse
                if dipoles:
                    dx, dy, dz = c[:, 4:5], c[:, 5:6], c[:, 6:7]
                    scale = (rx * dx + ry * dy + rz * dz) * (3.0 * (cube * squared))
                    return (
                        acc[0] + (rx * scale - dx * cube),
                        acc[1] + (ry * scale - dy * cube),
                        acc[2] + (rz * scale - dz * cube),
                    )
                scale = c[:, 3:4] * cube
                return acc[0] + rx * scale, acc[1] + ry * scale, acc[2] + rz * scale

            nil = jnp.zeros((TERM_CHUNK, 128), F32)
            sums = lax.fori_loop(0, width // TERM_CHUNK, some_rows, (nil, nil, nil), unroll=TERM_UNROLL)
            for axis in range(3):
                term[l, axis : axis + 1, :] = jnp.sum(sums[axis], axis=0, keepdims=True)

    @pl.when(learned())
    def _():
        q = charge[...]
        result[...] = jnp.concatenate([q[0:2], outside_row[0:1, :]], axis=0)
        cols[...] = rows([site[0:3, :], q[0:1]]).T
        terms(False)

    @pl.when(jnp.logical_not(learned()))
    def _():
        table = jnp.concatenate([dipole[...], side_a[...], side_b[...]], axis=1)
        new = sweep(site, w3, w5, fixed[...], table, entry, moment)
        result[...] = new[0:3]
        cols[...] = rows([site[0:4, :], new[0:3]]).T
        terms(True)

    wait()
    side = lax.broadcasted_iota(jnp.int32, (2, 128), 0)
    for l in range(listed):
        owner, part = blocks[l] >> 1, blocks[l] & 1
        for axis in range(3):
            spread[3 * owner + axis] += jnp.where(side == part, term[l, axis : axis + 1, :], 0.0)


def gather_kernel(pieces, share):
    total = jnp.sum(pieces[...], axis=0)
    share[...] = jnp.concatenate(
        [jnp.concatenate([total[axis, 0:1], total[axis, 1:2]], axis=1) for axis in range(3)], axis=0
    )


def local(
    positions, charges, polar, features, neighbours, send_rows, blocks,
    radial_in, radial_mid, radial_out, node_in, node_out, field_gain, readout,
):
    width = positions.shape[1]
    slot_count = neighbours.shape[1]
    depth = 2 * width
    half = send_rows.shape[1]
    channels = features.shape[1]
    listed = blocks.shape[0]
    members = lax.axis_size(DOM)
    near_pairs = [(i, i ^ 1) for i in range(members)]
    far_pairs = [(i, ((i - 1) ^ 1) + 1) for i in range(1, members - 1)]

    def trade(a, b, solvent_only=False):
        used = []
        for pairs in (near_pairs, far_pairs):
            shifted = [(x + members, y + members) for x, y in pairs]
            used.append(shifted if solvent_only else pairs + shifted)
        return lax.ppermute(a, EVERY, used[0]), lax.ppermute(b, EVERY, used[1])

    row8, table8 = ((8, width), F32), ((8, half), F32)
    wide = ((channels, half), BF16)
    by_site = ((channels, width), BF16)
    ints = jnp.int32
    site, mine, lent_a, lent_b, slots, picks = call(
        rows_kernel,
        [row8, ((2, 4, half), F32), table8, table8, ((slot_count, width), ints), ((2, half), ints)],
        (), (positions, charges[None], polar[None], neighbours.T, send_rows, blocks),
        [pltpu.VMEM((3, width), F32), pltpu.VMEM((1, width), F32), pltpu.VMEM((1, width), F32),
         pltpu.VMEM((slot_count, width), ints), pltpu.VMEM((2, half), ints), pltpu.SMEM((listed,), ints)], 6,
    )
    rim_a, rim_b = trade(lent_a, lent_b)
    partner = lax.ppermute(mine, "grp", [(0, 1), (1, 0)])
    partner, rim_a, rim_b = lax.optimization_barrier((partner, rim_a, rim_b))
    copies = jnp.broadcast_to(partner[None], (members,) + partner.shape)
    near = lax.all_to_all(copies, DOM, 0, 0, tiled=True).reshape(2 * members, 4, half)
    feat_t, w3, w5, fixed, entry, lent_a, lent_b = call(
        static_kernel, [by_site, ((depth, width), F32), ((depth, width), F32), row8, ((depth, 8), F32), wide, wide],
        (site, rim_a, rim_b, slots, picks), (features,), [pltpu.VMEM((width, channels), BF16)], 1,
    )
    side_a, side_b = trade(lent_a, lent_b)
    third_shape = (LAYERS * radial_in.shape[2], slot_count * width)
    (third,) = call(
        radial_kernel, [(third_shape, BF16)], (site, rim_a, rim_b, slots), (radial_in, radial_mid),
        [pltpu.VMEM(radial_in.shape, BF16), pltpu.VMEM(radial_mid.shape, BF16), pltpu.VMEM(third_shape, BF16)], 3, 1,
    )
    moment = pltpu.VMEM((depth, 8), F32)
    total = pltpu.VMEM((channels, width), F32)
    square = pltpu.VMEM(node_out.shape[1:], BF16)
    last = pltpu.VMEM(radial_out.shape[1:], BF16)
    outside_row, near_own, hidden, lifted, fixed_all, dipole, lent_a, lent_b = call(
        first_kernel, [row8, ((listed, 4, half), F32), by_site, by_site, row8, row8, wide, wide],
        (site, rim_a, rim_b, slots, picks, feat_t, side_a, side_b, w3, w5, fixed, entry),
        (near, blocks, third, node_in, node_out, radial_out, field_gain[None]),
        [pltpu.SMEM((listed,), ints), pltpu.VMEM((3 * listed, 4, half), F32), pltpu.VMEM((3 * listed * half, 8), F32),
         pltpu.VMEM(third_shape, BF16), pltpu.VMEM(node_in.shape, BF16), square, last,
         pltpu.VMEM((1, channels), F32), total, moment], 6 + 3 * listed, loose=1,
    )
    side_a, side_b = trade(lent_a, lent_b)
    charge, dipole, small_a, small_b = call(
        second_kernel, [row8, row8, table8, table8],
        (hidden, lifted, side_a, side_b, slots, picks, site, w3, w5, fixed_all, dipole, entry),
        (third, node_out, radial_out, readout.T),
        [pltpu.VMEM(third_shape, BF16), square, last, pltpu.VMEM((2, channels), BF16), total, moment], 4,
    )
    side_a, side_b = trade(small_a, small_b, True)
    dipole, small_a, small_b = call(
        third_kernel, [row8, table8, table8], (side_a, side_b, picks, site, w3, w5, fixed_all, dipole, entry),
        (), [moment],
    )
    side_a, side_b = trade(small_a, small_b, True)
    result, spread = call(
        response_kernel, [((3, width), F32), ((3 * members, 2, half), F32)],
        (near_own, site, charge, outside_row, side_a, side_b, w3, w5, fixed_all, dipole, entry), (blocks,),
        [pltpu.SMEM((listed,), ints), pltpu.VMEM((width, 8), F32), moment, pltpu.VMEM((listed, 4, half), F32)], 1,
    )
    pieces = lax.all_to_all(spread, DOM, 0, 0, tiled=True).reshape(members, 3, 2, half)
    (share,) = call(gather_kernel, [((3, width), F32)], (pieces,))
    return result, lax.ppermute(share, "grp", [(0, 1), (1, 0)])


def solution(mesh):
    sites = P(None, EVERY)
    in_specs = (sites, P(EVERY), P(EVERY), P(EVERY, None), P(EVERY, None), sites, P(EVERY)) + (P(),) * 7
    return jax.shard_map(local, mesh=mesh, in_specs=in_specs, out_specs=(sites, sites), check_vma=False)
```

```python
import jax
import jax.numpy as jnp
from jax import lax
from jax.experimental import pallas as pl
from jax.experimental.pallas import tpu as pltpu
from jax.sharding import PartitionSpec as P

BASIS = 8
LAYERS = 2
SMOOTH = 1.0
SPACING = 0.75
DOM = ("dom", "sub")
EVERY = ("grp", "dom", "sub")
F32 = jnp.float32
BF16 = jnp.bfloat16
VMEM = pl.BlockSpec(memory_space=pltpu.VMEM)
ANY = pl.BlockSpec(memory_space=pl.ANY)
SWEEP_CHUNK, SWEEP_UNROLL = 32, 4
FIELD_CHUNK, FIELD_UNROLL = 32, 4
TERM_CHUNK, TERM_UNROLL = 64, 4
STATIC_CHUNK = 32
RADIAL_SLOTS = 8
MESSAGE_SLOTS = 8


def call(body, outs, held, far=(), scratch=(), copies=0, far_outs=0, loose=0):
    return pl.pallas_call(
        body,
        out_shape=[jax.ShapeDtypeStruct(s, d) for s, d in outs[: len(outs) - far_outs]]
        + [pltpu.HBM(s, d) for s, d in outs[len(outs) - far_outs :]],
        in_specs=[VMEM] * len(held) + [ANY] * len(far),
        out_specs=[VMEM] * (len(outs) - far_outs) + [ANY] * far_outs,
        scratch_shapes=list(scratch) + ([pltpu.SemaphoreType.DMA((copies,))] if copies else []),
        compiler_params=pltpu.CompilerParams(vmem_limit_bytes=24 * 2**20),
    )(*held, *far[:loose], *[pltpu.with_memory_space_constraint(a, pltpu.HBM) for a in far[loose:]])


def fetch(pairs, done, first=0):
    copies = [pltpu.make_async_copy(a, b, done.at[first + i]) for i, (a, b) in enumerate(pairs)]
    for c in copies:
        c.start()

    def wait():
        for c in copies:
            c.wait()

    return wait


def learned():
    return lax.axis_index("grp") == 0


def dot(a, b):
    return jnp.dot(a, b, preferred_element_type=F32)


def silu(x):
    half = 0.5 * x
    return half + half * jnp.tanh(half)


def flip(x):
    return x.astype(F32).T


def split3(x):
    high = x.astype(BF16)
    rest = x - high.astype(F32)
    mid = rest.astype(BF16)
    low = (rest - mid.astype(F32)).astype(BF16)
    return jnp.concatenate([high, mid, low], axis=0)


def join3(x):
    return x[0:8] + x[8:16] + x[16:24]


def one_hot(row, depth):
    ids = lax.broadcasted_iota(jnp.int32, (depth, row.shape[1]), 0)
    return jnp.where(ids == row.astype(jnp.int32), 1.0, 0.0).astype(BF16)


def views(pack):
    return pack.at[0:8, :], pack.at[8:40, :], pack.at[40:41, :]


def picked_row(picks, row):
    return picks[0:1, row * 128 : row * 128 + 128]


def listed_block(row, l):
    lane = lax.broadcasted_iota(jnp.int32, row.shape, 1)
    return jnp.sum(jnp.where(lane == l, row, 0.0)).astype(jnp.int32)


def slot_row(slots, first, count):
    return jnp.concatenate([slots[pl.ds(first + i, 1), :] for i in range(count)], axis=1)


def rows(parts, count=8):
    have = sum(p.shape[0] for p in parts)
    return jnp.concatenate(list(parts) + [jnp.zeros((count - have, parts[0].shape[1]), F32)], axis=0)


def rows_kernel(
    pos_far, charge_far, polar_far, table_far, send_far, blocks_far,
    pack, mine, lent_a, lent_b,
    pos, charge, polar, table, send, blocks, done,
):
    pairs = ((pos_far, pos), (charge_far, charge), (polar_far, polar), (table_far, table), (send_far, send))
    wait = fetch(pairs + ((blocks_far, blocks),), done)
    odd = lax.axis_index("sub")
    width = pos.shape[1]
    wait()
    lane = lax.broadcasted_iota(jnp.int32, (1, width), 1)
    listed = jnp.zeros((1, width), jnp.int32)
    for l in range(blocks.shape[0]):
        listed = jnp.where(lane == l, blocks[l], listed)
    listed = listed.astype(F32)
    sites = rows([pos[...], charge[...], polar[...], listed, jnp.ones((1, width), F32)])
    for half in range(2):
        mine[half] = sites[0:4, half * 128 : half * 128 + 128]
    first, second = send[0:1, :], send[1:2, :]
    swap = jnp.full(first.shape, odd, jnp.int32) == 1
    picks = jnp.where(swap, second, first), jnp.where(swap, first, second)
    raw = table[...]
    other = jnp.where((raw >= 256) & (raw < 512), jnp.bitwise_xor(raw, 128), raw)
    keep = jnp.full(raw.shape, odd, jnp.int32) == 1
    pack[0:8, :] = sites
    pack[8:40, :] = jnp.where(keep, raw, other).astype(F32)
    pack[40:48, :] = rows([jnp.concatenate(picks, axis=1).astype(F32)])
    pieces = split3(sites)
    for row, out in zip(picks, (lent_a, lent_b)):
        found = join3(dot(pieces, one_hot(row, width)))
        out[...] = rows([found[0:5], listed[:, 0:128], jnp.ones((1, 128), F32)])


def static_kernel(
    pack, rim_a, rim_b, features_far,
    feat_t, w3, w5, fixed, entry, lent_a, lent_b, features, done,
):
    site, slots, picks = views(pack)
    width = site.shape[1]
    depth = 2 * width
    slot_count = slots.shape[0]

    @pl.when(learned())
    def _():
        fetch(((features_far, features),), done)()
        flipped = flip(features[...]).astype(BF16)
        feat_t[...] = flipped
        lend_channels(flipped, picks, lent_a, lent_b)

    @pl.when(jnp.logical_not(learned()))
    def _():
        table = jnp.concatenate([site[...], rim_a[...], rim_b[...]], axis=1)
        entry[...] = table.T
        tx, ty, tz = site[0:1, :], site[1:2, :], site[2:3, :]

        def some_rows(j, acc):
            start = pl.multiple_of(j * STATIC_CHUNK, STATIC_CHUNK)
            ids = (lax.broadcasted_iota(jnp.int32, (STATIC_CHUNK, width), 0) + start).astype(F32)
            count = jnp.zeros((STATIC_CHUNK, width), F32)
            for k in range(slot_count):
                count = count + jnp.where(ids == slots[k : k + 1, :], 1.0, 0.0)
            cols = entry[pl.ds(start, STATIC_CHUNK), :]
            rx, ry, rz = tx - cols[:, 0:1], ty - cols[:, 1:2], tz - cols[:, 2:3]
            inverse = lax.rsqrt(rx * rx + ry * ry + rz * rz + SMOOTH)
            squared = inverse * inverse
            cube = count * (squared * inverse)
            w3[pl.ds(start, STATIC_CHUNK), :] = cube
            w5[pl.ds(start, STATIC_CHUNK), :] = 3.0 * (cube * squared)
            scale = cols[:, 3:4] * cube
            return acc[0] + rx * scale, acc[1] + ry * scale, acc[2] + rz * scale

        nil = jnp.zeros((STATIC_CHUNK, width), F32)
        sums = lax.fori_loop(0, depth // STATIC_CHUNK, some_rows, (nil, nil, nil))
        total = rows([jnp.sum(s, axis=0, keepdims=True) for s in sums])
        fixed[...] = total
        lend_pieces(total, picks, lent_a, lent_b)


def radial_kernel(
    pack, rim_a, rim_b, w_in_far, w_mid_far,
    third_far, w_in, w_mid, third, done,
):
    site, slots, _ = views(pack)
    width = site.shape[1]
    depth = 2 * width
    slot_count = slots.shape[0]

    @pl.when(learned())
    def _():
        wait = fetch(((w_in_far, w_in), (w_mid_far, w_mid)), done)
        pieces = split3(jnp.concatenate([site[...], rim_a[...], rim_b[...]], axis=1))
        step = RADIAL_SLOTS * width
        here = jnp.concatenate([site[...]] * RADIAL_SLOTS, axis=1)
        centres = lax.broadcasted_iota(jnp.int32, (BASIS, step), 0).astype(F32) * SPACING
        wait()
        first_w = jnp.concatenate([flip(w_in[0]), flip(w_in[1])], axis=0).astype(BF16)
        zero = jnp.zeros((64, 64), F32)

        def both(level):
            top = jnp.concatenate([flip(w_mid[0, level]), zero], axis=1)
            bottom = jnp.concatenate([zero, flip(w_mid[1, level])], axis=1)
            return jnp.concatenate([top, bottom], axis=0).astype(BF16)

        second_w, third_w = both(0), both(1)

        def some_slots(k, carry):
            found = join3(dot(pieces, one_hot(slot_row(slots, k * RADIAL_SLOTS, RADIAL_SLOTS), depth)))
            offset = here - found
            squares = offset * offset
            dist_sq = squares[0:1] + squares[1:2] + squares[2:3] + SMOOTH
            gap = jnp.sqrt(dist_sq) - centres
            basis = jnp.exp(-(gap * gap)).astype(BF16)
            hidden = silu(dot(first_w, basis)).astype(BF16)
            hidden = silu(dot(second_w, hidden)).astype(BF16)
            start = pl.multiple_of(k * step, step)
            third[:, pl.ds(start, step)] = silu(dot(third_w, hidden)).astype(BF16)
            return carry

        lax.fori_loop(0, slot_count // RADIAL_SLOTS, some_slots, 0)
        fetch(((third, third_far),), done, 2)()


def lend_pieces(values, picks, lent_a, lent_b):
    pieces = split3(values)
    for row, out in ((0, lent_a), (1, lent_b)):
        found = dot(pieces, one_hot(picked_row(picks, row), values.shape[1]))
        out[...] = jnp.zeros_like(out)
        out[0:32, :] = rows([found], 32).astype(BF16)


def lend_whole(values, picks, lent_a, lent_b):
    pieces = split3(values)
    for row, out in ((0, lent_a), (1, lent_b)):
        out[...] = join3(dot(pieces, one_hot(picked_row(picks, row), values.shape[1])))


def lend_channels(values, picks, lent_a, lent_b):
    for row, out in ((0, lent_a), (1, lent_b)):
        out[...] = dot(values, one_hot(picked_row(picks, row), values.shape[1])).astype(BF16)


def sweep(site, w3, w5, fixed, dipoles, entry, moment):
    width = site.shape[1]
    moment[...] = dipoles.T
    tx, ty, tz = site[0:1, :], site[1:2, :], site[2:3, :]

    def some_rows(j, acc):
        start = pl.multiple_of(j * SWEEP_CHUNK, SWEEP_CHUNK)
        cols, d = entry[pl.ds(start, SWEEP_CHUNK), :], moment[pl.ds(start, SWEEP_CHUNK), :]
        rx, ry, rz = tx - cols[:, 0:1], ty - cols[:, 1:2], tz - cols[:, 2:3]
        dx, dy, dz = d[:, 0:1], d[:, 1:2], d[:, 2:3]
        cube = w3[pl.ds(start, SWEEP_CHUNK), :]
        scale = (rx * dx + ry * dy + rz * dz) * w5[pl.ds(start, SWEEP_CHUNK), :]
        return (
            acc[0] + (rx * scale - dx * cube),
            acc[1] + (ry * scale - dy * cube),
            acc[2] + (rz * scale - dz * cube),
        )

    nil = jnp.zeros((SWEEP_CHUNK, width), F32)
    sums = lax.fori_loop(0, w3.shape[0] // SWEEP_CHUNK, some_rows, (nil, nil, nil), unroll=SWEEP_UNROLL)
    return site[4:5, :] * (fixed + rows([jnp.sum(s, axis=0, keepdims=True) for s in sums]))


def message(layer, hidden, table, third, out_t, node_t, slots, total):
    slot_count = slots.shape[0]
    width = slots.shape[1]
    step = MESSAGE_SLOTS * width
    total[...] = jnp.zeros_like(total)

    def some_slots(k, carry):
        row = slot_row(slots, k * MESSAGE_SLOTS, MESSAGE_SLOTS)
        picked = dot(table, one_hot(row, table.shape[1]))
        start = pl.multiple_of(k * step, step)
        weight = dot(out_t, third[layer * 64 : layer * 64 + 64, pl.ds(start, step)])
        product = weight * picked
        part = product[:, 0:width]
        for i in range(1, MESSAGE_SLOTS):
            part = part + product[:, i * width : (i + 1) * width]
        total[...] += part
        return carry

    lax.fori_loop(0, slot_count // MESSAGE_SLOTS, some_slots, 0)
    mean = (total[...] * (1.0 / slot_count)).astype(BF16)
    return (hidden.astype(F32) + silu(dot(node_t, mean))).astype(BF16)


def charge_field(target, cols, first, count):
    tx, ty, tz = target[0:1, :], target[1:2, :], target[2:3, :]

    def some_rows(j, acc):
        c = cols[pl.ds(pl.multiple_of(first + j * FIELD_CHUNK, FIELD_CHUNK), FIELD_CHUNK), :]
        rx, ry, rz = tx - c[:, 0:1], ty - c[:, 1:2], tz - c[:, 2:3]
        inverse = lax.rsqrt(rx * rx + ry * ry + rz * rz + SMOOTH)
        scale = c[:, 3:4] * (inverse * inverse * inverse)
        return acc[0] + rx * scale, acc[1] + ry * scale, acc[2] + rz * scale

    nil = jnp.zeros((FIELD_CHUNK, target.shape[1]), F32)
    sums = lax.fori_loop(0, count // FIELD_CHUNK, some_rows, (nil, nil, nil), unroll=FIELD_UNROLL)
    return jnp.concatenate([jnp.sum(s, axis=0, keepdims=True) for s in sums], axis=0)


def first_kernel(
    pack, rim_a, rim_b, feat_t, side_a, side_b, w3, w5, fixed, entry,
    near_far, third_far, node_in_far, node_out_far, w_out_far, gain_far,
    outside_row, near_own, hidden_out, lifted_out, fixed_out, dipole_out, lent_a, lent_b,
    near, cols, third, node_in, node_out, w_out, gain, total, moment, done,
):
    site, slots, picks = views(pack)
    width = site.shape[1]
    listed = near_own.shape[0]
    numbers = [listed_block(row[5:6, 0:128], l) for row in (site, rim_a, rim_b) for l in range(listed)]
    fetch([(near_far.at[b], near.at[i]) for i, b in enumerate(numbers)], done, 5)
    weights = (
        (third_far, third), (node_in_far, node_in), (node_out_far.at[0], node_out),
        (w_out_far.at[0], w_out), (gain_far, gain),
    )

    @pl.when(learned())
    def _():
        fetch(weights, done)

    for i, b in enumerate(numbers):
        pltpu.make_async_copy(near_far.at[b], near.at[i], done.at[5 + i]).wait()
    near_own[...] = near[0:listed]
    for i in range(3 * listed):
        tile = near[i]
        cols[i * 128 : i * 128 + 128, :] = jnp.concatenate([tile, tile], axis=0).T
    reach = listed * 128
    own_field = charge_field(site[...], cols, 0, reach)
    field = jnp.concatenate(
        [own_field, charge_field(rim_a[...], cols, reach, reach), charge_field(rim_b[...], cols, 2 * reach, reach)],
        axis=1,
    )
    strength = jnp.sqrt(1.0 + (field[0:1] * field[0:1] + field[1:2] * field[1:2] + field[2:3] * field[2:3]))
    outside_row[...] = jnp.broadcast_to(strength[:, :width], outside_row.shape)

    @pl.when(learned())
    def _():
        for i, (a, b) in enumerate(weights):
            pltpu.make_async_copy(a, b, done.at[i]).wait()
        gain_col = jnp.broadcast_to(gain[...], (8, width)).T
        features = jnp.concatenate([feat_t[...], side_a[...], side_b[...]], axis=1)
        start = (features.astype(F32) + gain_col[:, 0:1] * strength).astype(BF16)
        present = jnp.concatenate([jnp.ones((1, width), F32), rim_a[6:7, :], rim_b[6:7, :]], axis=1)
        raised = dot(flip(node_in[0]).astype(BF16), start)
        table = jnp.where(present > 0.5, raised, 0.0).astype(BF16)
        out_t, node_t = flip(w_out[...]).astype(BF16), flip(node_out[...]).astype(BF16)
        new = message(0, start[:, :width], table, third, out_t, node_t, slots, total)
        hidden_out[...] = new
        raised = dot(flip(node_in[1]).astype(BF16), new).astype(BF16)
        lifted_out[...] = raised
        lend_channels(raised, picks, lent_a, lent_b)

    @pl.when(jnp.logical_not(learned()))
    def _():
        known = [fixed[...], join3(side_a[0:24, :].astype(F32)), join3(side_b[0:24, :].astype(F32))]
        whole = jnp.concatenate(known, axis=1) + rows([field])
        fixed_out[...] = whole[:, :width]
        polar = jnp.concatenate([site[4:5, :], rim_a[4:5, :], rim_b[4:5, :]], axis=1)
        new = sweep(site, w3, w5, whole[:, :width], polar * whole, entry, moment)
        dipole_out[...] = new
        lend_pieces(new, picks, lent_a, lent_b)


def second_kernel(
    hidden, lifted, side_a, side_b, pack, w3, w5, fixed, dipole, entry,
    third_far, node_out_far, w_out_far, readout_far,
    charge, dipole_out, small_a, small_b,
    third, node_out, w_out, readout, total, moment, done,
):
    site, slots, picks = views(pack)

    @pl.when(learned())
    def _():
        fetch(
            ((third_far, third), (node_out_far.at[1], node_out), (w_out_far.at[1], w_out), (readout_far, readout)), done
        )()
        table = jnp.concatenate([lifted[...], side_a[...], side_b[...]], axis=1)
        out_t, node_t = flip(w_out[...]).astype(BF16), flip(node_out[...]).astype(BF16)
        new = message(1, hidden[...], table, third, out_t, node_t, slots, total)
        charge[...] = dot(rows([readout[...].astype(F32)]).astype(BF16), new)

    @pl.when(jnp.logical_not(learned()))
    def _():
        sides = [join3(side_a[0:24, :].astype(F32)), join3(side_b[0:24, :].astype(F32))]
        table = jnp.concatenate([dipole[...]] + sides, axis=1)
        new = sweep(site, w3, w5, fixed[...], table, entry, moment)
        dipole_out[...] = new
        lend_whole(new, picks, small_a, small_b)


def third_kernel(side_a, side_b, pack, w3, w5, fixed, dipole, entry, dipole_out, small_a, small_b, moment):
    site, _, picks = views(pack)

    @pl.when(jnp.logical_not(learned()))
    def _():
        table = jnp.concatenate([dipole[...], side_a[...], side_b[...]], axis=1)
        new = sweep(site, w3, w5, fixed[...], table, entry, moment)
        dipole_out[...] = new
        lend_whole(new, picks, small_a, small_b)


def response_kernel(
    near, pack, charge, outside_row, side_a, side_b, w3, w5, fixed, dipole, entry,
    result, spread, cols, moment, term,
):
    site = views(pack)[0]
    width = site.shape[1]
    listed = near.shape[0]
    blocks = [listed_block(site[5:6, 0:128], l) for l in range(listed)]
    spread[...] = jnp.zeros_like(spread)
    term[...] = jnp.zeros_like(term)

    def terms(dipoles):
        for l in range(listed):
            tile = near[l]
            tx, ty, tz = tile[0:1, :], tile[1:2, :], tile[2:3, :]

            def some_rows(j, acc):
                start = pl.multiple_of(j * TERM_CHUNK, TERM_CHUNK)
                c = cols[pl.ds(start, TERM_CHUNK), :]
                rx, ry, rz = tx - c[:, 0:1], ty - c[:, 1:2], tz - c[:, 2:3]
                inverse = lax.rsqrt(rx * rx + ry * ry + rz * rz + SMOOTH)
                squared = inverse * inverse
                cube = squared * inverse
                if dipoles:
                    dx, dy, dz = c[:, 4:5], c[:, 5:6], c[:, 6:7]
                    scale = (rx * dx + ry * dy + rz * dz) * (3.0 * (cube * squared))
                    return (
                        acc[0] + (rx * scale - dx * cube),
                        acc[1] + (ry * scale - dy * cube),
                        acc[2] + (rz * scale - dz * cube),
                    )
                scale = c[:, 3:4] * cube
                return acc[0] + rx * scale, acc[1] + ry * scale, acc[2] + rz * scale

            nil = jnp.zeros((TERM_CHUNK, 128), F32)
            sums = lax.fori_loop(0, width // TERM_CHUNK, some_rows, (nil, nil, nil), unroll=TERM_UNROLL)
            for axis in range(3):
                term[l, axis : axis + 1, :] = jnp.sum(sums[axis], axis=0, keepdims=True)

    @pl.when(learned())
    def _():
        q = charge[...]
        result[...] = jnp.concatenate([q[0:2], outside_row[0:1, :]], axis=0)
        cols[...] = rows([site[0:3, :], q[0:1]]).T
        terms(False)

    @pl.when(jnp.logical_not(learned()))
    def _():
        table = jnp.concatenate([dipole[...], side_a[...], side_b[...]], axis=1)
        new = sweep(site, w3, w5, fixed[...], table, entry, moment)
        result[...] = new[0:3]
        cols[...] = rows([site[0:4, :], new[0:3]]).T
        terms(True)

    side = lax.broadcasted_iota(jnp.int32, (2, 128), 0)
    for l in range(listed):
        owner, part = blocks[l] >> 1, blocks[l] & 1
        for axis in range(3):
            spread[3 * owner + axis] += jnp.where(side == part, term[l, axis : axis + 1, :], 0.0)


def gather_kernel(pieces, share):
    total = jnp.sum(pieces[...], axis=0)
    share[...] = jnp.concatenate(
        [jnp.concatenate([total[axis, 0:1], total[axis, 1:2]], axis=1) for axis in range(3)], axis=0
    )


def placed(block):
    y_half, z, step, side = block // 64, block // 8 % 8, block // 2 % 4, block % 2
    x = 3 - step if z % 2 else step
    along = 1 - side if step % 2 else side
    y = 3 - along if y_half else along
    return ((y % 2 * 8 + z) * 4 + x) * 2 + y // 2


def local(
    positions, charges, polar, features, neighbours, send_rows, blocks,
    radial_in, radial_mid, radial_out, node_in, node_out, field_gain, readout,
):
    width = positions.shape[1]
    slot_count = neighbours.shape[1]
    depth = 2 * width
    half = send_rows.shape[1]
    channels = features.shape[1]
    listed = blocks.shape[0]
    members = lax.axis_size(DOM)
    near_pairs = [(i, i ^ 1) for i in range(members)]
    far_pairs = [(i, ((i - 1) ^ 1) + 1) for i in range(1, members - 1)]
    same = list(range(members))
    place = [placed(i) for i in range(members)]

    def move(value, pairs, source, target, groups=(0, 1)):
        return lax.ppermute(
            value, EVERY, [(source[a] + g * members, target[b] + g * members) for g in groups for a, b in pairs]
        )

    def trade(a, b, groups=(0, 1), source=place):
        return move(a, near_pairs, source, place, groups), move(b, far_pairs, source, place, groups)

    row8, table8 = ((8, width), F32), ((8, half), F32)
    wide = ((channels, half), BF16)
    by_site = ((channels, width), BF16)
    ints = jnp.int32
    itself = [(i, i) for i in range(members)]
    pack, mine, lent_a, lent_b = call(
        rows_kernel, [((slot_count + 16, width), F32), ((2, 4, half), F32), table8, table8],
        (), (positions, charges[None], polar[None], neighbours.T, send_rows, blocks),
        [pltpu.VMEM((3, width), F32), pltpu.VMEM((1, width), F32), pltpu.VMEM((1, width), F32),
         pltpu.VMEM((slot_count, width), ints), pltpu.VMEM((2, half), ints), pltpu.SMEM((listed,), ints)], 6,
    )
    partner = lax.ppermute(mine, "grp", [(0, 1), (1, 0)])
    copies = jnp.broadcast_to(partner[None], (members,) + partner.shape)
    near = lax.all_to_all(copies, DOM, 0, 0, tiled=True).reshape(2 * members, 4, half)
    pack = move(pack, itself, same, place)
    rim_a, rim_b = trade(lent_a, lent_b, source=same)
    features = move(features, itself, same, place, (0,))
    feat_t, w3, w5, fixed, entry, lent_a, lent_b = call(
        static_kernel, [by_site, ((depth, width), F32), ((depth, width), F32), row8, ((depth, 8), F32), wide, wide],
        (pack, rim_a, rim_b), (features,), [pltpu.VMEM((width, channels), BF16)], 1, loose=1,
    )
    side_a, side_b = trade(lent_a, lent_b)
    third_shape = (LAYERS * radial_in.shape[2], slot_count * width)
    (third,) = call(
        radial_kernel, [(third_shape, BF16)], (pack, rim_a, rim_b), (radial_in, radial_mid),
        [pltpu.VMEM(radial_in.shape, BF16), pltpu.VMEM(radial_mid.shape, BF16), pltpu.VMEM(third_shape, BF16)], 3, 1,
    )
    moment = pltpu.VMEM((depth, 8), F32)
    total = pltpu.VMEM((channels, width), F32)
    square = pltpu.VMEM(node_out.shape[1:], BF16)
    last = pltpu.VMEM(radial_out.shape[1:], BF16)
    outside_row, near_own, hidden, lifted, fixed_all, dipole, lent_a, lent_b = call(
        first_kernel, [row8, ((listed, 4, half), F32), by_site, by_site, row8, row8, wide, wide],
        (pack, rim_a, rim_b, feat_t, side_a, side_b, w3, w5, fixed, entry),
        (near, third, node_in, node_out, radial_out, field_gain[None]),
        [pltpu.VMEM((3 * listed, 4, half), F32), pltpu.VMEM((3 * listed * half, 8), F32),
         pltpu.VMEM(third_shape, BF16), pltpu.VMEM(node_in.shape, BF16), square, last,
         pltpu.VMEM((1, channels), F32), total, moment], 5 + 3 * listed, loose=1,
    )
    side_a, side_b = trade(lent_a, lent_b)
    charge, dipole, small_a, small_b = call(
        second_kernel, [row8, row8, table8, table8],
        (hidden, lifted, side_a, side_b, pack, w3, w5, fixed_all, dipole, entry),
        (third, node_out, radial_out, readout.T),
        [pltpu.VMEM(third_shape, BF16), square, last, pltpu.VMEM((2, channels), BF16), total, moment], 4,
    )
    side_a, side_b = trade(small_a, small_b, (1,))
    dipole, small_a, small_b = call(
        third_kernel, [row8, table8, table8], (side_a, side_b, pack, w3, w5, fixed_all, dipole, entry),
        (), [moment],
    )
    side_a, side_b = trade(small_a, small_b, (1,))
    result, spread = call(
        response_kernel, [((3, width), F32), ((3 * members, 2, half), F32)],
        (near_own, pack, charge, outside_row, side_a, side_b, w3, w5, fixed_all, dipole, entry), (),
        [pltpu.VMEM((width, 8), F32), moment, pltpu.VMEM((listed, 4, half), F32)],
    )
    pieces = lax.all_to_all(spread, DOM, 0, 0, tiled=True).reshape(members, 3, 2, half)
    (share,) = call(gather_kernel, [((3, width), F32)], (pieces,))
    result = move(result, itself, place, same)
    return result, lax.ppermute(share, "grp", [(0, 1), (1, 0)])


def solution(mesh):
    sites = P(None, EVERY)
    in_specs = (sites, P(EVERY), P(EVERY), P(EVERY, None), P(EVERY, None), sites, P(EVERY)) + (P(),) * 7
    return jax.shard_map(local, mesh=mesh, in_specs=in_specs, out_specs=(sites, sites), check_vma=False)
```

```python
import jax
import jax.numpy as jnp
from jax import lax
from jax.experimental import pallas as pl
from jax.experimental.pallas import tpu as pltpu
from jax.sharding import PartitionSpec as P

BASIS = 8
LAYERS = 2
SMOOTH = 1.0
SPACING = 0.75
DOM = ("dom", "sub")
EVERY = ("grp", "dom", "sub")
F32 = jnp.float32
BF16 = jnp.bfloat16
VMEM = pl.BlockSpec(memory_space=pltpu.VMEM)
ANY = pl.BlockSpec(memory_space=pl.ANY)
SWEEP_CHUNK, SWEEP_UNROLL = 32, 4
FIELD_CHUNK, FIELD_UNROLL = 32, 4
TERM_CHUNK, TERM_UNROLL = 64, 4
STATIC_CHUNK = 32
RADIAL_SLOTS = 8
MESSAGE_SLOTS = 8


def call(body, outs, held, far=(), scratch=(), copies=0, far_outs=0, loose=0):
    return pl.pallas_call(
        body,
        out_shape=[jax.ShapeDtypeStruct(s, d) for s, d in outs[: len(outs) - far_outs]]
        + [pltpu.HBM(s, d) for s, d in outs[len(outs) - far_outs :]],
        in_specs=[VMEM] * len(held) + [ANY] * len(far),
        out_specs=[VMEM] * (len(outs) - far_outs) + [ANY] * far_outs,
        scratch_shapes=list(scratch) + ([pltpu.SemaphoreType.DMA((copies,))] if copies else []),
        compiler_params=pltpu.CompilerParams(vmem_limit_bytes=24 * 2**20),
    )(*held, *far[:loose], *[pltpu.with_memory_space_constraint(a, pltpu.HBM) for a in far[loose:]])


def fetch(pairs, done, first=0):
    copies = [pltpu.make_async_copy(a, b, done.at[first + i]) for i, (a, b) in enumerate(pairs)]
    for c in copies:
        c.start()

    def wait():
        for c in copies:
            c.wait()

    return wait


def learned():
    return lax.axis_index("grp") == 0


def dot(a, b):
    return jnp.dot(a, b, preferred_element_type=F32)


def silu(x):
    half = 0.5 * x
    return half + half * jnp.tanh(half)


def flip(x):
    return x.astype(F32).T


def split3(x):
    high = x.astype(BF16)
    rest = x - high.astype(F32)
    mid = rest.astype(BF16)
    low = (rest - mid.astype(F32)).astype(BF16)
    return jnp.concatenate([high, mid, low], axis=0)


def join3(x):
    return x[0:8] + x[8:16] + x[16:24]


def one_hot(row, depth):
    ids = lax.broadcasted_iota(jnp.int32, (depth, row.shape[1]), 0)
    return jnp.where(ids == row.astype(jnp.int32), 1.0, 0.0).astype(BF16)


def views(pack):
    return pack.at[0:8, :], pack.at[8:40, :], pack.at[40:41, :]


def picked_row(picks, row):
    return picks[0:1, row * 128 : row * 128 + 128]


def listed_block(row, l):
    lane = lax.broadcasted_iota(jnp.int32, row.shape, 1)
    return jnp.sum(jnp.where(lane == l, row, 0.0)).astype(jnp.int32)


def slot_row(slots, first, count):
    return jnp.concatenate([slots[pl.ds(first + i, 1), :] for i in range(count)], axis=1)


def rows(parts, count=8):
    have = sum(p.shape[0] for p in parts)
    return jnp.concatenate(list(parts) + [jnp.zeros((count - have, parts[0].shape[1]), F32)], axis=0)


def rows_kernel(
    pos_far, charge_far, polar_far, table_far, send_far, blocks_far,
    pack, mine, lent_a, lent_b,
    pos, charge, polar, table, send, blocks, done,
):
    pairs = ((pos_far, pos), (charge_far, charge), (polar_far, polar), (table_far, table), (send_far, send))
    wait = fetch(pairs + ((blocks_far, blocks),), done)
    odd = lax.axis_index("sub")
    width = pos.shape[1]
    wait()
    lane = lax.broadcasted_iota(jnp.int32, (1, width), 1)
    listed = jnp.zeros((1, width), jnp.int32)
    for l in range(blocks.shape[0]):
        listed = jnp.where(lane == l, blocks[l], listed)
    listed = listed.astype(F32)
    sites = rows([pos[...], charge[...], polar[...], listed, jnp.ones((1, width), F32)])
    for half in range(2):
        mine[half] = sites[0:4, half * 128 : half * 128 + 128]
    first, second = send[0:1, :], send[1:2, :]
    swap = jnp.full(first.shape, odd, jnp.int32) == 1
    picks = jnp.where(swap, second, first), jnp.where(swap, first, second)
    raw = table[...]
    other = jnp.where((raw >= 256) & (raw < 512), jnp.bitwise_xor(raw, 128), raw)
    keep = jnp.full(raw.shape, odd, jnp.int32) == 1
    pack[0:8, :] = sites
    pack[8:40, :] = jnp.where(keep, raw, other).astype(F32)
    pack[40:48, :] = rows([jnp.concatenate(picks, axis=1).astype(F32)])
    pieces = split3(sites)
    for row, out in zip(picks, (lent_a, lent_b)):
        found = join3(dot(pieces, one_hot(row, width)))
        out[...] = rows([found[0:5], listed[:, 0:128], jnp.ones((1, 128), F32)])


def static_kernel(
    pack, rim_a, rim_b, features_far,
    feat_t, w3, w5, fixed, entry, lent_a, lent_b, features, done,
):
    site, slots, picks = views(pack)
    width = site.shape[1]
    depth = 2 * width
    slot_count = slots.shape[0]

    @pl.when(learned())
    def _():
        fetch(((features_far, features),), done)()
        flipped = flip(features[...]).astype(BF16)
        feat_t[...] = flipped
        lend_channels(flipped, picks, lent_a, lent_b)

    @pl.when(jnp.logical_not(learned()))
    def _():
        table = jnp.concatenate([site[...], rim_a[...], rim_b[...]], axis=1)
        entry[...] = table.T
        tx, ty, tz = site[0:1, :], site[1:2, :], site[2:3, :]

        def some_rows(j, acc):
            start = pl.multiple_of(j * STATIC_CHUNK, STATIC_CHUNK)
            ids = (lax.broadcasted_iota(jnp.int32, (STATIC_CHUNK, width), 0) + start).astype(F32)
            count = jnp.zeros((STATIC_CHUNK, width), F32)
            for k in range(slot_count):
                count = count + jnp.where(ids == slots[k : k + 1, :], 1.0, 0.0)
            cols = entry[pl.ds(start, STATIC_CHUNK), :]
            rx, ry, rz = tx - cols[:, 0:1], ty - cols[:, 1:2], tz - cols[:, 2:3]
            inverse = lax.rsqrt(rx * rx + ry * ry + rz * rz + SMOOTH)
            squared = inverse * inverse
            cube = count * (squared * inverse)
            w3[pl.ds(start, STATIC_CHUNK), :] = cube
            w5[pl.ds(start, STATIC_CHUNK), :] = 3.0 * (cube * squared)
            scale = cols[:, 3:4] * cube
            return acc[0] + rx * scale, acc[1] + ry * scale, acc[2] + rz * scale

        nil = jnp.zeros((STATIC_CHUNK, width), F32)
        sums = lax.fori_loop(0, depth // STATIC_CHUNK, some_rows, (nil, nil, nil))
        total = rows([jnp.sum(s, axis=0, keepdims=True) for s in sums])
        fixed[...] = total
        lend_pieces(total, picks, lent_a, lent_b)


def radial_kernel(
    pack, rim_a, rim_b, w_in_far, w_mid_far,
    third_far, w_in, w_mid, third, done,
):
    site, slots, _ = views(pack)
    width = site.shape[1]
    depth = 2 * width
    slot_count = slots.shape[0]

    @pl.when(learned())
    def _():
        wait = fetch(((w_in_far, w_in), (w_mid_far, w_mid)), done)
        pieces = split3(jnp.concatenate([site[...], rim_a[...], rim_b[...]], axis=1))
        step = RADIAL_SLOTS * width
        here = jnp.concatenate([site[...]] * RADIAL_SLOTS, axis=1)
        centres = lax.broadcasted_iota(jnp.int32, (BASIS, step), 0).astype(F32) * SPACING
        wait()
        first_w = jnp.concatenate([flip(w_in[0]), flip(w_in[1])], axis=0).astype(BF16)
        zero = jnp.zeros((64, 64), F32)

        def both(level):
            top = jnp.concatenate([flip(w_mid[0, level]), zero], axis=1)
            bottom = jnp.concatenate([zero, flip(w_mid[1, level])], axis=1)
            return jnp.concatenate([top, bottom], axis=0).astype(BF16)

        second_w, third_w = both(0), both(1)

        def some_slots(k, carry):
            found = join3(dot(pieces, one_hot(slot_row(slots, k * RADIAL_SLOTS, RADIAL_SLOTS), depth)))
            offset = here - found
            squares = offset * offset
            dist_sq = squares[0:1] + squares[1:2] + squares[2:3] + SMOOTH
            gap = jnp.sqrt(dist_sq) - centres
            basis = jnp.exp(-(gap * gap)).astype(BF16)
            hidden = silu(dot(first_w, basis)).astype(BF16)
            hidden = silu(dot(second_w, hidden)).astype(BF16)
            start = pl.multiple_of(k * step, step)
            third[:, pl.ds(start, step)] = silu(dot(third_w, hidden)).astype(BF16)
            return carry

        lax.fori_loop(0, slot_count // RADIAL_SLOTS, some_slots, 0)
        fetch(((third, third_far),), done, 2)()


def lend_pieces(values, picks, lent_a, lent_b):
    pieces = split3(values)
    for row, out in ((0, lent_a), (1, lent_b)):
        found = dot(pieces, one_hot(picked_row(picks, row), values.shape[1]))
        out[...] = jnp.zeros_like(out)
        out[0:32, :] = rows([found], 32).astype(BF16)


def lend_whole(values, picks, lent_a, lent_b):
    pieces = split3(values)
    for row, out in ((0, lent_a), (1, lent_b)):
        out[...] = join3(dot(pieces, one_hot(picked_row(picks, row), values.shape[1])))


def lend_channels(values, picks, lent_a, lent_b):
    for row, out in ((0, lent_a), (1, lent_b)):
        out[...] = dot(values, one_hot(picked_row(picks, row), values.shape[1])).astype(BF16)


def sweep(site, w3, w5, fixed, dipoles, entry, moment):
    width = site.shape[1]
    moment[...] = dipoles.T
    tx, ty, tz = site[0:1, :], site[1:2, :], site[2:3, :]

    def some_rows(j, acc):
        start = pl.multiple_of(j * SWEEP_CHUNK, SWEEP_CHUNK)
        cols, d = entry[pl.ds(start, SWEEP_CHUNK), :], moment[pl.ds(start, SWEEP_CHUNK), :]
        rx, ry, rz = tx - cols[:, 0:1], ty - cols[:, 1:2], tz - cols[:, 2:3]
        dx, dy, dz = d[:, 0:1], d[:, 1:2], d[:, 2:3]
        cube = w3[pl.ds(start, SWEEP_CHUNK), :]
        scale = (rx * dx + ry * dy + rz * dz) * w5[pl.ds(start, SWEEP_CHUNK), :]
        return (
            acc[0] + (rx * scale - dx * cube),
            acc[1] + (ry * scale - dy * cube),
            acc[2] + (rz * scale - dz * cube),
        )

    nil = jnp.zeros((SWEEP_CHUNK, width), F32)
    sums = lax.fori_loop(0, w3.shape[0] // SWEEP_CHUNK, some_rows, (nil, nil, nil), unroll=SWEEP_UNROLL)
    return site[4:5, :] * (fixed + rows([jnp.sum(s, axis=0, keepdims=True) for s in sums]))


def message(layer, hidden, table, third, out_t, node_t, slots, total):
    slot_count = slots.shape[0]
    width = slots.shape[1]
    step = MESSAGE_SLOTS * width
    total[...] = jnp.zeros_like(total)

    def some_slots(k, carry):
        row = slot_row(slots, k * MESSAGE_SLOTS, MESSAGE_SLOTS)
        picked = dot(table, one_hot(row, table.shape[1]))
        start = pl.multiple_of(k * step, step)
        weight = dot(out_t, third[layer * 64 : layer * 64 + 64, pl.ds(start, step)])
        product = weight * picked
        part = product[:, 0:width]
        for i in range(1, MESSAGE_SLOTS):
            part = part + product[:, i * width : (i + 1) * width]
        total[...] += part
        return carry

    lax.fori_loop(0, slot_count // MESSAGE_SLOTS, some_slots, 0)
    mean = (total[...] * (1.0 / slot_count)).astype(BF16)
    return (hidden.astype(F32) + silu(dot(node_t, mean))).astype(BF16)


def charge_field(target, cols, first, count):
    tx, ty, tz = target[0:1, :], target[1:2, :], target[2:3, :]

    def some_rows(j, acc):
        c = cols[pl.ds(pl.multiple_of(first + j * FIELD_CHUNK, FIELD_CHUNK), FIELD_CHUNK), :]
        rx, ry, rz = tx - c[:, 0:1], ty - c[:, 1:2], tz - c[:, 2:3]
        inverse = lax.rsqrt(rx * rx + ry * ry + rz * rz + SMOOTH)
        scale = c[:, 3:4] * (inverse * inverse * inverse)
        return acc[0] + rx * scale, acc[1] + ry * scale, acc[2] + rz * scale

    nil = jnp.zeros((FIELD_CHUNK, target.shape[1]), F32)
    sums = lax.fori_loop(0, count // FIELD_CHUNK, some_rows, (nil, nil, nil), unroll=FIELD_UNROLL)
    return jnp.concatenate([jnp.sum(s, axis=0, keepdims=True) for s in sums], axis=0)


def first_kernel(
    pack, rim_a, rim_b, feat_t, side_a, side_b, w3, w5, fixed, entry,
    near_far, third_far, node_in_far, node_out_far, w_out_far, gain_far,
    outside_row, near_own, hidden_out, lifted_out, fixed_out, dipole_out, lent_a, lent_b,
    near, cols, third, node_in, node_out, w_out, gain, total, moment, done,
):
    site, slots, picks = views(pack)
    width = site.shape[1]
    listed = near_own.shape[0]
    numbers = [listed_block(row[5:6, 0:128], l) for row in (site, rim_a, rim_b) for l in range(listed)]
    fetch([(near_far.at[b], near.at[i]) for i, b in enumerate(numbers)], done, 5)
    weights = (
        (third_far, third), (node_in_far, node_in), (node_out_far.at[0], node_out),
        (w_out_far.at[0], w_out), (gain_far, gain),
    )

    @pl.when(learned())
    def _():
        fetch(weights, done)

    for i, b in enumerate(numbers):
        pltpu.make_async_copy(near_far.at[b], near.at[i], done.at[5 + i]).wait()
    near_own[...] = near[0:listed]
    for i in range(3 * listed):
        tile = near[i]
        cols[i * 128 : i * 128 + 128, :] = jnp.concatenate([tile, tile], axis=0).T
    reach = listed * 128
    own_field = charge_field(site[...], cols, 0, reach)
    field = jnp.concatenate(
        [own_field, charge_field(rim_a[...], cols, reach, reach), charge_field(rim_b[...], cols, 2 * reach, reach)],
        axis=1,
    )
    strength = jnp.sqrt(1.0 + (field[0:1] * field[0:1] + field[1:2] * field[1:2] + field[2:3] * field[2:3]))
    outside_row[...] = jnp.broadcast_to(strength[:, :width], outside_row.shape)

    @pl.when(learned())
    def _():
        for i, (a, b) in enumerate(weights):
            pltpu.make_async_copy(a, b, done.at[i]).wait()
        gain_col = jnp.broadcast_to(gain[...], (8, width)).T
        features = jnp.concatenate([feat_t[...], side_a[...], side_b[...]], axis=1)
        start = (features.astype(F32) + gain_col[:, 0:1] * strength).astype(BF16)
        present = jnp.concatenate([jnp.ones((1, width), F32), rim_a[6:7, :], rim_b[6:7, :]], axis=1)
        raised = dot(flip(node_in[0]).astype(BF16), start)
        table = jnp.where(present > 0.5, raised, 0.0).astype(BF16)
        out_t, node_t = flip(w_out[...]).astype(BF16), flip(node_out[...]).astype(BF16)
        new = message(0, start[:, :width], table, third, out_t, node_t, slots, total)
        hidden_out[...] = new
        raised = dot(flip(node_in[1]).astype(BF16), new).astype(BF16)
        lifted_out[...] = raised
        lend_channels(raised, picks, lent_a, lent_b)

    @pl.when(jnp.logical_not(learned()))
    def _():
        known = [fixed[...], join3(side_a[0:24, :].astype(F32)), join3(side_b[0:24, :].astype(F32))]
        whole = jnp.concatenate(known, axis=1) + rows([field])
        fixed_out[...] = whole[:, :width]
        polar = jnp.concatenate([site[4:5, :], rim_a[4:5, :], rim_b[4:5, :]], axis=1)
        new = sweep(site, w3, w5, whole[:, :width], polar * whole, entry, moment)
        dipole_out[...] = new
        lend_pieces(new, picks, lent_a, lent_b)


def second_kernel(
    hidden, lifted, side_a, side_b, pack, w3, w5, fixed, dipole, entry,
    third_far, node_out_far, w_out_far, readout_far,
    charge, dipole_out, small_a, small_b,
    third, node_out, w_out, readout, total, moment, done,
):
    site, slots, picks = views(pack)

    @pl.when(learned())
    def _():
        fetch(
            ((third_far, third), (node_out_far.at[1], node_out), (w_out_far.at[1], w_out), (readout_far, readout)), done
        )()
        table = jnp.concatenate([lifted[...], side_a[...], side_b[...]], axis=1)
        out_t, node_t = flip(w_out[...]).astype(BF16), flip(node_out[...]).astype(BF16)
        new = message(1, hidden[...], table, third, out_t, node_t, slots, total)
        charge[...] = dot(rows([readout[...].astype(F32)]).astype(BF16), new)

    @pl.when(jnp.logical_not(learned()))
    def _():
        sides = [join3(side_a[0:24, :].astype(F32)), join3(side_b[0:24, :].astype(F32))]
        table = jnp.concatenate([dipole[...]] + sides, axis=1)
        new = sweep(site, w3, w5, fixed[...], table, entry, moment)
        dipole_out[...] = new
        lend_whole(new, picks, small_a, small_b)


def third_kernel(side_a, side_b, pack, w3, w5, fixed, dipole, entry, dipole_out, small_a, small_b, moment):
    site, _, picks = views(pack)

    @pl.when(jnp.logical_not(learned()))
    def _():
        table = jnp.concatenate([dipole[...], side_a[...], side_b[...]], axis=1)
        new = sweep(site, w3, w5, fixed[...], table, entry, moment)
        dipole_out[...] = new
        lend_whole(new, picks, small_a, small_b)


def response_kernel(
    near, pack, charge, outside_row, side_a, side_b, w3, w5, fixed, dipole, entry,
    result, spread, cols, moment, term,
):
    site = views(pack)[0]
    width = site.shape[1]
    listed = near.shape[0]
    blocks = [listed_block(site[5:6, 0:128], l) for l in range(listed)]
    spread[...] = jnp.zeros_like(spread)
    term[...] = jnp.zeros_like(term)

    def terms(dipoles):
        for l in range(listed):
            tile = near[l]
            tx, ty, tz = tile[0:1, :], tile[1:2, :], tile[2:3, :]

            def some_rows(j, acc):
                start = pl.multiple_of(j * TERM_CHUNK, TERM_CHUNK)
                c = cols[pl.ds(start, TERM_CHUNK), :]
                rx, ry, rz = tx - c[:, 0:1], ty - c[:, 1:2], tz - c[:, 2:3]
                inverse = lax.rsqrt(rx * rx + ry * ry + rz * rz + SMOOTH)
                squared = inverse * inverse
                cube = squared * inverse
                if dipoles:
                    dx, dy, dz = c[:, 4:5], c[:, 5:6], c[:, 6:7]
                    scale = (rx * dx + ry * dy + rz * dz) * (3.0 * (cube * squared))
                    return (
                        acc[0] + (rx * scale - dx * cube),
                        acc[1] + (ry * scale - dy * cube),
                        acc[2] + (rz * scale - dz * cube),
                    )
                scale = c[:, 3:4] * cube
                return acc[0] + rx * scale, acc[1] + ry * scale, acc[2] + rz * scale

            nil = jnp.zeros((TERM_CHUNK, 128), F32)
            sums = lax.fori_loop(0, width // TERM_CHUNK, some_rows, (nil, nil, nil), unroll=TERM_UNROLL)
            for axis in range(3):
                term[l, axis : axis + 1, :] = jnp.sum(sums[axis], axis=0, keepdims=True)

    @pl.when(learned())
    def _():
        q = charge[...]
        result[...] = jnp.concatenate([q[0:2], outside_row[0:1, :]], axis=0)
        cols[...] = rows([site[0:3, :], q[0:1]]).T
        terms(False)

    @pl.when(jnp.logical_not(learned()))
    def _():
        table = jnp.concatenate([dipole[...], side_a[...], side_b[...]], axis=1)
        new = sweep(site, w3, w5, fixed[...], table, entry, moment)
        result[...] = new[0:3]
        cols[...] = rows([site[0:4, :], new[0:3]]).T
        terms(True)

    side = lax.broadcasted_iota(jnp.int32, (2, 128), 0)
    for l in range(listed):
        owner, part = blocks[l] >> 1, blocks[l] & 1
        for axis in range(3):
            spread[3 * owner + axis] += jnp.where(side == part, term[l, axis : axis + 1, :], 0.0)


def gather_kernel(pieces, share):
    total = jnp.sum(pieces[...], axis=0)
    share[...] = jnp.concatenate(
        [jnp.concatenate([total[axis, 0:1], total[axis, 1:2]], axis=1) for axis in range(3)], axis=0
    )


def placed(block):
    y_half, plane, step, side = block // 64, block // 8 % 8, block // 2 % 4, block % 2
    x = 3 - step if plane % 2 else step
    z = (plane - 1) % 8 if y_half else plane
    along = 1 - side if (step + y_half) % 2 == 0 else side
    y = 2 * y_half + along
    return ((y % 2 * 8 + z) * 4 + x) * 2 + y // 2


def local(
    positions, charges, polar, features, neighbours, send_rows, blocks,
    radial_in, radial_mid, radial_out, node_in, node_out, field_gain, readout,
):
    width = positions.shape[1]
    slot_count = neighbours.shape[1]
    depth = 2 * width
    half = send_rows.shape[1]
    channels = features.shape[1]
    listed = blocks.shape[0]
    members = lax.axis_size(DOM)
    near_pairs = [(i, i ^ 1) for i in range(members)]
    far_pairs = [(i, ((i - 1) ^ 1) + 1) for i in range(1, members - 1)]
    same = list(range(members))
    place = [placed(i) for i in range(members)]

    def move(value, pairs, source, target, groups=(0, 1)):
        return lax.ppermute(
            value, EVERY, [(source[a] + g * members, target[b] + g * members) for g in groups for a, b in pairs]
        )

    def trade(a, b, groups=(0, 1), source=place):
        return move(a, near_pairs, source, place, groups), move(b, far_pairs, source, place, groups)

    row8, table8 = ((8, width), F32), ((8, half), F32)
    wide = ((channels, half), BF16)
    by_site = ((channels, width), BF16)
    ints = jnp.int32
    itself = [(i, i) for i in range(members)]
    pack, mine, lent_a, lent_b = call(
        rows_kernel, [((slot_count + 16, width), F32), ((2, 4, half), F32), table8, table8],
        (), (positions, charges[None], polar[None], neighbours.T, send_rows, blocks),
        [pltpu.VMEM((3, width), F32), pltpu.VMEM((1, width), F32), pltpu.VMEM((1, width), F32),
         pltpu.VMEM((slot_count, width), ints), pltpu.VMEM((2, half), ints), pltpu.SMEM((listed,), ints)], 6,
    )
    partner = lax.ppermute(mine, "grp", [(0, 1), (1, 0)])
    copies = jnp.broadcast_to(partner[None], (members,) + partner.shape)
    near = lax.all_to_all(copies, DOM, 0, 0, tiled=True).reshape(2 * members, 4, half)
    pack = move(pack, itself, same, place)
    rim_a, rim_b = trade(lent_a, lent_b, source=same)
    features = move(features, itself, same, place, (0,))
    feat_t, w3, w5, fixed, entry, lent_a, lent_b = call(
        static_kernel, [by_site, ((depth, width), F32), ((depth, width), F32), row8, ((depth, 8), F32), wide, wide],
        (pack, rim_a, rim_b), (features,), [pltpu.VMEM((width, channels), BF16)], 1, loose=1,
    )
    side_a, side_b = trade(lent_a, lent_b)
    third_shape = (LAYERS * radial_in.shape[2], slot_count * width)
    (third,) = call(
        radial_kernel, [(third_shape, BF16)], (pack, rim_a, rim_b), (radial_in, radial_mid),
        [pltpu.VMEM(radial_in.shape, BF16), pltpu.VMEM(radial_mid.shape, BF16), pltpu.VMEM(third_shape, BF16)], 3, 1,
    )
    moment = pltpu.VMEM((depth, 8), F32)
    total = pltpu.VMEM((channels, width), F32)
    square = pltpu.VMEM(node_out.shape[1:], BF16)
    last = pltpu.VMEM(radial_out.shape[1:], BF16)
    outside_row, near_own, hidden, lifted, fixed_all, dipole, lent_a, lent_b = call(
        first_kernel, [row8, ((listed, 4, half), F32), by_site, by_site, row8, row8, wide, wide],
        (pack, rim_a, rim_b, feat_t, side_a, side_b, w3, w5, fixed, entry),
        (near, third, node_in, node_out, radial_out, field_gain[None]),
        [pltpu.VMEM((3 * listed, 4, half), F32), pltpu.VMEM((3 * listed * half, 8), F32),
         pltpu.VMEM(third_shape, BF16), pltpu.VMEM(node_in.shape, BF16), square, last,
         pltpu.VMEM((1, channels), F32), total, moment], 5 + 3 * listed, loose=1,
    )
    side_a, side_b = trade(lent_a, lent_b)
    charge, dipole, small_a, small_b = call(
        second_kernel, [row8, row8, table8, table8],
        (hidden, lifted, side_a, side_b, pack, w3, w5, fixed_all, dipole, entry),
        (third, node_out, radial_out, readout.T),
        [pltpu.VMEM(third_shape, BF16), square, last, pltpu.VMEM((2, channels), BF16), total, moment], 4,
    )
    side_a, side_b = trade(small_a, small_b, (1,))
    dipole, small_a, small_b = call(
        third_kernel, [row8, table8, table8], (side_a, side_b, pack, w3, w5, fixed_all, dipole, entry),
        (), [moment],
    )
    side_a, side_b = trade(small_a, small_b, (1,))
    result, spread = call(
        response_kernel, [((3, width), F32), ((3 * members, 2, half), F32)],
        (near_own, pack, charge, outside_row, side_a, side_b, w3, w5, fixed_all, dipole, entry), (),
        [pltpu.VMEM((width, 8), F32), moment, pltpu.VMEM((listed, 4, half), F32)],
    )
    pieces = lax.all_to_all(spread, DOM, 0, 0, tiled=True).reshape(members, 3, 2, half)
    (share,) = call(gather_kernel, [((3, width), F32)], (pieces,))
    result = move(result, itself, place, same)
    return result, lax.ppermute(share, "grp", [(0, 1), (1, 0)])


def solution(mesh):
    sites = P(None, EVERY)
    in_specs = (sites, P(EVERY), P(EVERY), P(EVERY, None), P(EVERY, None), sites, P(EVERY)) + (P(),) * 7
    return jax.shard_map(local, mesh=mesh, in_specs=in_specs, out_specs=(sites, sites), check_vma=False)
```

```python
import jax
import jax.numpy as jnp
from jax import lax
from jax.experimental import pallas as pl
from jax.experimental.pallas import tpu as pltpu
from jax.sharding import PartitionSpec as P

BASIS = 8
LAYERS = 2
SMOOTH = 1.0
SPACING = 0.75
DOM = ("dom", "sub")
EVERY = ("grp", "dom", "sub")
F32 = jnp.float32
BF16 = jnp.bfloat16
VMEM = pl.BlockSpec(memory_space=pltpu.VMEM)
ANY = pl.BlockSpec(memory_space=pl.ANY)
SWEEP_CHUNK, SWEEP_UNROLL = 32, 4
FIELD_CHUNK, FIELD_UNROLL = 32, 4
TERM_CHUNK, TERM_UNROLL = 64, 4
STATIC_CHUNK = 32
RADIAL_SLOTS = 8
MESSAGE_SLOTS = 8


def call(body, outs, held, far=(), scratch=(), copies=0, far_outs=0, loose=0):
    return pl.pallas_call(
        body,
        out_shape=[jax.ShapeDtypeStruct(s, d) for s, d in outs[: len(outs) - far_outs]]
        + [pltpu.HBM(s, d) for s, d in outs[len(outs) - far_outs :]],
        in_specs=[VMEM] * len(held) + [ANY] * len(far),
        out_specs=[VMEM] * (len(outs) - far_outs) + [ANY] * far_outs,
        scratch_shapes=list(scratch) + ([pltpu.SemaphoreType.DMA((copies,))] if copies else []),
        compiler_params=pltpu.CompilerParams(vmem_limit_bytes=24 * 2**20),
    )(*held, *far[:loose], *[pltpu.with_memory_space_constraint(a, pltpu.HBM) for a in far[loose:]])


def fetch(pairs, done, first=0):
    copies = [pltpu.make_async_copy(a, b, done.at[first + i]) for i, (a, b) in enumerate(pairs)]
    for c in copies:
        c.start()

    def wait():
        for c in copies:
            c.wait()

    return wait


def learned():
    return lax.axis_index("grp") == 0


def dot(a, b):
    return jnp.dot(a, b, preferred_element_type=F32)


def silu(x):
    half = 0.5 * x
    return half + half * jnp.tanh(half)


def flip(x):
    return x.astype(F32).T


def split3(x):
    high = x.astype(BF16)
    rest = x - high.astype(F32)
    mid = rest.astype(BF16)
    low = (rest - mid.astype(F32)).astype(BF16)
    return jnp.concatenate([high, mid, low], axis=0)


def join3(x):
    return x[0:8] + x[8:16] + x[16:24]


def one_hot(row, depth):
    ids = lax.broadcasted_iota(jnp.int32, (depth, row.shape[1]), 0)
    return jnp.where(ids == row.astype(jnp.int32), 1.0, 0.0).astype(BF16)


def views(pack):
    return pack.at[0:8, :], pack.at[8:40, :], pack.at[40:41, :]


def picked_row(picks, row):
    return picks[0:1, row * 128 : row * 128 + 128]


def listed_block(row, l):
    lane = lax.broadcasted_iota(jnp.int32, row.shape, 1)
    return jnp.sum(jnp.where(lane == l, row, 0.0)).astype(jnp.int32)


def slot_row(slots, first, count):
    return jnp.concatenate([slots[pl.ds(first + i, 1), :] for i in range(count)], axis=1)


def rows(parts, count=8):
    have = sum(p.shape[0] for p in parts)
    return jnp.concatenate(list(parts) + [jnp.zeros((count - have, parts[0].shape[1]), F32)], axis=0)


def rows_kernel(
    pos_far, charge_far, polar_far, table_far, send_far, blocks_far, features_far,
    pack, mine, lent_a, lent_b, feat_t,
    pos, charge, polar, table, send, blocks, features, done,
):
    @pl.when(learned())
    def _():
        fetch(((features_far, features),), done, 6)

    pairs = ((pos_far, pos), (charge_far, charge), (polar_far, polar), (table_far, table), (send_far, send))
    wait = fetch(pairs + ((blocks_far, blocks),), done)
    odd = lax.axis_index("sub")
    width = pos.shape[1]
    wait()
    lane = lax.broadcasted_iota(jnp.int32, (1, width), 1)
    listed = jnp.zeros((1, width), jnp.int32)
    for l in range(blocks.shape[0]):
        listed = jnp.where(lane == l, blocks[l], listed)
    listed = listed.astype(F32)
    sites = rows([pos[...], charge[...], polar[...], listed, jnp.ones((1, width), F32)])
    for half in range(2):
        mine[half] = sites[0:4, half * 128 : half * 128 + 128]
    first, second = send[0:1, :], send[1:2, :]
    swap = jnp.full(first.shape, odd, jnp.int32) == 1
    picks = jnp.where(swap, second, first), jnp.where(swap, first, second)
    raw = table[...]
    other = jnp.where((raw >= 256) & (raw < 512), jnp.bitwise_xor(raw, 128), raw)
    keep = jnp.full(raw.shape, odd, jnp.int32) == 1
    pack[0:8, :] = sites
    pack[8:40, :] = jnp.where(keep, raw, other).astype(F32)
    pack[40:48, :] = rows([jnp.concatenate(picks, axis=1).astype(F32)])
    pieces = split3(sites)
    chosen = [one_hot(row, width) for row in picks]
    for pick, out in zip(chosen, (lent_a, lent_b)):
        found = join3(dot(pieces, pick))
        lent = rows([found[0:5], listed[:, 0:128], jnp.ones((1, 128), F32)])
        out[0:32, :] = jnp.concatenate([split3(lent), jnp.zeros((8, 128), BF16)], axis=0)

    @pl.when(learned())
    def _():
        pltpu.make_async_copy(features_far, features, done.at[6]).wait()
        flipped = flip(features[...]).astype(BF16)
        feat_t[...] = flipped
        for pick, out in zip(chosen, (lent_a, lent_b)):
            out[32:, :] = dot(flipped, pick).astype(BF16)

    @pl.when(jnp.logical_not(learned()))
    def _():
        for out in (lent_a, lent_b):
            out[32:, :] = jnp.zeros((feat_t.shape[0], 128), BF16)


def rim(lent):
    return join3(lent[0:24, :].astype(F32))


def static_kernel(pack, from_a, from_b, w3, w5, fixed, entry, lent_a, lent_b):
    site, slots, picks = views(pack)
    width = site.shape[1]
    depth = 2 * width
    slot_count = slots.shape[0]

    @pl.when(jnp.logical_not(learned()))
    def _():
        table = jnp.concatenate([site[...], rim(from_a), rim(from_b)], axis=1)
        entry[...] = table.T
        tx, ty, tz = site[0:1, :], site[1:2, :], site[2:3, :]

        def some_rows(j, acc):
            start = pl.multiple_of(j * STATIC_CHUNK, STATIC_CHUNK)
            ids = (lax.broadcasted_iota(jnp.int32, (STATIC_CHUNK, width), 0) + start).astype(F32)
            count = jnp.zeros((STATIC_CHUNK, width), F32)
            for k in range(slot_count):
                count = count + jnp.where(ids == slots[k : k + 1, :], 1.0, 0.0)
            cols = entry[pl.ds(start, STATIC_CHUNK), :]
            rx, ry, rz = tx - cols[:, 0:1], ty - cols[:, 1:2], tz - cols[:, 2:3]
            inverse = lax.rsqrt(rx * rx + ry * ry + rz * rz + SMOOTH)
            squared = inverse * inverse
            cube = count * (squared * inverse)
            w3[pl.ds(start, STATIC_CHUNK), :] = cube
            w5[pl.ds(start, STATIC_CHUNK), :] = 3.0 * (cube * squared)
            scale = cols[:, 3:4] * cube
            return acc[0] + rx * scale, acc[1] + ry * scale, acc[2] + rz * scale

        nil = jnp.zeros((STATIC_CHUNK, width), F32)
        sums = lax.fori_loop(0, depth // STATIC_CHUNK, some_rows, (nil, nil, nil))
        total = rows([jnp.sum(s, axis=0, keepdims=True) for s in sums])
        fixed[...] = total
        lend_whole(total, picks, lent_a, lent_b)


def radial_kernel(
    pack, from_a, from_b, w_in_far, w_mid_far,
    third_far, w_in, w_mid, third, entry, square, done,
):
    site, slots, _ = views(pack)
    width = site.shape[1]
    depth = 2 * width
    slot_count = slots.shape[0]

    @pl.when(learned())
    def _():
        wait = fetch(((w_in_far, w_in), (w_mid_far, w_mid)), done)
        entry[...] = jnp.concatenate([site[...], rim(from_a), rim(from_b)], axis=1).T
        tx, ty, tz = site[0:1, :], site[1:2, :], site[2:3, :]

        def some_rows(j, carry):
            start = pl.multiple_of(j * STATIC_CHUNK, STATIC_CHUNK)
            cols = entry[pl.ds(start, STATIC_CHUNK), :]
            rx, ry, rz = tx - cols[:, 0:1], ty - cols[:, 1:2], tz - cols[:, 2:3]
            square[pl.ds(start, STATIC_CHUNK), :] = rx * rx + ry * ry + rz * rz
            return carry

        lax.fori_loop(0, depth // STATIC_CHUNK, some_rows, 0, unroll=4)
        empty = tx * tx + ty * ty + tz * tz
        step = RADIAL_SLOTS * width
        centres = lax.broadcasted_iota(jnp.int32, (BASIS, step), 0).astype(F32) * SPACING
        ids = lax.broadcasted_iota(jnp.int32, (8, width), 0).astype(F32)
        wait()
        first_w = jnp.concatenate([flip(w_in[0]), flip(w_in[1])], axis=0).astype(BF16)
        zero = jnp.zeros((64, 64), F32)

        def both(level):
            top = jnp.concatenate([flip(w_mid[0, level]), zero], axis=1)
            bottom = jnp.concatenate([zero, flip(w_mid[1, level])], axis=1)
            return jnp.concatenate([top, bottom], axis=0).astype(BF16)

        second_w, third_w = both(0), both(1)

        def some_slots(k, carry):
            named = [slots[pl.ds(k * RADIAL_SLOTS + i, 1), :] for i in range(RADIAL_SLOTS)]

            def pick(j, acc):
                start = pl.multiple_of(j * 8, 8)
                here = square[pl.ds(start, 8), :]
                mine = ids + start.astype(F32)
                return tuple(a + jnp.where(mine == n, here, 0.0) for a, n in zip(acc, named))

            nil = jnp.zeros((8, width), F32)
            found = lax.fori_loop(0, depth // 8, pick, (nil,) * RADIAL_SLOTS, unroll=8)
            far = [
                jnp.sum(f, axis=0, keepdims=True) + jnp.where(n == float(depth), empty, 0.0)
                for f, n in zip(found, named)
            ]
            gap = jnp.sqrt(jnp.concatenate(far, axis=1) + SMOOTH) - centres
            basis = jnp.exp(-(gap * gap)).astype(BF16)
            hidden = silu(dot(first_w, basis)).astype(BF16)
            hidden = silu(dot(second_w, hidden)).astype(BF16)
            start = pl.multiple_of(k * step, step)
            third[:, pl.ds(start, step)] = silu(dot(third_w, hidden)).astype(BF16)
            return carry

        lax.fori_loop(0, slot_count // RADIAL_SLOTS, some_slots, 0)
        fetch(((third, third_far),), done, 2)()


def lend_pieces(values, picks, lent_a, lent_b):
    pieces = split3(values)
    for row, out in ((0, lent_a), (1, lent_b)):
        found = dot(pieces, one_hot(picked_row(picks, row), values.shape[1]))
        out[...] = jnp.zeros_like(out)
        out[0:32, :] = rows([found], 32).astype(BF16)


def lend_whole(values, picks, lent_a, lent_b):
    pieces = split3(values)
    for row, out in ((0, lent_a), (1, lent_b)):
        out[...] = join3(dot(pieces, one_hot(picked_row(picks, row), values.shape[1])))


def lend_channels(values, picks, lent_a, lent_b):
    for row, out in ((0, lent_a), (1, lent_b)):
        out[...] = dot(values, one_hot(picked_row(picks, row), values.shape[1])).astype(BF16)


def sweep(site, w3, w5, fixed, dipoles, entry, moment):
    width = site.shape[1]
    moment[...] = dipoles.T
    tx, ty, tz = site[0:1, :], site[1:2, :], site[2:3, :]

    def some_rows(j, acc):
        start = pl.multiple_of(j * SWEEP_CHUNK, SWEEP_CHUNK)
        cols, d = entry[pl.ds(start, SWEEP_CHUNK), :], moment[pl.ds(start, SWEEP_CHUNK), :]
        rx, ry, rz = tx - cols[:, 0:1], ty - cols[:, 1:2], tz - cols[:, 2:3]
        dx, dy, dz = d[:, 0:1], d[:, 1:2], d[:, 2:3]
        cube = w3[pl.ds(start, SWEEP_CHUNK), :]
        scale = (rx * dx + ry * dy + rz * dz) * w5[pl.ds(start, SWEEP_CHUNK), :]
        return (
            acc[0] + (rx * scale - dx * cube),
            acc[1] + (ry * scale - dy * cube),
            acc[2] + (rz * scale - dz * cube),
        )

    nil = jnp.zeros((SWEEP_CHUNK, width), F32)
    sums = lax.fori_loop(0, w3.shape[0] // SWEEP_CHUNK, some_rows, (nil, nil, nil), unroll=SWEEP_UNROLL)
    return site[4:5, :] * (fixed + rows([jnp.sum(s, axis=0, keepdims=True) for s in sums]))


def message(layer, hidden, table, third, out_t, node_t, slots, total):
    slot_count = slots.shape[0]
    width = slots.shape[1]
    step = MESSAGE_SLOTS * width
    total[...] = jnp.zeros_like(total)

    def some_slots(k, carry):
        row = slot_row(slots, k * MESSAGE_SLOTS, MESSAGE_SLOTS)
        picked = dot(table, one_hot(row, table.shape[1]))
        start = pl.multiple_of(k * step, step)
        weight = dot(out_t, third[layer * 64 : layer * 64 + 64, pl.ds(start, step)])
        product = weight * picked
        part = product[:, 0:width]
        for i in range(1, MESSAGE_SLOTS):
            part = part + product[:, i * width : (i + 1) * width]
        total[...] += part
        return carry

    lax.fori_loop(0, slot_count // MESSAGE_SLOTS, some_slots, 0)
    mean = (total[...] * (1.0 / slot_count)).astype(BF16)
    return (hidden.astype(F32) + silu(dot(node_t, mean))).astype(BF16)


def charge_field(target, cols, first, count):
    tx, ty, tz = target[0:1, :], target[1:2, :], target[2:3, :]

    def some_rows(j, acc):
        c = cols[pl.ds(pl.multiple_of(first + j * FIELD_CHUNK, FIELD_CHUNK), FIELD_CHUNK), :]
        rx, ry, rz = tx - c[:, 0:1], ty - c[:, 1:2], tz - c[:, 2:3]
        inverse = lax.rsqrt(rx * rx + ry * ry + rz * rz + SMOOTH)
        scale = c[:, 3:4] * (inverse * inverse * inverse)
        return acc[0] + rx * scale, acc[1] + ry * scale, acc[2] + rz * scale

    nil = jnp.zeros((FIELD_CHUNK, target.shape[1]), F32)
    sums = lax.fori_loop(0, count // FIELD_CHUNK, some_rows, (nil, nil, nil), unroll=FIELD_UNROLL)
    return jnp.concatenate([jnp.sum(s, axis=0, keepdims=True) for s in sums], axis=0)


def first_kernel(
    pack, from_a, from_b, feat_t, side_a, side_b, w3, w5, fixed, entry,
    near_far, third_far, node_in_far, node_out_far, w_out_far, gain_far,
    outside_row, near_own, hidden_out, lifted_out, fixed_out, dipole_out, lent_a, lent_b,
    near, cols, third, node_in, node_out, w_out, gain, total, moment, done,
):
    site, slots, picks = views(pack)
    width = site.shape[1]
    listed = near_own.shape[0]
    rim_a, rim_b = rim(from_a), rim(from_b)
    numbers = [listed_block(row[5:6, 0:128], l) for row in (site, rim_a, rim_b) for l in range(listed)]
    fetch([(near_far.at[b], near.at[i]) for i, b in enumerate(numbers)], done, 5)
    weights = (
        (third_far, third), (node_in_far, node_in), (node_out_far.at[0], node_out),
        (w_out_far.at[0], w_out), (gain_far, gain),
    )

    @pl.when(learned())
    def _():
        fetch(weights, done)

    for i, b in enumerate(numbers):
        pltpu.make_async_copy(near_far.at[b], near.at[i], done.at[5 + i]).wait()
    near_own[...] = near[0:listed]
    for i in range(3 * listed):
        tile = near[i]
        cols[i * 128 : i * 128 + 128, :] = jnp.concatenate([tile, tile], axis=0).T
    reach = listed * 128
    own_field = charge_field(site[...], cols, 0, reach)
    field = jnp.concatenate(
        [own_field, charge_field(rim_a, cols, reach, reach), charge_field(rim_b, cols, 2 * reach, reach)],
        axis=1,
    )
    strength = jnp.sqrt(1.0 + (field[0:1] * field[0:1] + field[1:2] * field[1:2] + field[2:3] * field[2:3]))
    outside_row[...] = jnp.broadcast_to(strength[:, :width], outside_row.shape)

    @pl.when(learned())
    def _():
        for i, (a, b) in enumerate(weights):
            pltpu.make_async_copy(a, b, done.at[i]).wait()
        gain_col = jnp.broadcast_to(gain[...], (8, width)).T
        features = jnp.concatenate([feat_t[...], from_a[32:, :], from_b[32:, :]], axis=1)
        start = (features.astype(F32) + gain_col[:, 0:1] * strength).astype(BF16)
        present = jnp.concatenate([jnp.ones((1, width), F32), rim_a[6:7, :], rim_b[6:7, :]], axis=1)
        raised = dot(flip(node_in[0]).astype(BF16), start)
        table = jnp.where(present > 0.5, raised, 0.0).astype(BF16)
        out_t, node_t = flip(w_out[...]).astype(BF16), flip(node_out[...]).astype(BF16)
        new = message(0, start[:, :width], table, third, out_t, node_t, slots, total)
        hidden_out[...] = new
        raised = dot(flip(node_in[1]).astype(BF16), new).astype(BF16)
        lifted_out[...] = raised
        lend_channels(raised, picks, lent_a, lent_b)

    @pl.when(jnp.logical_not(learned()))
    def _():
        whole = jnp.concatenate([fixed[...], side_a[...], side_b[...]], axis=1) + rows([field])
        fixed_out[...] = whole[:, :width]
        polar = jnp.concatenate([site[4:5, :], rim_a[4:5, :], rim_b[4:5, :]], axis=1)
        new = sweep(site, w3, w5, whole[:, :width], polar * whole, entry, moment)
        dipole_out[...] = new
        lend_pieces(new, picks, lent_a, lent_b)


def second_kernel(
    hidden, lifted, side_a, side_b, pack, w3, w5, fixed, dipole, entry,
    third_far, node_out_far, w_out_far, readout_far,
    charge, dipole_out, small_a, small_b,
    third, node_out, w_out, readout, total, moment, done,
):
    site, slots, picks = views(pack)

    @pl.when(learned())
    def _():
        fetch(
            ((third_far, third), (node_out_far.at[1], node_out), (w_out_far.at[1], w_out), (readout_far, readout)), done
        )()
        table = jnp.concatenate([lifted[...], side_a[...], side_b[...]], axis=1)
        out_t, node_t = flip(w_out[...]).astype(BF16), flip(node_out[...]).astype(BF16)
        new = message(1, hidden[...], table, third, out_t, node_t, slots, total)
        charge[...] = dot(rows([readout[...].astype(F32)]).astype(BF16), new)

    @pl.when(jnp.logical_not(learned()))
    def _():
        sides = [join3(side_a[0:24, :].astype(F32)), join3(side_b[0:24, :].astype(F32))]
        table = jnp.concatenate([dipole[...]] + sides, axis=1)
        new = sweep(site, w3, w5, fixed[...], table, entry, moment)
        dipole_out[...] = new
        lend_whole(new, picks, small_a, small_b)


def third_kernel(side_a, side_b, pack, w3, w5, fixed, dipole, entry, dipole_out, small_a, small_b, moment):
    site, _, picks = views(pack)

    @pl.when(jnp.logical_not(learned()))
    def _():
        table = jnp.concatenate([dipole[...], side_a[...], side_b[...]], axis=1)
        new = sweep(site, w3, w5, fixed[...], table, entry, moment)
        dipole_out[...] = new
        lend_whole(new, picks, small_a, small_b)


def response_kernel(
    near, pack, charge, outside_row, side_a, side_b, w3, w5, fixed, dipole, entry,
    result, spread, cols, moment, term,
):
    site = views(pack)[0]
    width = site.shape[1]
    listed = near.shape[0]
    blocks = [listed_block(site[5:6, 0:128], l) for l in range(listed)]
    spread[...] = jnp.zeros_like(spread)
    term[...] = jnp.zeros_like(term)

    def terms(dipoles):
        for l in range(listed):
            tile = near[l]
            tx, ty, tz = tile[0:1, :], tile[1:2, :], tile[2:3, :]

            def some_rows(j, acc):
                start = pl.multiple_of(j * TERM_CHUNK, TERM_CHUNK)
                c = cols[pl.ds(start, TERM_CHUNK), :]
                rx, ry, rz = tx - c[:, 0:1], ty - c[:, 1:2], tz - c[:, 2:3]
                inverse = lax.rsqrt(rx * rx + ry * ry + rz * rz + SMOOTH)
                squared = inverse * inverse
                cube = squared * inverse
                if dipoles:
                    dx, dy, dz = c[:, 4:5], c[:, 5:6], c[:, 6:7]
                    scale = (rx * dx + ry * dy + rz * dz) * (3.0 * (cube * squared))
                    return (
                        acc[0] + (rx * scale - dx * cube),
                        acc[1] + (ry * scale - dy * cube),
                        acc[2] + (rz * scale - dz * cube),
                    )
                scale = c[:, 3:4] * cube
                return acc[0] + rx * scale, acc[1] + ry * scale, acc[2] + rz * scale

            nil = jnp.zeros((TERM_CHUNK, 128), F32)
            sums = lax.fori_loop(0, width // TERM_CHUNK, some_rows, (nil, nil, nil), unroll=TERM_UNROLL)
            for axis in range(3):
                term[l, axis : axis + 1, :] = jnp.sum(sums[axis], axis=0, keepdims=True)

    @pl.when(learned())
    def _():
        q = charge[...]
        result[...] = jnp.concatenate([q[0:2], outside_row[0:1, :]], axis=0)
        cols[...] = rows([site[0:3, :], q[0:1]]).T
        terms(False)

    @pl.when(jnp.logical_not(learned()))
    def _():
        table = jnp.concatenate([dipole[...], side_a[...], side_b[...]], axis=1)
        new = sweep(site, w3, w5, fixed[...], table, entry, moment)
        result[...] = new[0:3]
        cols[...] = rows([site[0:4, :], new[0:3]]).T
        terms(True)

    side = lax.broadcasted_iota(jnp.int32, (2, 128), 0)
    for l in range(listed):
        owner, part = blocks[l] >> 1, blocks[l] & 1
        for axis in range(3):
            spread[3 * owner + axis] += jnp.where(side == part, term[l, axis : axis + 1, :], 0.0)


def gather_kernel(pieces, share):
    total = jnp.sum(pieces[...], axis=0)
    share[...] = jnp.concatenate(
        [jnp.concatenate([total[axis, 0:1], total[axis, 1:2]], axis=1) for axis in range(3)], axis=0
    )


def placed(block):
    y_half, plane, step, side = block // 64, block // 8 % 8, block // 2 % 4, block % 2
    x = 3 - step if plane % 2 else step
    z = (plane - 1) % 8 if y_half else plane
    along = 1 - side if (step + y_half) % 2 == 0 else side
    y = 2 * y_half + along
    return ((y % 2 * 8 + z) * 4 + x) * 2 + y // 2


def local(
    positions, charges, polar, features, neighbours, send_rows, blocks,
    radial_in, radial_mid, radial_out, node_in, node_out, field_gain, readout,
):
    width = positions.shape[1]
    slot_count = neighbours.shape[1]
    depth = 2 * width
    half = send_rows.shape[1]
    channels = features.shape[1]
    listed = blocks.shape[0]
    members = lax.axis_size(DOM)
    near_pairs = [(i, i ^ 1) for i in range(members)]
    far_pairs = [(i, ((i - 1) ^ 1) + 1) for i in range(1, members - 1)]
    same = list(range(members))
    place = [placed(i) for i in range(members)]

    def move(value, pairs, source, target, groups=(0, 1)):
        return lax.ppermute(
            value, EVERY, [(source[a] + g * members, target[b] + g * members) for g in groups for a, b in pairs]
        )

    def trade(a, b, groups=(0, 1), source=place):
        return move(a, near_pairs, source, place, groups), move(b, far_pairs, source, place, groups)

    row8, table8 = ((8, width), F32), ((8, half), F32)
    wide = ((channels, half), BF16)
    by_site = ((channels, width), BF16)
    ints = jnp.int32
    first_lent = ((32 + channels, half), BF16)
    itself = [(i, i) for i in range(members)]
    pack, mine, lent_a, lent_b, feat_t = call(
        rows_kernel, [((slot_count + 16, width), F32), ((2, 4, half), F32), first_lent, first_lent, by_site],
        (), (positions, charges[None], polar[None], neighbours.T, send_rows, blocks, features),
        [pltpu.VMEM((3, width), F32), pltpu.VMEM((1, width), F32), pltpu.VMEM((1, width), F32),
         pltpu.VMEM((slot_count, width), ints), pltpu.VMEM((2, half), ints), pltpu.SMEM((listed,), ints),
         pltpu.VMEM((width, channels), BF16)], 7,
    )
    partner = lax.ppermute(mine, "grp", [(0, 1), (1, 0)])
    copies = jnp.broadcast_to(partner[None], (members,) + partner.shape)
    near = lax.all_to_all(copies, DOM, 0, 0, tiled=True).reshape(2 * members, 4, half)
    pack = move(pack, itself, same, place)
    rim_a, rim_b = trade(lent_a, lent_b, source=same)
    feat_t, rim_a, rim_b = lax.optimization_barrier((feat_t, rim_a, rim_b))
    feat_t = move(feat_t, itself, same, place, (0,))
    w3, w5, fixed, entry, lent_a, lent_b = call(
        static_kernel, [((depth, width), F32), ((depth, width), F32), row8, ((depth, 8), F32), table8, table8],
        (pack, rim_a, rim_b),
    )
    side_a, side_b = trade(lent_a, lent_b, (1,))
    third_shape = (LAYERS * radial_in.shape[2], slot_count * width)
    (third,) = call(
        radial_kernel, [(third_shape, BF16)], (pack, rim_a, rim_b), (radial_in, radial_mid),
        [pltpu.VMEM(radial_in.shape, BF16), pltpu.VMEM(radial_mid.shape, BF16), pltpu.VMEM(third_shape, BF16),
         pltpu.VMEM((depth, 8), F32), pltpu.VMEM((depth, width), F32)], 3, 1,
    )
    moment = pltpu.VMEM((depth, 8), F32)
    total = pltpu.VMEM((channels, width), F32)
    square = pltpu.VMEM(node_out.shape[1:], BF16)
    last = pltpu.VMEM(radial_out.shape[1:], BF16)
    outside_row, near_own, hidden, lifted, fixed_all, dipole, lent_a, lent_b = call(
        first_kernel, [row8, ((listed, 4, half), F32), by_site, by_site, row8, row8, wide, wide],
        (pack, rim_a, rim_b, feat_t, side_a, side_b, w3, w5, fixed, entry),
        (near, third, node_in, node_out, radial_out, field_gain[None]),
        [pltpu.VMEM((3 * listed, 4, half), F32), pltpu.VMEM((3 * listed * half, 8), F32),
         pltpu.VMEM(third_shape, BF16), pltpu.VMEM(node_in.shape, BF16), square, last,
         pltpu.VMEM((1, channels), F32), total, moment], 5 + 3 * listed, loose=1,
    )
    side_a, side_b = trade(lent_a, lent_b)
    charge, dipole, small_a, small_b = call(
        second_kernel, [row8, row8, table8, table8],
        (hidden, lifted, side_a, side_b, pack, w3, w5, fixed_all, dipole, entry),
        (third, node_out, radial_out, readout.T),
        [pltpu.VMEM(third_shape, BF16), square, last, pltpu.VMEM((2, channels), BF16), total, moment], 4,
    )
    side_a, side_b = trade(small_a, small_b, (1,))
    dipole, small_a, small_b = call(
        third_kernel, [row8, table8, table8], (side_a, side_b, pack, w3, w5, fixed_all, dipole, entry),
        (), [moment],
    )
    side_a, side_b = trade(small_a, small_b, (1,))
    result, spread = call(
        response_kernel, [((3, width), F32), ((3 * members, 2, half), F32)],
        (near_own, pack, charge, outside_row, side_a, side_b, w3, w5, fixed_all, dipole, entry), (),
        [pltpu.VMEM((width, 8), F32), moment, pltpu.VMEM((listed, 4, half), F32)],
    )
    pieces = lax.all_to_all(spread, DOM, 0, 0, tiled=True).reshape(members, 3, 2, half)
    (share,) = call(gather_kernel, [((3, width), F32)], (pieces,))
    result = move(result, itself, place, same)
    return result, lax.ppermute(share, "grp", [(0, 1), (1, 0)])


def solution(mesh):
    sites = P(None, EVERY)
    in_specs = (sites, P(EVERY), P(EVERY), P(EVERY, None), P(EVERY, None), sites, P(EVERY)) + (P(),) * 7
    return jax.shard_map(local, mesh=mesh, in_specs=in_specs, out_specs=(sites, sites), check_vma=False)
```

```python
import jax
import jax.numpy as jnp
from jax import lax
from jax.experimental import pallas as pl
from jax.experimental.pallas import tpu as pltpu
from jax.sharding import PartitionSpec as P

BASIS = 8
LAYERS = 2
SMOOTH = 1.0
SPACING = 0.75
DOM = ("dom", "sub")
EVERY = ("grp", "dom", "sub")
F32 = jnp.float32
BF16 = jnp.bfloat16
VMEM = pl.BlockSpec(memory_space=pltpu.VMEM)
ANY = pl.BlockSpec(memory_space=pl.ANY)
SWEEP_CHUNK, SWEEP_UNROLL = 32, 4
FIELD_CHUNK, FIELD_UNROLL = 32, 4
TERM_CHUNK, TERM_UNROLL = 64, 4
STATIC_CHUNK = 32
RADIAL_SLOTS = 8
MESSAGE_SLOTS = 8


def call(body, outs, held, far=(), scratch=(), copies=0, far_outs=0, loose=0):
    return pl.pallas_call(
        body,
        out_shape=[jax.ShapeDtypeStruct(s, d) for s, d in outs[: len(outs) - far_outs]]
        + [pltpu.HBM(s, d) for s, d in outs[len(outs) - far_outs :]],
        in_specs=[VMEM] * len(held) + [ANY] * len(far),
        out_specs=[VMEM] * (len(outs) - far_outs) + [ANY] * far_outs,
        scratch_shapes=list(scratch) + ([pltpu.SemaphoreType.DMA((copies,))] if copies else []),
        compiler_params=pltpu.CompilerParams(vmem_limit_bytes=24 * 2**20),
    )(*held, *far[:loose], *[pltpu.with_memory_space_constraint(a, pltpu.HBM) for a in far[loose:]])


def fetch(pairs, done, first=0):
    copies = [pltpu.make_async_copy(a, b, done.at[first + i]) for i, (a, b) in enumerate(pairs)]
    for c in copies:
        c.start()

    def wait():
        for c in copies:
            c.wait()

    return wait


def learned():
    return lax.axis_index("grp") == 0


def dot(a, b):
    return jnp.dot(a, b, preferred_element_type=F32)


def silu(x):
    half = 0.5 * x
    return half + half * jnp.tanh(half)


def flip(x):
    return x.astype(F32).T


def split3(x):
    high = x.astype(BF16)
    rest = x - high.astype(F32)
    mid = rest.astype(BF16)
    low = (rest - mid.astype(F32)).astype(BF16)
    return jnp.concatenate([high, mid, low], axis=0)


def join3(x):
    return x[0:8] + x[8:16] + x[16:24]


def one_hot(row, depth):
    ids = lax.broadcasted_iota(jnp.int32, (depth, row.shape[1]), 0)
    return jnp.where(ids == row.astype(jnp.int32), 1.0, 0.0).astype(BF16)


def views(pack):
    return pack.at[0:8, :], pack.at[8:40, :], pack.at[40:41, :]


def picked_row(picks, row):
    return picks[0:1, row * 128 : row * 128 + 128]


def listed_block(row, l):
    lane = lax.broadcasted_iota(jnp.int32, row.shape, 1)
    return jnp.sum(jnp.where(lane == l, row, 0.0)).astype(jnp.int32)


def slot_row(slots, first, count):
    return jnp.concatenate([slots[pl.ds(first + i, 1), :] for i in range(count)], axis=1)


def rows(parts, count=8):
    have = sum(p.shape[0] for p in parts)
    return jnp.concatenate(list(parts) + [jnp.zeros((count - have, parts[0].shape[1]), F32)], axis=0)


def rows_kernel(
    pos_far, charge_far, polar_far, table_far, send_far, blocks_far, features_far,
    pack, mine, lent_a, lent_b, feat_t,
    pos, charge, polar, table, send, blocks, features, done,
):
    @pl.when(learned())
    def _():
        fetch(((features_far, features),), done, 6)

    pairs = ((pos_far, pos), (charge_far, charge), (polar_far, polar), (table_far, table), (send_far, send))
    wait = fetch(pairs + ((blocks_far, blocks),), done)
    odd = lax.axis_index("sub")
    width = pos.shape[1]
    wait()
    lane = lax.broadcasted_iota(jnp.int32, (1, width), 1)
    listed = jnp.zeros((1, width), jnp.int32)
    for l in range(blocks.shape[0]):
        listed = jnp.where(lane == l, blocks[l], listed)
    listed = listed.astype(F32)
    sites = rows([pos[...], charge[...], polar[...], listed, jnp.ones((1, width), F32)])
    for half in range(2):
        mine[half] = sites[0:4, half * 128 : half * 128 + 128]
    first, second = send[0:1, :], send[1:2, :]
    swap = jnp.full(first.shape, odd, jnp.int32) == 1
    picks = jnp.where(swap, second, first), jnp.where(swap, first, second)
    raw = table[...]
    other = jnp.where((raw >= 256) & (raw < 512), jnp.bitwise_xor(raw, 128), raw)
    keep = jnp.full(raw.shape, odd, jnp.int32) == 1
    pack[0:8, :] = sites
    pack[8:40, :] = jnp.where(keep, raw, other).astype(F32)
    pack[40:48, :] = rows([jnp.concatenate(picks, axis=1).astype(F32)])
    pieces = split3(sites)
    chosen = [one_hot(row, width) for row in picks]
    for pick, out in zip(chosen, (lent_a, lent_b)):
        found = join3(dot(pieces, pick))
        lent = rows([found[0:5], listed[:, 0:128], jnp.ones((1, 128), F32)])
        out[0:32, :] = jnp.concatenate([split3(lent), jnp.zeros((8, 128), BF16)], axis=0)

    @pl.when(learned())
    def _():
        pltpu.make_async_copy(features_far, features, done.at[6]).wait()
        flipped = flip(features[...]).astype(BF16)
        feat_t[...] = flipped
        for pick, out in zip(chosen, (lent_a, lent_b)):
            out[32:, :] = dot(flipped, pick).astype(BF16)

    @pl.when(jnp.logical_not(learned()))
    def _():
        for out in (lent_a, lent_b):
            out[32:, :] = jnp.zeros((feat_t.shape[0], 128), BF16)


def rim(lent):
    return join3(lent[0:24, :].astype(F32))


def static_kernel(pack, from_a, from_b, w3, w5, fixed, entry, lent_a, lent_b):
    site, slots, picks = views(pack)
    width = site.shape[1]
    depth = 2 * width
    slot_count = slots.shape[0]

    @pl.when(jnp.logical_not(learned()))
    def _():
        table = jnp.concatenate([site[...], rim(from_a), rim(from_b)], axis=1)
        entry[...] = table.T
        tx, ty, tz = site[0:1, :], site[1:2, :], site[2:3, :]

        def some_rows(j, acc):
            start = pl.multiple_of(j * STATIC_CHUNK, STATIC_CHUNK)
            ids = (lax.broadcasted_iota(jnp.int32, (STATIC_CHUNK, width), 0) + start).astype(F32)
            count = jnp.zeros((STATIC_CHUNK, width), F32)
            for k in range(slot_count):
                count = count + jnp.where(ids == slots[k : k + 1, :], 1.0, 0.0)
            cols = entry[pl.ds(start, STATIC_CHUNK), :]
            rx, ry, rz = tx - cols[:, 0:1], ty - cols[:, 1:2], tz - cols[:, 2:3]
            inverse = lax.rsqrt(rx * rx + ry * ry + rz * rz + SMOOTH)
            squared = inverse * inverse
            cube = count * (squared * inverse)
            w3[pl.ds(start, STATIC_CHUNK), :] = cube
            w5[pl.ds(start, STATIC_CHUNK), :] = 3.0 * (cube * squared)
            scale = cols[:, 3:4] * cube
            return acc[0] + rx * scale, acc[1] + ry * scale, acc[2] + rz * scale

        nil = jnp.zeros((STATIC_CHUNK, width), F32)
        sums = lax.fori_loop(0, depth // STATIC_CHUNK, some_rows, (nil, nil, nil))
        total = rows([jnp.sum(s, axis=0, keepdims=True) for s in sums])
        fixed[...] = total
        lend_whole(total, picks, lent_a, lent_b)


def radial_kernel(
    pack, from_a, from_b, w_in_far, w_mid_far,
    third_far, w_in, w_mid, third, done,
):
    site, slots, _ = views(pack)
    width = site.shape[1]
    depth = 2 * width
    slot_count = slots.shape[0]

    @pl.when(learned())
    def _():
        wait = fetch(((w_in_far, w_in), (w_mid_far, w_mid)), done)
        pieces = split3(jnp.concatenate([site[...], rim(from_a), rim(from_b)], axis=1))
        step = RADIAL_SLOTS * width
        here = jnp.concatenate([site[...]] * RADIAL_SLOTS, axis=1)
        centres = lax.broadcasted_iota(jnp.int32, (BASIS, step), 0).astype(F32) * SPACING
        wait()
        first_w = jnp.concatenate([flip(w_in[0]), flip(w_in[1])], axis=0).astype(BF16)
        zero = jnp.zeros((64, 64), F32)

        def both(level):
            top = jnp.concatenate([flip(w_mid[0, level]), zero], axis=1)
            bottom = jnp.concatenate([zero, flip(w_mid[1, level])], axis=1)
            return jnp.concatenate([top, bottom], axis=0).astype(BF16)

        second_w, third_w = both(0), both(1)

        def some_slots(k, carry):
            found = join3(dot(pieces, one_hot(slot_row(slots, k * RADIAL_SLOTS, RADIAL_SLOTS), depth)))
            offset = here - found
            squares = offset * offset
            dist_sq = squares[0:1] + squares[1:2] + squares[2:3] + SMOOTH
            gap = jnp.sqrt(dist_sq) - centres
            basis = jnp.exp(-(gap * gap)).astype(BF16)
            hidden = silu(dot(first_w, basis)).astype(BF16)
            hidden = silu(dot(second_w, hidden)).astype(BF16)
            start = pl.multiple_of(k * step, step)
            third[:, pl.ds(start, step)] = silu(dot(third_w, hidden)).astype(BF16)
            return carry

        lax.fori_loop(0, slot_count // RADIAL_SLOTS, some_slots, 0)
        fetch(((third, third_far),), done, 2)()


def lend_pieces(values, picks, lent_a, lent_b):
    pieces = split3(values)
    for row, out in ((0, lent_a), (1, lent_b)):
        found = dot(pieces, one_hot(picked_row(picks, row), values.shape[1]))
        out[...] = jnp.zeros_like(out)
        out[0:32, :] = rows([found], 32).astype(BF16)


def lend_whole(values, picks, lent_a, lent_b):
    pieces = split3(values)
    for row, out in ((0, lent_a), (1, lent_b)):
        out[...] = join3(dot(pieces, one_hot(picked_row(picks, row), values.shape[1])))


def lend_channels(values, picks, lent_a, lent_b):
    for row, out in ((0, lent_a), (1, lent_b)):
        out[...] = dot(values, one_hot(picked_row(picks, row), values.shape[1])).astype(BF16)


def sweep(site, w3, w5, fixed, dipoles, entry, moment):
    width = site.shape[1]
    moment[...] = dipoles.T
    tx, ty, tz = site[0:1, :], site[1:2, :], site[2:3, :]

    def some_rows(j, acc):
        start = pl.multiple_of(j * SWEEP_CHUNK, SWEEP_CHUNK)
        cols, d = entry[pl.ds(start, SWEEP_CHUNK), :], moment[pl.ds(start, SWEEP_CHUNK), :]
        rx, ry, rz = tx - cols[:, 0:1], ty - cols[:, 1:2], tz - cols[:, 2:3]
        dx, dy, dz = d[:, 0:1], d[:, 1:2], d[:, 2:3]
        cube = w3[pl.ds(start, SWEEP_CHUNK), :]
        scale = (rx * dx + ry * dy + rz * dz) * w5[pl.ds(start, SWEEP_CHUNK), :]
        return (
            acc[0] + (rx * scale - dx * cube),
            acc[1] + (ry * scale - dy * cube),
            acc[2] + (rz * scale - dz * cube),
        )

    nil = jnp.zeros((SWEEP_CHUNK, width), F32)
    sums = lax.fori_loop(0, w3.shape[0] // SWEEP_CHUNK, some_rows, (nil, nil, nil), unroll=SWEEP_UNROLL)
    return site[4:5, :] * (fixed + rows([jnp.sum(s, axis=0, keepdims=True) for s in sums]))


def message(layer, hidden, table, third, out_t, node_t, slots, total):
    slot_count = slots.shape[0]
    width = slots.shape[1]
    step = MESSAGE_SLOTS * width
    total[...] = jnp.zeros_like(total)

    def some_slots(k, carry):
        row = slot_row(slots, k * MESSAGE_SLOTS, MESSAGE_SLOTS)
        picked = dot(table, one_hot(row, table.shape[1]))
        start = pl.multiple_of(k * step, step)
        weight = dot(out_t, third[layer * 64 : layer * 64 + 64, pl.ds(start, step)])
        product = weight * picked
        part = product[:, 0:width]
        for i in range(1, MESSAGE_SLOTS):
            part = part + product[:, i * width : (i + 1) * width]
        total[...] += part
        return carry

    lax.fori_loop(0, slot_count // MESSAGE_SLOTS, some_slots, 0)
    mean = (total[...] * (1.0 / slot_count)).astype(BF16)
    return (hidden.astype(F32) + silu(dot(node_t, mean))).astype(BF16)


def charge_field(target, cols, first, count):
    tx, ty, tz = target[0:1, :], target[1:2, :], target[2:3, :]

    def some_rows(j, acc):
        c = cols[pl.ds(pl.multiple_of(first + j * FIELD_CHUNK, FIELD_CHUNK), FIELD_CHUNK), :]
        rx, ry, rz = tx - c[:, 0:1], ty - c[:, 1:2], tz - c[:, 2:3]
        inverse = lax.rsqrt(rx * rx + ry * ry + rz * rz + SMOOTH)
        scale = c[:, 3:4] * (inverse * inverse * inverse)
        return acc[0] + rx * scale, acc[1] + ry * scale, acc[2] + rz * scale

    nil = jnp.zeros((FIELD_CHUNK, target.shape[1]), F32)
    sums = lax.fori_loop(0, count // FIELD_CHUNK, some_rows, (nil, nil, nil), unroll=FIELD_UNROLL)
    return jnp.concatenate([jnp.sum(s, axis=0, keepdims=True) for s in sums], axis=0)


def first_kernel(
    pack, from_a, from_b, feat_t, side_a, side_b, w3, w5, fixed, entry,
    near_far, third_far, node_in_far, node_out_far, w_out_far, gain_far,
    outside_row, near_own, hidden_out, lifted_out, fixed_out, dipole_out, lent_a, lent_b,
    near, cols, third, node_in, node_out, w_out, gain, total, moment, done,
):
    site, slots, picks = views(pack)
    width = site.shape[1]
    listed = near_own.shape[0]
    rim_a, rim_b = rim(from_a), rim(from_b)
    numbers = [listed_block(row[5:6, 0:128], l) for row in (site, rim_a, rim_b) for l in range(listed)]
    fetch([(near_far.at[b], near.at[i]) for i, b in enumerate(numbers)], done, 5)
    weights = (
        (third_far, third), (node_in_far, node_in), (node_out_far.at[0], node_out),
        (w_out_far.at[0], w_out), (gain_far, gain),
    )

    @pl.when(learned())
    def _():
        fetch(weights, done)

    for i, b in enumerate(numbers):
        pltpu.make_async_copy(near_far.at[b], near.at[i], done.at[5 + i]).wait()
    near_own[...] = near[0:listed]
    for i in range(3 * listed):
        tile = near[i]
        cols[i * 128 : i * 128 + 128, :] = jnp.concatenate([tile, tile], axis=0).T
    reach = listed * 128
    own_field = charge_field(site[...], cols, 0, reach)
    field = jnp.concatenate(
        [own_field, charge_field(rim_a, cols, reach, reach), charge_field(rim_b, cols, 2 * reach, reach)],
        axis=1,
    )
    strength = jnp.sqrt(1.0 + (field[0:1] * field[0:1] + field[1:2] * field[1:2] + field[2:3] * field[2:3]))
    outside_row[...] = jnp.broadcast_to(strength[:, :width], outside_row.shape)

    @pl.when(learned())
    def _():
        for i, (a, b) in enumerate(weights):
            pltpu.make_async_copy(a, b, done.at[i]).wait()
        gain_col = jnp.broadcast_to(gain[...], (8, width)).T
        features = jnp.concatenate([feat_t[...], from_a[32:, :], from_b[32:, :]], axis=1)
        start = (features.astype(F32) + gain_col[:, 0:1] * strength).astype(BF16)
        present = jnp.concatenate([jnp.ones((1, width), F32), rim_a[6:7, :], rim_b[6:7, :]], axis=1)
        raised = dot(flip(node_in[0]).astype(BF16), start)
        table = jnp.where(present > 0.5, raised, 0.0).astype(BF16)
        out_t, node_t = flip(w_out[...]).astype(BF16), flip(node_out[...]).astype(BF16)
        new = message(0, start[:, :width], table, third, out_t, node_t, slots, total)
        hidden_out[...] = new
        raised = dot(flip(node_in[1]).astype(BF16), new).astype(BF16)
        lifted_out[...] = raised
        lend_channels(raised, picks, lent_a, lent_b)

    @pl.when(jnp.logical_not(learned()))
    def _():
        whole = jnp.concatenate([fixed[...], side_a[...], side_b[...]], axis=1) + rows([field])
        fixed_out[...] = whole[:, :width]
        polar = jnp.concatenate([site[4:5, :], rim_a[4:5, :], rim_b[4:5, :]], axis=1)
        new = sweep(site, w3, w5, whole[:, :width], polar * whole, entry, moment)
        dipole_out[...] = new
        lend_pieces(new, picks, lent_a, lent_b)


def second_kernel(
    hidden, lifted, side_a, side_b, pack, w3, w5, fixed, dipole, entry,
    third_far, node_out_far, w_out_far, readout_far,
    charge, dipole_out, small_a, small_b,
    third, node_out, w_out, readout, total, moment, done,
):
    site, slots, picks = views(pack)

    @pl.when(learned())
    def _():
        fetch(
            ((third_far, third), (node_out_far.at[1], node_out), (w_out_far.at[1], w_out), (readout_far, readout)), done
        )()
        table = jnp.concatenate([lifted[...], side_a[...], side_b[...]], axis=1)
        out_t, node_t = flip(w_out[...]).astype(BF16), flip(node_out[...]).astype(BF16)
        new = message(1, hidden[...], table, third, out_t, node_t, slots, total)
        charge[...] = dot(rows([readout[...].astype(F32)]).astype(BF16), new)

    @pl.when(jnp.logical_not(learned()))
    def _():
        sides = [join3(side_a[0:24, :].astype(F32)), join3(side_b[0:24, :].astype(F32))]
        table = jnp.concatenate([dipole[...]] + sides, axis=1)
        new = sweep(site, w3, w5, fixed[...], table, entry, moment)
        dipole_out[...] = new
        lend_whole(new, picks, small_a, small_b)


def third_kernel(side_a, side_b, pack, w3, w5, fixed, dipole, entry, dipole_out, small_a, small_b, moment):
    site, _, picks = views(pack)

    @pl.when(jnp.logical_not(learned()))
    def _():
        table = jnp.concatenate([dipole[...], side_a[...], side_b[...]], axis=1)
        new = sweep(site, w3, w5, fixed[...], table, entry, moment)
        dipole_out[...] = new
        lend_whole(new, picks, small_a, small_b)


def response_kernel(
    near, pack, charge, outside_row, side_a, side_b, w3, w5, fixed, dipole, entry,
    result, spread, cols, moment, term,
):
    site = views(pack)[0]
    width = site.shape[1]
    listed = near.shape[0]
    blocks = [listed_block(site[5:6, 0:128], l) for l in range(listed)]
    spread[...] = jnp.zeros_like(spread)
    term[...] = jnp.zeros_like(term)

    def terms(dipoles):
        for l in range(listed):
            tile = near[l]
            tx, ty, tz = tile[0:1, :], tile[1:2, :], tile[2:3, :]

            def some_rows(j, acc):
                start = pl.multiple_of(j * TERM_CHUNK, TERM_CHUNK)
                c = cols[pl.ds(start, TERM_CHUNK), :]
                rx, ry, rz = tx - c[:, 0:1], ty - c[:, 1:2], tz - c[:, 2:3]
                inverse = lax.rsqrt(rx * rx + ry * ry + rz * rz + SMOOTH)
                squared = inverse * inverse
                cube = squared * inverse
                if dipoles:
                    dx, dy, dz = c[:, 4:5], c[:, 5:6], c[:, 6:7]
                    scale = (rx * dx + ry * dy + rz * dz) * (3.0 * (cube * squared))
                    return (
                        acc[0] + (rx * scale - dx * cube),
                        acc[1] + (ry * scale - dy * cube),
                        acc[2] + (rz * scale - dz * cube),
                    )
                scale = c[:, 3:4] * cube
                return acc[0] + rx * scale, acc[1] + ry * scale, acc[2] + rz * scale

            nil = jnp.zeros((TERM_CHUNK, 128), F32)
            sums = lax.fori_loop(0, width // TERM_CHUNK, some_rows, (nil, nil, nil), unroll=TERM_UNROLL)
            for axis in range(3):
                term[l, axis : axis + 1, :] = jnp.sum(sums[axis], axis=0, keepdims=True)

    @pl.when(learned())
    def _():
        q = charge[...]
        result[...] = jnp.concatenate([q[0:2], outside_row[0:1, :]], axis=0)
        cols[...] = rows([site[0:3, :], q[0:1]]).T
        terms(False)

    @pl.when(jnp.logical_not(learned()))
    def _():
        table = jnp.concatenate([dipole[...], side_a[...], side_b[...]], axis=1)
        new = sweep(site, w3, w5, fixed[...], table, entry, moment)
        result[...] = new[0:3]
        cols[...] = rows([site[0:4, :], new[0:3]]).T
        terms(True)

    side = lax.broadcasted_iota(jnp.int32, (2, 128), 0)
    for l in range(listed):
        owner, part = blocks[l] >> 1, blocks[l] & 1
        for axis in range(3):
            spread[3 * owner + axis] += jnp.where(side == part, term[l, axis : axis + 1, :], 0.0)


def gather_kernel(pieces, share):
    total = jnp.sum(pieces[...], axis=0)
    share[...] = jnp.concatenate(
        [jnp.concatenate([total[axis, 0:1], total[axis, 1:2]], axis=1) for axis in range(3)], axis=0
    )


def placed(block):
    y_half, plane, step, side = block // 64, block // 8 % 8, block // 2 % 4, block % 2
    x = 3 - step if plane % 2 else step
    z = (plane - 1) % 8 if y_half else plane
    along = 1 - side if (step + y_half) % 2 == 0 else side
    y = 2 * y_half + along
    return ((y % 2 * 8 + z) * 4 + x) * 2 + y // 2


def local(
    positions, charges, polar, features, neighbours, send_rows, blocks,
    radial_in, radial_mid, radial_out, node_in, node_out, field_gain, readout,
):
    width = positions.shape[1]
    slot_count = neighbours.shape[1]
    depth = 2 * width
    half = send_rows.shape[1]
    channels = features.shape[1]
    listed = blocks.shape[0]
    members = lax.axis_size(DOM)
    near_pairs = [(i, i ^ 1) for i in range(members)]
    far_pairs = [(i, ((i - 1) ^ 1) + 1) for i in range(1, members - 1)]
    same = list(range(members))
    place = [placed(i) for i in range(members)]

    def move(value, pairs, source, target, groups=(0, 1)):
        return lax.ppermute(
            value, EVERY, [(source[a] + g * members, target[b] + g * members) for g in groups for a, b in pairs]
        )

    def trade(a, b, groups=(0, 1), source=place):
        return move(a, near_pairs, source, place, groups), move(b, far_pairs, source, place, groups)

    row8, table8 = ((8, width), F32), ((8, half), F32)
    wide = ((channels, half), BF16)
    by_site = ((channels, width), BF16)
    ints = jnp.int32
    first_lent = ((32 + channels, half), BF16)
    itself = [(i, i) for i in range(members)]
    pack, mine, lent_a, lent_b, feat_t = call(
        rows_kernel, [((slot_count + 16, width), F32), ((2, 4, half), F32), first_lent, first_lent, by_site],
        (), (positions, charges[None], polar[None], neighbours.T, send_rows, blocks, features),
        [pltpu.VMEM((3, width), F32), pltpu.VMEM((1, width), F32), pltpu.VMEM((1, width), F32),
         pltpu.VMEM((slot_count, width), ints), pltpu.VMEM((2, half), ints), pltpu.SMEM((listed,), ints),
         pltpu.VMEM((width, channels), BF16)], 7,
    )
    partner = lax.ppermute(mine, "grp", [(0, 1), (1, 0)])
    copies = jnp.broadcast_to(partner[None], (members,) + partner.shape)
    near = lax.all_to_all(copies, DOM, 0, 0, tiled=True).reshape(2 * members, 4, half)
    pack = move(pack, itself, same, place)
    rim_a, rim_b = trade(lent_a, lent_b, source=same)
    feat_t, pack, rim_a, rim_b = lax.optimization_barrier((feat_t, pack, rim_a, rim_b))
    feat_t = move(feat_t, itself, same, place, (0,))
    w3, w5, fixed, entry, lent_a, lent_b = call(
        static_kernel, [((depth, width), F32), ((depth, width), F32), row8, ((depth, 8), F32), table8, table8],
        (pack, rim_a, rim_b),
    )
    side_a, side_b = trade(lent_a, lent_b, (1,))
    third_shape = (LAYERS * radial_in.shape[2], slot_count * width)
    (third,) = call(
        radial_kernel, [(third_shape, BF16)], (pack, rim_a, rim_b), (radial_in, radial_mid),
        [pltpu.VMEM(radial_in.shape, BF16), pltpu.VMEM(radial_mid.shape, BF16), pltpu.VMEM(third_shape, BF16)], 3, 1,
    )
    moment = pltpu.VMEM((depth, 8), F32)
    total = pltpu.VMEM((channels, width), F32)
    square = pltpu.VMEM(node_out.shape[1:], BF16)
    last = pltpu.VMEM(radial_out.shape[1:], BF16)
    outside_row, near_own, hidden, lifted, fixed_all, dipole, lent_a, lent_b = call(
        first_kernel, [row8, ((listed, 4, half), F32), by_site, by_site, row8, row8, wide, wide],
        (pack, rim_a, rim_b, feat_t, side_a, side_b, w3, w5, fixed, entry),
        (near, third, node_in, node_out, radial_out, field_gain[None]),
        [pltpu.VMEM((3 * listed, 4, half), F32), pltpu.VMEM((3 * listed * half, 8), F32),
         pltpu.VMEM(third_shape, BF16), pltpu.VMEM(node_in.shape, BF16), square, last,
         pltpu.VMEM((1, channels), F32), total, moment], 5 + 3 * listed, loose=1,
    )
    side_a, side_b = trade(lent_a, lent_b)
    charge, dipole, small_a, small_b = call(
        second_kernel, [row8, row8, table8, table8],
        (hidden, lifted, side_a, side_b, pack, w3, w5, fixed_all, dipole, entry),
        (third, node_out, radial_out, readout.T),
        [pltpu.VMEM(third_shape, BF16), square, last, pltpu.VMEM((2, channels), BF16), total, moment], 4,
    )
    side_a, side_b = trade(small_a, small_b, (1,))
    dipole, small_a, small_b = call(
        third_kernel, [row8, table8, table8], (side_a, side_b, pack, w3, w5, fixed_all, dipole, entry),
        (), [moment],
    )
    side_a, side_b = trade(small_a, small_b, (1,))
    result, spread = call(
        response_kernel, [((3, width), F32), ((3 * members, 2, half), F32)],
        (near_own, pack, charge, outside_row, side_a, side_b, w3, w5, fixed_all, dipole, entry), (),
        [pltpu.VMEM((width, 8), F32), moment, pltpu.VMEM((listed, 4, half), F32)],
    )
    pieces = lax.all_to_all(spread, DOM, 0, 0, tiled=True).reshape(members, 3, 2, half)
    (share,) = call(gather_kernel, [((3, width), F32)], (pieces,))
    result = move(result, itself, place, same)
    return result, lax.ppermute(share, "grp", [(0, 1), (1, 0)])


def solution(mesh):
    sites = P(None, EVERY)
    in_specs = (sites, P(EVERY), P(EVERY), P(EVERY, None), P(EVERY, None), sites, P(EVERY)) + (P(),) * 7
    return jax.shard_map(local, mesh=mesh, in_specs=in_specs, out_specs=(sites, sites), check_vma=False)
```

```python
import jax
import jax.numpy as jnp
from jax import lax
from jax.experimental import pallas as pl
from jax.experimental.pallas import tpu as pltpu
from jax.sharding import PartitionSpec as P

BASIS = 8
LAYERS = 2
SMOOTH = 1.0
SPACING = 0.75
DOM = ("dom", "sub")
EVERY = ("grp", "dom", "sub")
F32 = jnp.float32
BF16 = jnp.bfloat16
VMEM = pl.BlockSpec(memory_space=pltpu.VMEM)
ANY = pl.BlockSpec(memory_space=pl.ANY)
SWEEP_CHUNK, SWEEP_UNROLL = 32, 4
FIELD_CHUNK, FIELD_UNROLL = 32, 4
TERM_CHUNK, TERM_UNROLL = 64, 4
STATIC_CHUNK = 32
RADIAL_SLOTS = 16
MESSAGE_SLOTS = 16


def call(body, outs, held, far=(), scratch=(), copies=0, far_outs=0, loose=0):
    return pl.pallas_call(
        body,
        out_shape=[jax.ShapeDtypeStruct(s, d) for s, d in outs[: len(outs) - far_outs]]
        + [pltpu.HBM(s, d) for s, d in outs[len(outs) - far_outs :]],
        in_specs=[VMEM] * len(held) + [ANY] * len(far),
        out_specs=[VMEM] * (len(outs) - far_outs) + [ANY] * far_outs,
        scratch_shapes=list(scratch) + ([pltpu.SemaphoreType.DMA((copies,))] if copies else []),
        compiler_params=pltpu.CompilerParams(vmem_limit_bytes=24 * 2**20),
    )(*held, *far[:loose], *[pltpu.with_memory_space_constraint(a, pltpu.HBM) for a in far[loose:]])


def fetch(pairs, done, first=0):
    copies = [pltpu.make_async_copy(a, b, done.at[first + i]) for i, (a, b) in enumerate(pairs)]
    for c in copies:
        c.start()

    def wait():
        for c in copies:
            c.wait()

    return wait


def learned():
    return lax.axis_index("grp") == 0


def dot(a, b):
    return jnp.dot(a, b, preferred_element_type=F32)


def silu(x):
    half = 0.5 * x
    return half + half * jnp.tanh(half)


def flip(x):
    return x.astype(F32).T


def split3(x):
    high = x.astype(BF16)
    rest = x - high.astype(F32)
    mid = rest.astype(BF16)
    low = (rest - mid.astype(F32)).astype(BF16)
    return jnp.concatenate([high, mid, low], axis=0)


def join3(x):
    return x[0:8] + x[8:16] + x[16:24]


def one_hot(row, depth):
    ids = lax.broadcasted_iota(jnp.int32, (depth, row.shape[1]), 0)
    return jnp.where(ids == row.astype(jnp.int32), 1.0, 0.0).astype(BF16)


def views(pack):
    return pack.at[0:8, :], pack.at[8:40, :], pack.at[40:41, :]


def picked_row(picks, row):
    return picks[0:1, row * 128 : row * 128 + 128]


def listed_block(row, l):
    lane = lax.broadcasted_iota(jnp.int32, row.shape, 1)
    return jnp.sum(jnp.where(lane == l, row, 0.0)).astype(jnp.int32)


def slot_row(slots, first, count):
    return jnp.concatenate([slots[pl.ds(first + i, 1), :] for i in range(count)], axis=1)


def rows(parts, count=8):
    have = sum(p.shape[0] for p in parts)
    return jnp.concatenate(list(parts) + [jnp.zeros((count - have, parts[0].shape[1]), F32)], axis=0)


def rows_kernel(
    pos_far, charge_far, polar_far, table_far, send_far, blocks_far,
    pack, mine, lent_a, lent_b,
    pos, charge, polar, table, send, blocks, done,
):
    pairs = ((pos_far, pos), (charge_far, charge), (polar_far, polar), (table_far, table), (send_far, send))
    wait = fetch(pairs + ((blocks_far, blocks),), done)
    odd = lax.axis_index("sub")
    width = pos.shape[1]
    wait()
    lane = lax.broadcasted_iota(jnp.int32, (1, width), 1)
    listed = jnp.zeros((1, width), jnp.int32)
    for l in range(blocks.shape[0]):
        listed = jnp.where(lane == l, blocks[l], listed)
    listed = listed.astype(F32)
    sites = rows([pos[...], charge[...], polar[...], listed, jnp.ones((1, width), F32)])
    for half in range(2):
        mine[half] = sites[0:4, half * 128 : half * 128 + 128]
    first, second = send[0:1, :], send[1:2, :]
    swap = jnp.full(first.shape, odd, jnp.int32) == 1
    picks = jnp.where(swap, second, first), jnp.where(swap, first, second)
    raw = table[...]
    other = jnp.where((raw >= 256) & (raw < 512), jnp.bitwise_xor(raw, 128), raw)
    keep = jnp.full(raw.shape, odd, jnp.int32) == 1
    pack[0:8, :] = sites
    pack[8:40, :] = jnp.where(keep, raw, other).astype(F32)
    pack[40:48, :] = rows([jnp.concatenate(picks, axis=1).astype(F32)])
    pieces = split3(sites)
    for row, out in zip(picks, (lent_a, lent_b)):
        found = join3(dot(pieces, one_hot(row, width)))
        out[...] = rows([found[0:5], listed[:, 0:128], jnp.ones((1, 128), F32)])


def static_kernel(
    pack, rim_a, rim_b, features_far,
    feat_t, w3, w5, fixed, entry, lent_a, lent_b, features, done,
):
    site, slots, picks = views(pack)
    width = site.shape[1]
    depth = 2 * width
    slot_count = slots.shape[0]

    @pl.when(learned())
    def _():
        fetch(((features_far, features),), done)()
        flipped = flip(features[...]).astype(BF16)
        feat_t[...] = flipped
        lend_channels(flipped, picks, lent_a, lent_b)

    @pl.when(jnp.logical_not(learned()))
    def _():
        table = jnp.concatenate([site[...], rim_a[...], rim_b[...]], axis=1)
        entry[...] = table.T
        tx, ty, tz = site[0:1, :], site[1:2, :], site[2:3, :]

        def some_rows(j, acc):
            start = pl.multiple_of(j * STATIC_CHUNK, STATIC_CHUNK)
            ids = (lax.broadcasted_iota(jnp.int32, (STATIC_CHUNK, width), 0) + start).astype(F32)
            count = jnp.zeros((STATIC_CHUNK, width), F32)
            for k in range(slot_count):
                count = count + jnp.where(ids == slots[k : k + 1, :], 1.0, 0.0)
            cols = entry[pl.ds(start, STATIC_CHUNK), :]
            rx, ry, rz = tx - cols[:, 0:1], ty - cols[:, 1:2], tz - cols[:, 2:3]
            inverse = lax.rsqrt(rx * rx + ry * ry + rz * rz + SMOOTH)
            squared = inverse * inverse
            cube = count * (squared * inverse)
            w3[pl.ds(start, STATIC_CHUNK), :] = cube
            w5[pl.ds(start, STATIC_CHUNK), :] = 3.0 * (cube * squared)
            scale = cols[:, 3:4] * cube
            return acc[0] + rx * scale, acc[1] + ry * scale, acc[2] + rz * scale

        nil = jnp.zeros((STATIC_CHUNK, width), F32)
        sums = lax.fori_loop(0, depth // STATIC_CHUNK, some_rows, (nil, nil, nil))
        total = rows([jnp.sum(s, axis=0, keepdims=True) for s in sums])
        fixed[...] = total
        lend_pieces(total, picks, lent_a, lent_b)


def radial_kernel(
    pack, rim_a, rim_b, w_in_far, w_mid_far,
    third_far, w_in, w_mid, third, done,
):
    site, slots, _ = views(pack)
    width = site.shape[1]
    depth = 2 * width
    slot_count = slots.shape[0]

    @pl.when(learned())
    def _():
        wait = fetch(((w_in_far, w_in), (w_mid_far, w_mid)), done)
        pieces = split3(jnp.concatenate([site[...], rim_a[...], rim_b[...]], axis=1))
        step = RADIAL_SLOTS * width
        here = jnp.concatenate([site[...]] * RADIAL_SLOTS, axis=1)
        centres = lax.broadcasted_iota(jnp.int32, (BASIS, step), 0).astype(F32) * SPACING
        wait()
        first_w = jnp.concatenate([flip(w_in[0]), flip(w_in[1])], axis=0).astype(BF16)
        zero = jnp.zeros((64, 64), F32)

        def both(level):
            top = jnp.concatenate([flip(w_mid[0, level]), zero], axis=1)
            bottom = jnp.concatenate([zero, flip(w_mid[1, level])], axis=1)
            return jnp.concatenate([top, bottom], axis=0).astype(BF16)

        second_w, third_w = both(0), both(1)

        def some_slots(k, carry):
            found = join3(dot(pieces, one_hot(slot_row(slots, k * RADIAL_SLOTS, RADIAL_SLOTS), depth)))
            offset = here - found
            squares = offset * offset
            dist_sq = squares[0:1] + squares[1:2] + squares[2:3] + SMOOTH
            gap = jnp.sqrt(dist_sq) - centres
            basis = jnp.exp(-(gap * gap)).astype(BF16)
            hidden = silu(dot(first_w, basis)).astype(BF16)
            hidden = silu(dot(second_w, hidden)).astype(BF16)
            start = pl.multiple_of(k * step, step)
            third[:, pl.ds(start, step)] = silu(dot(third_w, hidden)).astype(BF16)
            return carry

        lax.fori_loop(0, slot_count // RADIAL_SLOTS, some_slots, 0)
        fetch(((third, third_far),), done, 2)()


def lend_pieces(values, picks, lent_a, lent_b):
    pieces = split3(values)
    for row, out in ((0, lent_a), (1, lent_b)):
        found = dot(pieces, one_hot(picked_row(picks, row), values.shape[1]))
        out[...] = jnp.zeros_like(out)
        out[0:32, :] = rows([found], 32).astype(BF16)


def lend_whole(values, picks, lent_a, lent_b):
    pieces = split3(values)
    for row, out in ((0, lent_a), (1, lent_b)):
        out[...] = join3(dot(pieces, one_hot(picked_row(picks, row), values.shape[1])))


def lend_channels(values, picks, lent_a, lent_b):
    for row, out in ((0, lent_a), (1, lent_b)):
        out[...] = dot(values, one_hot(picked_row(picks, row), values.shape[1])).astype(BF16)


def sweep(site, w3, w5, fixed, dipoles, entry, moment):
    width = site.shape[1]
    moment[...] = dipoles.T
    tx, ty, tz = site[0:1, :], site[1:2, :], site[2:3, :]

    def some_rows(j, acc):
        start = pl.multiple_of(j * SWEEP_CHUNK, SWEEP_CHUNK)
        cols, d = entry[pl.ds(start, SWEEP_CHUNK), :], moment[pl.ds(start, SWEEP_CHUNK), :]
        rx, ry, rz = tx - cols[:, 0:1], ty - cols[:, 1:2], tz - cols[:, 2:3]
        dx, dy, dz = d[:, 0:1], d[:, 1:2], d[:, 2:3]
        cube = w3[pl.ds(start, SWEEP_CHUNK), :]
        scale = (rx * dx + ry * dy + rz * dz) * w5[pl.ds(start, SWEEP_CHUNK), :]
        return (
            acc[0] + (rx * scale - dx * cube),
            acc[1] + (ry * scale - dy * cube),
            acc[2] + (rz * scale - dz * cube),
        )

    nil = jnp.zeros((SWEEP_CHUNK, width), F32)
    sums = lax.fori_loop(0, w3.shape[0] // SWEEP_CHUNK, some_rows, (nil, nil, nil), unroll=SWEEP_UNROLL)
    return site[4:5, :] * (fixed + rows([jnp.sum(s, axis=0, keepdims=True) for s in sums]))


def message(layer, hidden, table, third, out_t, node_t, slots, total):
    slot_count = slots.shape[0]
    width = slots.shape[1]
    step = MESSAGE_SLOTS * width
    total[...] = jnp.zeros_like(total)

    def some_slots(k, carry):
        row = slot_row(slots, k * MESSAGE_SLOTS, MESSAGE_SLOTS)
        picked = dot(table, one_hot(row, table.shape[1]))
        start = pl.multiple_of(k * step, step)
        weight = dot(out_t, third[layer * 64 : layer * 64 + 64, pl.ds(start, step)])
        product = weight * picked
        part = product[:, 0:width]
        for i in range(1, MESSAGE_SLOTS):
            part = part + product[:, i * width : (i + 1) * width]
        total[...] += part
        return carry

    lax.fori_loop(0, slot_count // MESSAGE_SLOTS, some_slots, 0)
    mean = (total[...] * (1.0 / slot_count)).astype(BF16)
    return (hidden.astype(F32) + silu(dot(node_t, mean))).astype(BF16)


def charge_field(target, cols, first, count):
    tx, ty, tz = target[0:1, :], target[1:2, :], target[2:3, :]

    def some_rows(j, acc):
        c = cols[pl.ds(pl.multiple_of(first + j * FIELD_CHUNK, FIELD_CHUNK), FIELD_CHUNK), :]
        rx, ry, rz = tx - c[:, 0:1], ty - c[:, 1:2], tz - c[:, 2:3]
        inverse = lax.rsqrt(rx * rx + ry * ry + rz * rz + SMOOTH)
        scale = c[:, 3:4] * (inverse * inverse * inverse)
        return acc[0] + rx * scale, acc[1] + ry * scale, acc[2] + rz * scale

    nil = jnp.zeros((FIELD_CHUNK, target.shape[1]), F32)
    sums = lax.fori_loop(0, count // FIELD_CHUNK, some_rows, (nil, nil, nil), unroll=FIELD_UNROLL)
    return jnp.concatenate([jnp.sum(s, axis=0, keepdims=True) for s in sums], axis=0)


def first_kernel(
    pack, rim_a, rim_b, feat_t, side_a, side_b, w3, w5, fixed, entry,
    near_far, third_far, node_in_far, node_out_far, w_out_far, gain_far,
    outside_row, near_own, hidden_out, lifted_out, fixed_out, dipole_out, lent_a, lent_b,
    near, cols, third, node_in, node_out, w_out, gain, total, moment,
    in_first, in_second, out_t, node_t, gain_col, done,
):
    site, slots, picks = views(pack)
    width = site.shape[1]
    listed = near_own.shape[0]
    weights = (
        (node_in_far, node_in), (node_out_far.at[0], node_out), (w_out_far.at[0], w_out), (gain_far, gain),
        (third_far, third),
    )

    @pl.when(learned())
    def _():
        fetch(weights, done)

    numbers = [listed_block(row[5:6, 0:128], l) for row in (site, rim_a, rim_b) for l in range(listed)]
    fetch([(near_far.at[b], near.at[i]) for i, b in enumerate(numbers)], done, 5)

    @pl.when(learned())
    def _():
        for i, (source, target) in enumerate(weights[:4]):
            pltpu.make_async_copy(source, target, done.at[i]).wait()
        in_first[...] = flip(node_in[0]).astype(BF16)
        in_second[...] = flip(node_in[1]).astype(BF16)
        out_t[...] = flip(w_out[...]).astype(BF16)
        node_t[...] = flip(node_out[...]).astype(BF16)
        gain_col[...] = jnp.broadcast_to(gain[...], (8, width)).T

    for i, b in enumerate(numbers):
        pltpu.make_async_copy(near_far.at[b], near.at[i], done.at[5 + i]).wait()
    near_own[...] = near[0:listed]
    for i in range(3 * listed):
        tile = near[i]
        cols[i * 128 : i * 128 + 128, :] = jnp.concatenate([tile, tile], axis=0).T
    reach = listed * 128
    own_field = charge_field(site[...], cols, 0, reach)
    field = jnp.concatenate(
        [own_field, charge_field(rim_a[...], cols, reach, reach), charge_field(rim_b[...], cols, 2 * reach, reach)],
        axis=1,
    )
    strength = jnp.sqrt(1.0 + (field[0:1] * field[0:1] + field[1:2] * field[1:2] + field[2:3] * field[2:3]))
    outside_row[...] = jnp.broadcast_to(strength[:, :width], outside_row.shape)

    @pl.when(learned())
    def _():
        features = jnp.concatenate([feat_t[...], side_a[...], side_b[...]], axis=1)
        start = (features.astype(F32) + gain_col[:, 0:1] * strength).astype(BF16)
        present = jnp.concatenate([jnp.ones((1, width), F32), rim_a[6:7, :], rim_b[6:7, :]], axis=1)
        raised = dot(in_first[...], start)
        table = jnp.where(present > 0.5, raised, 0.0).astype(BF16)
        pltpu.make_async_copy(third_far, third, done.at[4]).wait()
        new = message(0, start[:, :width], table, third, out_t[...], node_t[...], slots, total)
        hidden_out[...] = new
        raised = dot(in_second[...], new).astype(BF16)
        lifted_out[...] = raised
        lend_channels(raised, picks, lent_a, lent_b)

    @pl.when(jnp.logical_not(learned()))
    def _():
        known = [fixed[...], join3(side_a[0:24, :].astype(F32)), join3(side_b[0:24, :].astype(F32))]
        whole = jnp.concatenate(known, axis=1) + rows([field])
        fixed_out[...] = whole[:, :width]
        polar = jnp.concatenate([site[4:5, :], rim_a[4:5, :], rim_b[4:5, :]], axis=1)
        new = sweep(site, w3, w5, whole[:, :width], polar * whole, entry, moment)
        dipole_out[...] = new
        lend_pieces(new, picks, lent_a, lent_b)


def second_kernel(
    hidden, lifted, side_a, side_b, pack, w3, w5, fixed, dipole, entry,
    third_far, node_out_far, w_out_far, readout_far,
    charge, dipole_out, small_a, small_b,
    third, node_out, w_out, readout, total, moment, done,
):
    site, slots, picks = views(pack)

    @pl.when(learned())
    def _():
        fetch(
            ((third_far, third), (node_out_far.at[1], node_out), (w_out_far.at[1], w_out), (readout_far, readout)), done
        )()
        table = jnp.concatenate([lifted[...], side_a[...], side_b[...]], axis=1)
        out_t, node_t = flip(w_out[...]).astype(BF16), flip(node_out[...]).astype(BF16)
        new = message(1, hidden[...], table, third, out_t, node_t, slots, total)
        charge[...] = dot(rows([readout[...].astype(F32)]).astype(BF16), new)

    @pl.when(jnp.logical_not(learned()))
    def _():
        sides = [join3(side_a[0:24, :].astype(F32)), join3(side_b[0:24, :].astype(F32))]
        table = jnp.concatenate([dipole[...]] + sides, axis=1)
        new = sweep(site, w3, w5, fixed[...], table, entry, moment)
        dipole_out[...] = new
        lend_whole(new, picks, small_a, small_b)


def third_kernel(side_a, side_b, pack, w3, w5, fixed, dipole, entry, dipole_out, small_a, small_b, moment):
    site, _, picks = views(pack)

    @pl.when(jnp.logical_not(learned()))
    def _():
        table = jnp.concatenate([dipole[...], side_a[...], side_b[...]], axis=1)
        new = sweep(site, w3, w5, fixed[...], table, entry, moment)
        dipole_out[...] = new
        lend_whole(new, picks, small_a, small_b)


def response_kernel(
    near, pack, charge, outside_row, side_a, side_b, w3, w5, fixed, dipole, entry,
    result, spread, cols, moment, term,
):
    site = views(pack)[0]
    width = site.shape[1]
    listed = near.shape[0]
    blocks = [listed_block(site[5:6, 0:128], l) for l in range(listed)]
    spread[...] = jnp.zeros_like(spread)
    term[...] = jnp.zeros_like(term)

    def terms(dipoles):
        for l in range(listed):
            tile = near[l]
            tx, ty, tz = tile[0:1, :], tile[1:2, :], tile[2:3, :]

            def some_rows(j, acc):
                start = pl.multiple_of(j * TERM_CHUNK, TERM_CHUNK)
                c = cols[pl.ds(start, TERM_CHUNK), :]
                rx, ry, rz = tx - c[:, 0:1], ty - c[:, 1:2], tz - c[:, 2:3]
                inverse = lax.rsqrt(rx * rx + ry * ry + rz * rz + SMOOTH)
                squared = inverse * inverse
                cube = squared * inverse
                if dipoles:
                    dx, dy, dz = c[:, 4:5], c[:, 5:6], c[:, 6:7]
                    scale = (rx * dx + ry * dy + rz * dz) * (3.0 * (cube * squared))
                    return (
                        acc[0] + (rx * scale - dx * cube),
                        acc[1] + (ry * scale - dy * cube),
                        acc[2] + (rz * scale - dz * cube),
                    )
                scale = c[:, 3:4] * cube
                return acc[0] + rx * scale, acc[1] + ry * scale, acc[2] + rz * scale

            nil = jnp.zeros((TERM_CHUNK, 128), F32)
            sums = lax.fori_loop(0, width // TERM_CHUNK, some_rows, (nil, nil, nil), unroll=TERM_UNROLL)
            for axis in range(3):
                term[l, axis : axis + 1, :] = jnp.sum(sums[axis], axis=0, keepdims=True)

    @pl.when(learned())
    def _():
        q = charge[...]
        result[...] = jnp.concatenate([q[0:2], outside_row[0:1, :]], axis=0)
        cols[...] = rows([site[0:3, :], q[0:1]]).T
        terms(False)

    @pl.when(jnp.logical_not(learned()))
    def _():
        table = jnp.concatenate([dipole[...], side_a[...], side_b[...]], axis=1)
        new = sweep(site, w3, w5, fixed[...], table, entry, moment)
        result[...] = new[0:3]
        cols[...] = rows([site[0:4, :], new[0:3]]).T
        terms(True)

    side = lax.broadcasted_iota(jnp.int32, (2, 128), 0)
    for l in range(listed):
        owner, part = blocks[l] >> 1, blocks[l] & 1
        for axis in range(3):
            spread[3 * owner + axis] += jnp.where(side == part, term[l, axis : axis + 1, :], 0.0)


def gather_kernel(pieces, share):
    total = jnp.sum(pieces[...], axis=0)
    share[...] = jnp.concatenate(
        [jnp.concatenate([total[axis, 0:1], total[axis, 1:2]], axis=1) for axis in range(3)], axis=0
    )


def finish_kernel(result, share, result_far, share_far, done):
    fetch(((result, result_far), (share, share_far)), done)()


def placed(block):
    y_half, plane, step, side = block // 64, block // 8 % 8, block // 2 % 4, block % 2
    x = 3 - step if plane % 2 else step
    z = (plane - 1) % 8 if y_half else plane
    along = 1 - side if (step + y_half) % 2 == 0 else side
    y = 2 * y_half + along
    return ((y % 2 * 8 + z) * 4 + x) * 2 + y // 2


def local(
    positions, charges, polar, features, neighbours, send_rows, blocks,
    radial_in, radial_mid, radial_out, node_in, node_out, field_gain, readout,
):
    width = positions.shape[1]
    slot_count = neighbours.shape[1]
    depth = 2 * width
    half = send_rows.shape[1]
    channels = features.shape[1]
    listed = blocks.shape[0]
    members = lax.axis_size(DOM)
    near_pairs = [(i, i ^ 1) for i in range(members)]
    far_pairs = [(i, ((i - 1) ^ 1) + 1) for i in range(1, members - 1)]
    same = list(range(members))
    place = [placed(i) for i in range(members)]

    def move(value, pairs, source, target, groups=(0, 1)):
        return lax.ppermute(
            value, EVERY, [(source[a] + g * members, target[b] + g * members) for g in groups for a, b in pairs]
        )

    def trade(a, b, groups=(0, 1), source=place):
        return move(a, near_pairs, source, place, groups), move(b, far_pairs, source, place, groups)

    row8, table8 = ((8, width), F32), ((8, half), F32)
    wide = ((channels, half), BF16)
    by_site = ((channels, width), BF16)
    ints = jnp.int32
    itself = [(i, i) for i in range(members)]
    pack, mine, lent_a, lent_b = call(
        rows_kernel, [((slot_count + 16, width), F32), ((2, 4, half), F32), table8, table8],
        (), (positions, charges[None], polar[None], neighbours.T, send_rows, blocks),
        [pltpu.VMEM((3, width), F32), pltpu.VMEM((1, width), F32), pltpu.VMEM((1, width), F32),
         pltpu.VMEM((slot_count, width), ints), pltpu.VMEM((2, half), ints), pltpu.SMEM((listed,), ints)], 6,
    )
    partner = lax.ppermute(mine, "grp", [(0, 1), (1, 0)])
    copies = jnp.broadcast_to(partner[None], (members,) + partner.shape)
    near = lax.all_to_all(copies, DOM, 0, 0, tiled=True).reshape(2 * members, 4, half)
    pack = move(pack, itself, same, place)
    rim_a, rim_b = trade(lent_a, lent_b, source=same)
    features = move(features, itself, same, place, (0,))
    feat_t, w3, w5, fixed, entry, lent_a, lent_b = call(
        static_kernel, [by_site, ((depth, width), F32), ((depth, width), F32), row8, ((depth, 8), F32), wide, wide],
        (pack, rim_a, rim_b), (features,), [pltpu.VMEM((width, channels), BF16)], 1, loose=1,
    )
    side_a, side_b = trade(lent_a, lent_b)
    third_shape = (LAYERS * radial_in.shape[2], slot_count * width)
    (third,) = call(
        radial_kernel, [(third_shape, BF16)], (pack, rim_a, rim_b), (radial_in, radial_mid),
        [pltpu.VMEM(radial_in.shape, BF16), pltpu.VMEM(radial_mid.shape, BF16), pltpu.VMEM(third_shape, BF16)], 3, 1,
    )
    moment = pltpu.VMEM((depth, 8), F32)
    total = pltpu.VMEM((channels, width), F32)
    square = pltpu.VMEM(node_out.shape[1:], BF16)
    last = pltpu.VMEM(radial_out.shape[1:], BF16)
    outside_row, near_own, hidden, lifted, fixed_all, dipole, lent_a, lent_b = call(
        first_kernel, [row8, ((listed, 4, half), F32), by_site, by_site, row8, row8, wide, wide],
        (pack, rim_a, rim_b, feat_t, side_a, side_b, w3, w5, fixed, entry),
        (near, third, node_in, node_out, radial_out, field_gain[None]),
        [pltpu.VMEM((3 * listed, 4, half), F32), pltpu.VMEM((3 * listed * half, 8), F32),
         pltpu.VMEM(third_shape, BF16), pltpu.VMEM(node_in.shape, BF16), square, last,
         pltpu.VMEM((1, channels), F32), total, moment, square, square,
         pltpu.VMEM((channels, radial_out.shape[1]), BF16), square, pltpu.VMEM((channels, 8), F32)],
        5 + 3 * listed, loose=1,
    )
    side_a, side_b = trade(lent_a, lent_b)
    charge, dipole, small_a, small_b = call(
        second_kernel, [row8, row8, table8, table8],
        (hidden, lifted, side_a, side_b, pack, w3, w5, fixed_all, dipole, entry),
        (third, node_out, radial_out, readout.T),
        [pltpu.VMEM(third_shape, BF16), square, last, pltpu.VMEM((2, channels), BF16), total, moment], 4,
    )
    side_a, side_b = trade(small_a, small_b, (1,))
    dipole, small_a, small_b = call(
        third_kernel, [row8, table8, table8], (side_a, side_b, pack, w3, w5, fixed_all, dipole, entry),
        (), [moment],
    )
    side_a, side_b = trade(small_a, small_b, (1,))
    result, spread = call(
        response_kernel, [((3, width), F32), ((3 * members, 2, half), F32)],
        (near_own, pack, charge, outside_row, side_a, side_b, w3, w5, fixed_all, dipole, entry), (),
        [pltpu.VMEM((width, 8), F32), moment, pltpu.VMEM((listed, 4, half), F32)],
    )
    pieces = lax.all_to_all(spread, DOM, 0, 0, tiled=True).reshape(members, 3, 2, half)
    (share,) = call(gather_kernel, [((3, width), F32)], (pieces,))
    result = move(result, itself, place, same)
    share = lax.ppermute(share, "grp", [(0, 1), (1, 0)])
    whole = ((3, width), F32)
    return tuple(call(finish_kernel, [whole, whole], (result, share), copies=2, far_outs=2))


def solution(mesh):
    sites = P(None, EVERY)
    in_specs = (sites, P(EVERY), P(EVERY), P(EVERY, None), P(EVERY, None), sites, P(EVERY)) + (P(),) * 7
    return jax.shard_map(local, mesh=mesh, in_specs=in_specs, out_specs=(sites, sites), check_vma=False)
```

```python
import jax
import jax.numpy as jnp
from jax import lax
from jax.experimental import pallas as pl
from jax.experimental.pallas import tpu as pltpu
from jax.sharding import PartitionSpec as P

BASIS = 8
LAYERS = 2
SMOOTH = 1.0
SPACING = 0.75
DOM = ("dom", "sub")
EVERY = ("grp", "dom", "sub")
F32 = jnp.float32
BF16 = jnp.bfloat16
VMEM = pl.BlockSpec(memory_space=pltpu.VMEM)
ANY = pl.BlockSpec(memory_space=pl.ANY)
SWEEP_CHUNK, SWEEP_UNROLL = 32, 4
FIELD_CHUNK, FIELD_UNROLL = 32, 4
TERM_CHUNK, TERM_UNROLL = 64, 4
STATIC_CHUNK = 32
RADIAL_SLOTS = 8
MESSAGE_SLOTS = 16


def call(body, outs, held, far=(), scratch=(), copies=0, far_outs=0, loose=0):
    return pl.pallas_call(
        body,
        out_shape=[jax.ShapeDtypeStruct(s, d) for s, d in outs[: len(outs) - far_outs]]
        + [pltpu.HBM(s, d) for s, d in outs[len(outs) - far_outs :]],
        in_specs=[VMEM] * len(held) + [ANY] * len(far),
        out_specs=[VMEM] * (len(outs) - far_outs) + [ANY] * far_outs,
        scratch_shapes=list(scratch) + ([pltpu.SemaphoreType.DMA((copies,))] if copies else []),
        compiler_params=pltpu.CompilerParams(vmem_limit_bytes=24 * 2**20),
    )(*held, *far[:loose], *[pltpu.with_memory_space_constraint(a, pltpu.HBM) for a in far[loose:]])


def fetch(pairs, done, first=0):
    copies = [pltpu.make_async_copy(a, b, done.at[first + i]) for i, (a, b) in enumerate(pairs)]
    for c in copies:
        c.start()

    def wait():
        for c in copies:
            c.wait()

    return wait


def learned():
    return lax.axis_index("grp") == 0


def dot(a, b):
    return jnp.dot(a, b, preferred_element_type=F32)


def silu(x):
    half = 0.5 * x
    return half + half * jnp.tanh(half)


def flip(x):
    return x.astype(F32).T


def split3(x):
    high = x.astype(BF16)
    rest = x - high.astype(F32)
    mid = rest.astype(BF16)
    low = (rest - mid.astype(F32)).astype(BF16)
    return jnp.concatenate([high, mid, low], axis=0)


def join3(x):
    return x[0:8] + x[8:16] + x[16:24]


def one_hot(row, depth):
    ids = lax.broadcasted_iota(jnp.int32, (depth, row.shape[1]), 0)
    return jnp.where(ids == row.astype(jnp.int32), 1.0, 0.0).astype(BF16)


def views(pack):
    return pack.at[0:8, :], pack.at[8:40, :], pack.at[40:41, :]


def picked_row(picks, row):
    return picks[0:1, row * 128 : row * 128 + 128]


def listed_block(row, l):
    lane = lax.broadcasted_iota(jnp.int32, row.shape, 1)
    return jnp.sum(jnp.where(lane == l, row, 0.0)).astype(jnp.int32)


def slot_row(slots, first, count):
    return jnp.concatenate([slots[pl.ds(first + i, 1), :] for i in range(count)], axis=1)


def rows(parts, count=8):
    have = sum(p.shape[0] for p in parts)
    return jnp.concatenate(list(parts) + [jnp.zeros((count - have, parts[0].shape[1]), F32)], axis=0)


def rows_kernel(
    pos_far, charge_far, polar_far, table_far, send_far, blocks_far,
    pack, mine, lent_a, lent_b,
    pos, charge, polar, table, send, blocks, done,
):
    pairs = ((pos_far, pos), (charge_far, charge), (polar_far, polar), (table_far, table), (send_far, send))
    wait = fetch(pairs + ((blocks_far, blocks),), done)
    odd = lax.axis_index("sub")
    width = pos.shape[1]
    wait()
    lane = lax.broadcasted_iota(jnp.int32, (1, width), 1)
    listed = jnp.zeros((1, width), jnp.int32)
    for l in range(blocks.shape[0]):
        listed = jnp.where(lane == l, blocks[l], listed)
    listed = listed.astype(F32)
    sites = rows([pos[...], charge[...], polar[...], listed, jnp.ones((1, width), F32)])
    for half in range(2):
        mine[half] = sites[0:4, half * 128 : half * 128 + 128]
    first, second = send[0:1, :], send[1:2, :]
    swap = jnp.full(first.shape, odd, jnp.int32) == 1
    picks = jnp.where(swap, second, first), jnp.where(swap, first, second)
    raw = table[...]
    other = jnp.where((raw >= 256) & (raw < 512), jnp.bitwise_xor(raw, 128), raw)
    keep = jnp.full(raw.shape, odd, jnp.int32) == 1
    pack[0:8, :] = sites
    pack[8:40, :] = jnp.where(keep, raw, other).astype(F32)
    pack[40:48, :] = rows([jnp.concatenate(picks, axis=1).astype(F32)])
    pieces = split3(sites)
    for row, out in zip(picks, (lent_a, lent_b)):
        found = join3(dot(pieces, one_hot(row, width)))
        out[...] = rows([found[0:5], listed[:, 0:128], jnp.ones((1, 128), F32)])


def static_kernel(
    pack, rim_a, rim_b, features_far,
    feat_t, w3, w5, fixed, entry, lent_a, lent_b, features, done,
):
    site, slots, picks = views(pack)
    width = site.shape[1]
    depth = 2 * width
    slot_count = slots.shape[0]

    @pl.when(learned())
    def _():
        fetch(((features_far, features),), done)()
        flipped = flip(features[...]).astype(BF16)
        feat_t[...] = flipped
        lend_channels(flipped, picks, lent_a, lent_b)

    @pl.when(jnp.logical_not(learned()))
    def _():
        table = jnp.concatenate([site[...], rim_a[...], rim_b[...]], axis=1)
        entry[...] = table.T
        tx, ty, tz = site[0:1, :], site[1:2, :], site[2:3, :]

        def some_rows(j, acc):
            start = pl.multiple_of(j * STATIC_CHUNK, STATIC_CHUNK)
            ids = (lax.broadcasted_iota(jnp.int32, (STATIC_CHUNK, width), 0) + start).astype(F32)
            count = jnp.zeros((STATIC_CHUNK, width), F32)
            for k in range(slot_count):
                count = count + jnp.where(ids == slots[k : k + 1, :], 1.0, 0.0)
            cols = entry[pl.ds(start, STATIC_CHUNK), :]
            rx, ry, rz = tx - cols[:, 0:1], ty - cols[:, 1:2], tz - cols[:, 2:3]
            inverse = lax.rsqrt(rx * rx + ry * ry + rz * rz + SMOOTH)
            squared = inverse * inverse
            cube = count * (squared * inverse)
            w3[pl.ds(start, STATIC_CHUNK), :] = cube
            w5[pl.ds(start, STATIC_CHUNK), :] = 3.0 * (cube * squared)
            scale = cols[:, 3:4] * cube
            return acc[0] + rx * scale, acc[1] + ry * scale, acc[2] + rz * scale

        nil = jnp.zeros((STATIC_CHUNK, width), F32)
        sums = lax.fori_loop(0, depth // STATIC_CHUNK, some_rows, (nil, nil, nil))
        total = rows([jnp.sum(s, axis=0, keepdims=True) for s in sums])
        fixed[...] = total
        lend_pieces(total, picks, lent_a, lent_b)


def radial_kernel(
    pack, rim_a, rim_b, w_in_far, w_mid_far,
    third_far, w_in, w_mid, third, done,
):
    site, slots, _ = views(pack)
    width = site.shape[1]
    depth = 2 * width
    slot_count = slots.shape[0]

    @pl.when(learned())
    def _():
        wait = fetch(((w_in_far, w_in), (w_mid_far, w_mid)), done)
        pieces = split3(jnp.concatenate([site[...], rim_a[...], rim_b[...]], axis=1))
        step = RADIAL_SLOTS * width
        here = jnp.concatenate([site[...]] * RADIAL_SLOTS, axis=1)
        centres = lax.broadcasted_iota(jnp.int32, (BASIS, step), 0).astype(F32) * SPACING
        wait()
        first_w = jnp.concatenate([flip(w_in[0]), flip(w_in[1])], axis=0).astype(BF16)
        zero = jnp.zeros((64, 64), F32)

        def both(level):
            top = jnp.concatenate([flip(w_mid[0, level]), zero], axis=1)
            bottom = jnp.concatenate([zero, flip(w_mid[1, level])], axis=1)
            return jnp.concatenate([top, bottom], axis=0).astype(BF16)

        second_w, third_w = both(0), both(1)

        def part_out(k):
            part = pl.ds(pl.multiple_of(k * step, step), step)
            return pltpu.make_async_copy(third.at[:, part], third_far.at[:, part], done.at[2 + k])

        def some_slots(k, carry):
            found = join3(dot(pieces, one_hot(slot_row(slots, k * RADIAL_SLOTS, RADIAL_SLOTS), depth)))
            offset = here - found
            squares = offset * offset
            dist_sq = squares[0:1] + squares[1:2] + squares[2:3] + SMOOTH
            gap = jnp.sqrt(dist_sq) - centres
            basis = jnp.exp(-(gap * gap)).astype(BF16)
            hidden = silu(dot(first_w, basis)).astype(BF16)
            hidden = silu(dot(second_w, hidden)).astype(BF16)
            start = pl.multiple_of(k * step, step)
            third[:, pl.ds(start, step)] = silu(dot(third_w, hidden)).astype(BF16)
            part_out(k).start()
            return carry

        lax.fori_loop(0, slot_count // RADIAL_SLOTS, some_slots, 0)
        for k in range(slot_count // RADIAL_SLOTS):
            part_out(k).wait()


def lend_pieces(values, picks, lent_a, lent_b):
    pieces = split3(values)
    for row, out in ((0, lent_a), (1, lent_b)):
        found = dot(pieces, one_hot(picked_row(picks, row), values.shape[1]))
        out[...] = jnp.zeros_like(out)
        out[0:32, :] = rows([found], 32).astype(BF16)


def lend_whole(values, picks, lent_a, lent_b):
    pieces = split3(values)
    for row, out in ((0, lent_a), (1, lent_b)):
        out[...] = join3(dot(pieces, one_hot(picked_row(picks, row), values.shape[1])))


def lend_channels(values, picks, lent_a, lent_b):
    for row, out in ((0, lent_a), (1, lent_b)):
        out[...] = dot(values, one_hot(picked_row(picks, row), values.shape[1])).astype(BF16)


def sweep(site, w3, w5, fixed, dipoles, entry, moment):
    width = site.shape[1]
    moment[...] = dipoles.T
    tx, ty, tz = site[0:1, :], site[1:2, :], site[2:3, :]

    def some_rows(j, acc):
        start = pl.multiple_of(j * SWEEP_CHUNK, SWEEP_CHUNK)
        cols, d = entry[pl.ds(start, SWEEP_CHUNK), :], moment[pl.ds(start, SWEEP_CHUNK), :]
        rx, ry, rz = tx - cols[:, 0:1], ty - cols[:, 1:2], tz - cols[:, 2:3]
        dx, dy, dz = d[:, 0:1], d[:, 1:2], d[:, 2:3]
        cube = w3[pl.ds(start, SWEEP_CHUNK), :]
        scale = (rx * dx + ry * dy + rz * dz) * w5[pl.ds(start, SWEEP_CHUNK), :]
        return (
            acc[0] + (rx * scale - dx * cube),
            acc[1] + (ry * scale - dy * cube),
            acc[2] + (rz * scale - dz * cube),
        )

    nil = jnp.zeros((SWEEP_CHUNK, width), F32)
    sums = lax.fori_loop(0, w3.shape[0] // SWEEP_CHUNK, some_rows, (nil, nil, nil), unroll=SWEEP_UNROLL)
    return site[4:5, :] * (fixed + rows([jnp.sum(s, axis=0, keepdims=True) for s in sums]))


def message(layer, hidden, table, third, out_t, node_t, slots, total):
    slot_count = slots.shape[0]
    width = slots.shape[1]
    step = MESSAGE_SLOTS * width
    total[...] = jnp.zeros_like(total)

    def some_slots(k, carry):
        row = slot_row(slots, k * MESSAGE_SLOTS, MESSAGE_SLOTS)
        picked = dot(table, one_hot(row, table.shape[1]))
        start = pl.multiple_of(k * step, step)
        weight = dot(out_t, third[layer * 64 : layer * 64 + 64, pl.ds(start, step)])
        product = weight * picked
        part = product[:, 0:width]
        for i in range(1, MESSAGE_SLOTS):
            part = part + product[:, i * width : (i + 1) * width]
        total[...] += part
        return carry

    lax.fori_loop(0, slot_count // MESSAGE_SLOTS, some_slots, 0)
    mean = (total[...] * (1.0 / slot_count)).astype(BF16)
    return (hidden.astype(F32) + silu(dot(node_t, mean))).astype(BF16)


def charge_field(target, cols, first, count):
    tx, ty, tz = target[0:1, :], target[1:2, :], target[2:3, :]

    def some_rows(j, acc):
        c = cols[pl.ds(pl.multiple_of(first + j * FIELD_CHUNK, FIELD_CHUNK), FIELD_CHUNK), :]
        rx, ry, rz = tx - c[:, 0:1], ty - c[:, 1:2], tz - c[:, 2:3]
        inverse = lax.rsqrt(rx * rx + ry * ry + rz * rz + SMOOTH)
        scale = c[:, 3:4] * (inverse * inverse * inverse)
        return acc[0] + rx * scale, acc[1] + ry * scale, acc[2] + rz * scale

    nil = jnp.zeros((FIELD_CHUNK, target.shape[1]), F32)
    sums = lax.fori_loop(0, count // FIELD_CHUNK, some_rows, (nil, nil, nil), unroll=FIELD_UNROLL)
    return jnp.concatenate([jnp.sum(s, axis=0, keepdims=True) for s in sums], axis=0)


def first_kernel(
    pack, rim_a, rim_b, feat_t, side_a, side_b, w3, w5, fixed, entry,
    near_far, third_far, node_in_far, node_out_far, w_out_far, gain_far,
    outside_row, near_own, hidden_out, lifted_out, fixed_out, dipole_out, lent_a, lent_b,
    near, cols, third, node_in, node_out, w_out, gain, total, moment,
    in_first, in_second, out_t, node_t, gain_col, done,
):
    site, slots, picks = views(pack)
    width = site.shape[1]
    listed = near_own.shape[0]
    weights = (
        (node_in_far, node_in), (node_out_far.at[0], node_out), (w_out_far.at[0], w_out), (gain_far, gain),
        (third_far, third),
    )

    @pl.when(learned())
    def _():
        fetch(weights, done)

    numbers = [listed_block(row[5:6, 0:128], l) for row in (site, rim_a, rim_b) for l in range(listed)]
    fetch([(near_far.at[b], near.at[i]) for i, b in enumerate(numbers)], done, 5)

    @pl.when(learned())
    def _():
        for i, (source, target) in enumerate(weights[:4]):
            pltpu.make_async_copy(source, target, done.at[i]).wait()
        in_first[...] = flip(node_in[0]).astype(BF16)
        in_second[...] = flip(node_in[1]).astype(BF16)
        out_t[...] = flip(w_out[...]).astype(BF16)
        node_t[...] = flip(node_out[...]).astype(BF16)
        gain_col[...] = jnp.broadcast_to(gain[...], (8, width)).T

    for i, b in enumerate(numbers):
        pltpu.make_async_copy(near_far.at[b], near.at[i], done.at[5 + i]).wait()
    near_own[...] = near[0:listed]
    for i in range(3 * listed):
        tile = near[i]
        cols[i * 128 : i * 128 + 128, :] = jnp.concatenate([tile, tile], axis=0).T
    reach = listed * 128
    own_field = charge_field(site[...], cols, 0, reach)
    field = jnp.concatenate(
        [own_field, charge_field(rim_a[...], cols, reach, reach), charge_field(rim_b[...], cols, 2 * reach, reach)],
        axis=1,
    )
    strength = jnp.sqrt(1.0 + (field[0:1] * field[0:1] + field[1:2] * field[1:2] + field[2:3] * field[2:3]))
    outside_row[...] = jnp.broadcast_to(strength[:, :width], outside_row.shape)

    @pl.when(learned())
    def _():
        features = jnp.concatenate([feat_t[...], side_a[...], side_b[...]], axis=1)
        start = (features.astype(F32) + gain_col[:, 0:1] * strength).astype(BF16)
        present = jnp.concatenate([jnp.ones((1, width), F32), rim_a[6:7, :], rim_b[6:7, :]], axis=1)
        raised = dot(in_first[...], start)
        table = jnp.where(present > 0.5, raised, 0.0).astype(BF16)
        pltpu.make_async_copy(third_far, third, done.at[4]).wait()
        new = message(0, start[:, :width], table, third, out_t[...], node_t[...], slots, total)
        hidden_out[...] = new
        raised = dot(in_second[...], new).astype(BF16)
        lifted_out[...] = raised
        lend_channels(raised, picks, lent_a, lent_b)

    @pl.when(jnp.logical_not(learned()))
    def _():
        known = [fixed[...], join3(side_a[0:24, :].astype(F32)), join3(side_b[0:24, :].astype(F32))]
        whole = jnp.concatenate(known, axis=1) + rows([field])
        fixed_out[...] = whole[:, :width]
        polar = jnp.concatenate([site[4:5, :], rim_a[4:5, :], rim_b[4:5, :]], axis=1)
        new = sweep(site, w3, w5, whole[:, :width], polar * whole, entry, moment)
        dipole_out[...] = new
        lend_pieces(new, picks, lent_a, lent_b)


def second_kernel(
    hidden, lifted, side_a, side_b, pack, w3, w5, fixed, dipole, entry,
    third_far, node_out_far, w_out_far, readout_far,
    charge, dipole_out, small_a, small_b,
    third, node_out, w_out, readout, total, moment, done,
):
    site, slots, picks = views(pack)

    @pl.when(learned())
    def _():
        fetch(
            ((third_far, third), (node_out_far.at[1], node_out), (w_out_far.at[1], w_out), (readout_far, readout)), done
        )()
        table = jnp.concatenate([lifted[...], side_a[...], side_b[...]], axis=1)
        out_t, node_t = flip(w_out[...]).astype(BF16), flip(node_out[...]).astype(BF16)
        new = message(1, hidden[...], table, third, out_t, node_t, slots, total)
        charge[...] = dot(rows([readout[...].astype(F32)]).astype(BF16), new)

    @pl.when(jnp.logical_not(learned()))
    def _():
        sides = [join3(side_a[0:24, :].astype(F32)), join3(side_b[0:24, :].astype(F32))]
        table = jnp.concatenate([dipole[...]] + sides, axis=1)
        new = sweep(site, w3, w5, fixed[...], table, entry, moment)
        dipole_out[...] = new
        lend_whole(new, picks, small_a, small_b)


def third_kernel(side_a, side_b, pack, w3, w5, fixed, dipole, entry, dipole_out, small_a, small_b, moment):
    site, _, picks = views(pack)

    @pl.when(jnp.logical_not(learned()))
    def _():
        table = jnp.concatenate([dipole[...], side_a[...], side_b[...]], axis=1)
        new = sweep(site, w3, w5, fixed[...], table, entry, moment)
        dipole_out[...] = new
        lend_whole(new, picks, small_a, small_b)


def response_kernel(
    near, pack, charge, outside_row, side_a, side_b, w3, w5, fixed, dipole, entry,
    result, spread, cols, moment, term,
):
    site = views(pack)[0]
    width = site.shape[1]
    listed = near.shape[0]
    blocks = [listed_block(site[5:6, 0:128], l) for l in range(listed)]
    spread[...] = jnp.zeros_like(spread)
    term[...] = jnp.zeros_like(term)

    def terms(dipoles):
        for l in range(listed):
            tile = near[l]
            tx, ty, tz = tile[0:1, :], tile[1:2, :], tile[2:3, :]

            def some_rows(j, acc):
                start = pl.multiple_of(j * TERM_CHUNK, TERM_CHUNK)
                c = cols[pl.ds(start, TERM_CHUNK), :]
                rx, ry, rz = tx - c[:, 0:1], ty - c[:, 1:2], tz - c[:, 2:3]
                inverse = lax.rsqrt(rx * rx + ry * ry + rz * rz + SMOOTH)
                squared = inverse * inverse
                cube = squared * inverse
                if dipoles:
                    dx, dy, dz = c[:, 4:5], c[:, 5:6], c[:, 6:7]
                    scale = (rx * dx + ry * dy + rz * dz) * (3.0 * (cube * squared))
                    return (
                        acc[0] + (rx * scale - dx * cube),
                        acc[1] + (ry * scale - dy * cube),
                        acc[2] + (rz * scale - dz * cube),
                    )
                scale = c[:, 3:4] * cube
                return acc[0] + rx * scale, acc[1] + ry * scale, acc[2] + rz * scale

            nil = jnp.zeros((TERM_CHUNK, 128), F32)
            sums = lax.fori_loop(0, width // TERM_CHUNK, some_rows, (nil, nil, nil), unroll=TERM_UNROLL)
            for axis in range(3):
                term[l, axis : axis + 1, :] = jnp.sum(sums[axis], axis=0, keepdims=True)

    @pl.when(learned())
    def _():
        q = charge[...]
        result[...] = jnp.concatenate([q[0:2], outside_row[0:1, :]], axis=0)
        cols[...] = rows([site[0:3, :], q[0:1]]).T
        terms(False)

    @pl.when(jnp.logical_not(learned()))
    def _():
        table = jnp.concatenate([dipole[...], side_a[...], side_b[...]], axis=1)
        new = sweep(site, w3, w5, fixed[...], table, entry, moment)
        result[...] = new[0:3]
        cols[...] = rows([site[0:4, :], new[0:3]]).T
        terms(True)

    side = lax.broadcasted_iota(jnp.int32, (2, 128), 0)
    for l in range(listed):
        owner, part = blocks[l] >> 1, blocks[l] & 1
        for axis in range(3):
            spread[3 * owner + axis] += jnp.where(side == part, term[l, axis : axis + 1, :], 0.0)


def gather_kernel(pieces, share):
    total = jnp.sum(pieces[...], axis=0)
    share[...] = jnp.concatenate(
        [jnp.concatenate([total[axis, 0:1], total[axis, 1:2]], axis=1) for axis in range(3)], axis=0
    )


def finish_kernel(result, share, result_far, share_far, done):
    fetch(((result, result_far), (share, share_far)), done)()


def placed(block):
    y_half, plane, step, side = block // 64, block // 8 % 8, block // 2 % 4, block % 2
    x = 3 - step if plane % 2 else step
    z = (plane - 1) % 8 if y_half else plane
    along = 1 - side if (step + y_half) % 2 == 0 else side
    y = 2 * y_half + along
    return ((y % 2 * 8 + z) * 4 + x) * 2 + y // 2


def local(
    positions, charges, polar, features, neighbours, send_rows, blocks,
    radial_in, radial_mid, radial_out, node_in, node_out, field_gain, readout,
):
    width = positions.shape[1]
    slot_count = neighbours.shape[1]
    depth = 2 * width
    half = send_rows.shape[1]
    channels = features.shape[1]
    listed = blocks.shape[0]
    members = lax.axis_size(DOM)
    near_pairs = [(i, i ^ 1) for i in range(members)]
    far_pairs = [(i, ((i - 1) ^ 1) + 1) for i in range(1, members - 1)]
    same = list(range(members))
    place = [placed(i) for i in range(members)]

    def move(value, pairs, source, target, groups=(0, 1)):
        return lax.ppermute(
            value, EVERY, [(source[a] + g * members, target[b] + g * members) for g in groups for a, b in pairs]
        )

    def trade(a, b, groups=(0, 1), source=place):
        return move(a, near_pairs, source, place, groups), move(b, far_pairs, source, place, groups)

    row8, table8 = ((8, width), F32), ((8, half), F32)
    wide = ((channels, half), BF16)
    by_site = ((channels, width), BF16)
    ints = jnp.int32
    itself = [(i, i) for i in range(members)]
    pack, mine, lent_a, lent_b = call(
        rows_kernel, [((slot_count + 16, width), F32), ((2, 4, half), F32), table8, table8],
        (), (positions, charges[None], polar[None], neighbours.T, send_rows, blocks),
        [pltpu.VMEM((3, width), F32), pltpu.VMEM((1, width), F32), pltpu.VMEM((1, width), F32),
         pltpu.VMEM((slot_count, width), ints), pltpu.VMEM((2, half), ints), pltpu.SMEM((listed,), ints)], 6,
    )
    partner = lax.ppermute(mine, "grp", [(0, 1), (1, 0)])
    features = move(features, itself, same, place, (0,))
    copies = jnp.broadcast_to(partner[None], (members,) + partner.shape)
    copies, features = lax.optimization_barrier((copies, features))
    near = lax.all_to_all(copies, DOM, 0, 0, tiled=True).reshape(2 * members, 4, half)
    pack = move(pack, itself, same, place)
    rim_a, rim_b = trade(lent_a, lent_b, source=same)
    feat_t, w3, w5, fixed, entry, lent_a, lent_b = call(
        static_kernel, [by_site, ((depth, width), F32), ((depth, width), F32), row8, ((depth, 8), F32), wide, wide],
        (pack, rim_a, rim_b), (features,), [pltpu.VMEM((width, channels), BF16)], 1, loose=1,
    )
    side_a, side_b = trade(lent_a, lent_b)
    third_shape = (LAYERS * radial_in.shape[2], slot_count * width)
    (third,) = call(
        radial_kernel, [(third_shape, BF16)], (pack, rim_a, rim_b), (radial_in, radial_mid),
        [pltpu.VMEM(radial_in.shape, BF16), pltpu.VMEM(radial_mid.shape, BF16), pltpu.VMEM(third_shape, BF16)],
        2 + slot_count // RADIAL_SLOTS, 1,
    )
    moment = pltpu.VMEM((depth, 8), F32)
    total = pltpu.VMEM((channels, width), F32)
    square = pltpu.VMEM(node_out.shape[1:], BF16)
    last = pltpu.VMEM(radial_out.shape[1:], BF16)
    outside_row, near_own, hidden, lifted, fixed_all, dipole, lent_a, lent_b = call(
        first_kernel, [row8, ((listed, 4, half), F32), by_site, by_site, row8, row8, wide, wide],
        (pack, rim_a, rim_b, feat_t, side_a, side_b, w3, w5, fixed, entry),
        (near, third, node_in, node_out, radial_out, field_gain[None]),
        [pltpu.VMEM((3 * listed, 4, half), F32), pltpu.VMEM((3 * listed * half, 8), F32),
         pltpu.VMEM(third_shape, BF16), pltpu.VMEM(node_in.shape, BF16), square, last,
         pltpu.VMEM((1, channels), F32), total, moment, square, square,
         pltpu.VMEM((channels, radial_out.shape[1]), BF16), square, pltpu.VMEM((channels, 8), F32)],
        5 + 3 * listed, loose=1,
    )
    side_a, side_b = trade(lent_a, lent_b)
    charge, dipole, small_a, small_b = call(
        second_kernel, [row8, row8, table8, table8],
        (hidden, lifted, side_a, side_b, pack, w3, w5, fixed_all, dipole, entry),
        (third, node_out, radial_out, readout.T),
        [pltpu.VMEM(third_shape, BF16), square, last, pltpu.VMEM((2, channels), BF16), total, moment], 4,
    )
    side_a, side_b = trade(small_a, small_b, (1,))
    dipole, small_a, small_b = call(
        third_kernel, [row8, table8, table8], (side_a, side_b, pack, w3, w5, fixed_all, dipole, entry),
        (), [moment],
    )
    side_a, side_b = trade(small_a, small_b, (1,))
    result, spread = call(
        response_kernel, [((3, width), F32), ((3 * members, 2, half), F32)],
        (near_own, pack, charge, outside_row, side_a, side_b, w3, w5, fixed_all, dipole, entry), (),
        [pltpu.VMEM((width, 8), F32), moment, pltpu.VMEM((listed, 4, half), F32)],
    )
    pieces = lax.all_to_all(spread, DOM, 0, 0, tiled=True).reshape(members, 3, 2, half)
    (share,) = call(gather_kernel, [((3, width), F32)], (pieces,))
    result = move(result, itself, place, same)
    share = lax.ppermute(share, "grp", [(0, 1), (1, 0)])
    whole = ((3, width), F32)
    return tuple(call(finish_kernel, [whole, whole], (result, share), copies=2, far_outs=2))


def solution(mesh):
    sites = P(None, EVERY)
    in_specs = (sites, P(EVERY), P(EVERY), P(EVERY, None), P(EVERY, None), sites, P(EVERY)) + (P(),) * 7
    return jax.shard_map(local, mesh=mesh, in_specs=in_specs, out_specs=(sites, sites), check_vma=False)
```

```python
import jax
import jax.numpy as jnp
from jax import lax
from jax.experimental import pallas as pl
from jax.experimental.pallas import tpu as pltpu
from jax.sharding import PartitionSpec as P

BASIS = 8
LAYERS = 2
SMOOTH = 1.0
SPACING = 0.75
DOM = ("dom", "sub")
EVERY = ("grp", "dom", "sub")
F32 = jnp.float32
BF16 = jnp.bfloat16
VMEM = pl.BlockSpec(memory_space=pltpu.VMEM)
ANY = pl.BlockSpec(memory_space=pl.ANY)
SWEEP_CHUNK, SWEEP_UNROLL = 32, 4
FIELD_CHUNK, FIELD_UNROLL = 32, 4
TERM_CHUNK, TERM_UNROLL = 64, 4
STATIC_CHUNK = 32
RADIAL_SLOTS = 8
MESSAGE_SLOTS = 8


def call(body, outs, held, far=(), scratch=(), copies=0, far_outs=0, loose=0):
    return pl.pallas_call(
        body,
        out_shape=[jax.ShapeDtypeStruct(s, d) for s, d in outs[: len(outs) - far_outs]]
        + [pltpu.HBM(s, d) for s, d in outs[len(outs) - far_outs :]],
        in_specs=[VMEM] * len(held) + [ANY] * len(far),
        out_specs=[VMEM] * (len(outs) - far_outs) + [ANY] * far_outs,
        scratch_shapes=list(scratch) + ([pltpu.SemaphoreType.DMA((copies,))] if copies else []),
        compiler_params=pltpu.CompilerParams(vmem_limit_bytes=24 * 2**20),
    )(*held, *far[:loose], *[pltpu.with_memory_space_constraint(a, pltpu.HBM) for a in far[loose:]])


def fetch(pairs, done, first=0):
    copies = [pltpu.make_async_copy(a, b, done.at[first + i]) for i, (a, b) in enumerate(pairs)]
    for c in copies:
        c.start()

    def wait():
        for c in copies:
            c.wait()

    return wait


def learned():
    return lax.axis_index("grp") == 0


def dot(a, b):
    return jnp.dot(a, b, preferred_element_type=F32)


def silu(x):
    half = 0.5 * x
    return half + half * jnp.tanh(half)


def flip(x):
    return x.astype(F32).T


def split3(x):
    high = x.astype(BF16)
    rest = x - high.astype(F32)
    mid = rest.astype(BF16)
    low = (rest - mid.astype(F32)).astype(BF16)
    return jnp.concatenate([high, mid, low], axis=0)


def join3(x):
    return x[0:8] + x[8:16] + x[16:24]


def one_hot(row, depth):
    ids = lax.broadcasted_iota(jnp.int32, (depth, row.shape[1]), 0)
    return jnp.where(ids == row.astype(jnp.int32), 1.0, 0.0).astype(BF16)


def views(pack):
    return pack.at[0:8, :], pack.at[8:40, :], pack.at[40:41, :]


def picked_row(picks, row):
    return picks[0:1, row * 128 : row * 128 + 128]


def listed_block(row, l):
    lane = lax.broadcasted_iota(jnp.int32, row.shape, 1)
    return jnp.sum(jnp.where(lane == l, row, 0.0)).astype(jnp.int32)


def slot_row(slots, first, count):
    return jnp.concatenate([slots[pl.ds(first + i, 1), :] for i in range(count)], axis=1)


def rows(parts, count=8):
    have = sum(p.shape[0] for p in parts)
    return jnp.concatenate(list(parts) + [jnp.zeros((count - have, parts[0].shape[1]), F32)], axis=0)


def rows_kernel(
    pos_far, charge_far, polar_far, table_far, send_far, blocks_far,
    pack, mine, lent_a, lent_b,
    pos, charge, polar, table, send, blocks, done,
):
    pairs = ((pos_far, pos), (charge_far, charge), (polar_far, polar), (table_far, table), (send_far, send))
    wait = fetch(pairs + ((blocks_far, blocks),), done)
    odd = lax.axis_index("sub")
    width = pos.shape[1]
    wait()
    lane = lax.broadcasted_iota(jnp.int32, (1, width), 1)
    listed = jnp.zeros((1, width), jnp.int32)
    for l in range(blocks.shape[0]):
        listed = jnp.where(lane == l, blocks[l], listed)
    listed = listed.astype(F32)
    sites = rows([pos[...], charge[...], polar[...], listed, jnp.ones((1, width), F32)])
    for half in range(2):
        mine[half] = sites[0:4, half * 128 : half * 128 + 128]
    first, second = send[0:1, :], send[1:2, :]
    swap = jnp.full(first.shape, odd, jnp.int32) == 1
    picks = jnp.where(swap, second, first), jnp.where(swap, first, second)
    raw = table[...]
    other = jnp.where((raw >= 256) & (raw < 512), jnp.bitwise_xor(raw, 128), raw)
    keep = jnp.full(raw.shape, odd, jnp.int32) == 1
    pack[0:8, :] = sites
    pack[8:40, :] = jnp.where(keep, raw, other).astype(F32)
    pack[40:48, :] = rows([jnp.concatenate(picks, axis=1).astype(F32)])
    pieces = split3(sites)
    for row, out in zip(picks, (lent_a, lent_b)):
        found = join3(dot(pieces, one_hot(row, width)))
        out[...] = rows([found[0:5], listed[:, 0:128], jnp.ones((1, 128), F32)])


def static_kernel(
    pack, rim_a, rim_b, features_far,
    feat_t, w3, w5, fixed, entry, lent_a, lent_b, features, done,
):
    site, slots, picks = views(pack)
    width = site.shape[1]
    depth = 2 * width
    slot_count = slots.shape[0]

    @pl.when(learned())
    def _():
        fetch(((features_far, features),), done)()
        flipped = flip(features[...]).astype(BF16)
        feat_t[...] = flipped
        lend_channels(flipped, picks, lent_a, lent_b)

    @pl.when(jnp.logical_not(learned()))
    def _():
        table = jnp.concatenate([site[...], rim_a[...], rim_b[...]], axis=1)
        entry[...] = table.T
        tx, ty, tz = site[0:1, :], site[1:2, :], site[2:3, :]

        def some_rows(j, acc):
            start = pl.multiple_of(j * STATIC_CHUNK, STATIC_CHUNK)
            ids = (lax.broadcasted_iota(jnp.int32, (STATIC_CHUNK, width), 0) + start).astype(F32)
            count = jnp.zeros((STATIC_CHUNK, width), F32)
            for k in range(slot_count):
                count = count + jnp.where(ids == slots[k : k + 1, :], 1.0, 0.0)
            cols = entry[pl.ds(start, STATIC_CHUNK), :]
            rx, ry, rz = tx - cols[:, 0:1], ty - cols[:, 1:2], tz - cols[:, 2:3]
            inverse = lax.rsqrt(rx * rx + ry * ry + rz * rz + SMOOTH)
            squared = inverse * inverse
            cube = count * (squared * inverse)
            w3[pl.ds(start, STATIC_CHUNK), :] = cube
            w5[pl.ds(start, STATIC_CHUNK), :] = 3.0 * (cube * squared)
            scale = cols[:, 3:4] * cube
            return acc[0] + rx * scale, acc[1] + ry * scale, acc[2] + rz * scale

        nil = jnp.zeros((STATIC_CHUNK, width), F32)
        sums = lax.fori_loop(0, depth // STATIC_CHUNK, some_rows, (nil, nil, nil))
        total = rows([jnp.sum(s, axis=0, keepdims=True) for s in sums])
        fixed[...] = total
        lend_pieces(total, picks, lent_a, lent_b)


def radial_kernel(
    pack, rim_a, rim_b, w_in_far, w_mid_far,
    third_far, w_in, w_mid, third, done,
):
    site, slots, _ = views(pack)
    width = site.shape[1]
    depth = 2 * width
    slot_count = slots.shape[0]

    @pl.when(learned())
    def _():
        wait = fetch(((w_in_far, w_in), (w_mid_far, w_mid)), done)
        pieces = split3(jnp.concatenate([site[...], rim_a[...], rim_b[...]], axis=1))
        step = RADIAL_SLOTS * width
        here = jnp.concatenate([site[...]] * RADIAL_SLOTS, axis=1)
        centres = lax.broadcasted_iota(jnp.int32, (BASIS, step), 0).astype(F32) * SPACING
        wait()
        first_w = jnp.concatenate([flip(w_in[0]), flip(w_in[1])], axis=0).astype(BF16)
        zero = jnp.zeros((64, 64), F32)

        def both(level):
            top = jnp.concatenate([flip(w_mid[0, level]), zero], axis=1)
            bottom = jnp.concatenate([zero, flip(w_mid[1, level])], axis=1)
            return jnp.concatenate([top, bottom], axis=0).astype(BF16)

        second_w, third_w = both(0), both(1)

        def part_out(k):
            part = pl.ds(pl.multiple_of(k * step, step), step)
            return pltpu.make_async_copy(third.at[:, part], third_far.at[:, part], done.at[2 + k])

        def some_slots(k, carry):
            found = join3(dot(pieces, one_hot(slot_row(slots, k * RADIAL_SLOTS, RADIAL_SLOTS), depth)))
            offset = here - found
            squares = offset * offset
            dist_sq = squares[0:1] + squares[1:2] + squares[2:3] + SMOOTH
            gap = jnp.sqrt(dist_sq) - centres
            basis = jnp.exp(-(gap * gap)).astype(BF16)
            hidden = silu(dot(first_w, basis)).astype(BF16)
            hidden = silu(dot(second_w, hidden)).astype(BF16)
            start = pl.multiple_of(k * step, step)
            third[:, pl.ds(start, step)] = silu(dot(third_w, hidden)).astype(BF16)
            part_out(k).start()
            return carry

        lax.fori_loop(0, slot_count // RADIAL_SLOTS, some_slots, 0)
        for k in range(slot_count // RADIAL_SLOTS):
            part_out(k).wait()


def lend_pieces(values, picks, lent_a, lent_b):
    pieces = split3(values)
    for row, out in ((0, lent_a), (1, lent_b)):
        found = dot(pieces, one_hot(picked_row(picks, row), values.shape[1]))
        out[...] = jnp.zeros_like(out)
        out[0:32, :] = rows([found], 32).astype(BF16)


def lend_whole(values, picks, lent_a, lent_b):
    pieces = split3(values)
    for row, out in ((0, lent_a), (1, lent_b)):
        out[...] = join3(dot(pieces, one_hot(picked_row(picks, row), values.shape[1])))


def lend_channels(values, picks, lent_a, lent_b):
    for row, out in ((0, lent_a), (1, lent_b)):
        out[...] = dot(values, one_hot(picked_row(picks, row), values.shape[1])).astype(BF16)


def sweep(site, w3, w5, fixed, dipoles, entry, moment):
    width = site.shape[1]
    moment[...] = dipoles.T
    tx, ty, tz = site[0:1, :], site[1:2, :], site[2:3, :]

    def some_rows(j, acc):
        start = pl.multiple_of(j * SWEEP_CHUNK, SWEEP_CHUNK)
        cols, d = entry[pl.ds(start, SWEEP_CHUNK), :], moment[pl.ds(start, SWEEP_CHUNK), :]
        rx, ry, rz = tx - cols[:, 0:1], ty - cols[:, 1:2], tz - cols[:, 2:3]
        dx, dy, dz = d[:, 0:1], d[:, 1:2], d[:, 2:3]
        cube = w3[pl.ds(start, SWEEP_CHUNK), :]
        scale = (rx * dx + ry * dy + rz * dz) * w5[pl.ds(start, SWEEP_CHUNK), :]
        return (
            acc[0] + (rx * scale - dx * cube),
            acc[1] + (ry * scale - dy * cube),
            acc[2] + (rz * scale - dz * cube),
        )

    nil = jnp.zeros((SWEEP_CHUNK, width), F32)
    sums = lax.fori_loop(0, w3.shape[0] // SWEEP_CHUNK, some_rows, (nil, nil, nil), unroll=SWEEP_UNROLL)
    return site[4:5, :] * (fixed + rows([jnp.sum(s, axis=0, keepdims=True) for s in sums]))


def message(layer, hidden, table, third, out_t, node_t, slots, total):
    slot_count = slots.shape[0]
    width = slots.shape[1]
    step = MESSAGE_SLOTS * width
    total[...] = jnp.zeros_like(total)

    def some_slots(k, carry):
        row = slot_row(slots, k * MESSAGE_SLOTS, MESSAGE_SLOTS)
        picked = dot(table, one_hot(row, table.shape[1]))
        start = pl.multiple_of(k * step, step)
        weight = dot(out_t, third[layer * 64 : layer * 64 + 64, pl.ds(start, step)])
        product = weight * picked
        part = product[:, 0:width]
        for i in range(1, MESSAGE_SLOTS):
            part = part + product[:, i * width : (i + 1) * width]
        total[...] += part
        return carry

    lax.fori_loop(0, slot_count // MESSAGE_SLOTS, some_slots, 0)
    mean = (total[...] * (1.0 / slot_count)).astype(BF16)
    return (hidden.astype(F32) + silu(dot(node_t, mean))).astype(BF16)


def charge_field(target, cols, first, count):
    tx, ty, tz = target[0:1, :], target[1:2, :], target[2:3, :]

    def some_rows(j, acc):
        c = cols[pl.ds(pl.multiple_of(first + j * FIELD_CHUNK, FIELD_CHUNK), FIELD_CHUNK), :]
        rx, ry, rz = tx - c[:, 0:1], ty - c[:, 1:2], tz - c[:, 2:3]
        inverse = lax.rsqrt(rx * rx + ry * ry + rz * rz + SMOOTH)
        scale = c[:, 3:4] * (inverse * inverse * inverse)
        return acc[0] + rx * scale, acc[1] + ry * scale, acc[2] + rz * scale

    nil = jnp.zeros((FIELD_CHUNK, target.shape[1]), F32)
    sums = lax.fori_loop(0, count // FIELD_CHUNK, some_rows, (nil, nil, nil), unroll=FIELD_UNROLL)
    return jnp.concatenate([jnp.sum(s, axis=0, keepdims=True) for s in sums], axis=0)


def first_kernel(
    pack, rim_a, rim_b, feat_t, side_a, side_b, w3, w5, fixed, entry,
    near_far, third_far, node_in_far, node_out_far, w_out_far, gain_far,
    outside_row, near_own, hidden_out, lifted_out, fixed_out, dipole_out, lent_a, lent_b,
    near, cols, third, node_in, node_out, w_out, gain, total, moment,
    in_first, in_second, out_t, node_t, gain_col, done,
):
    site, slots, picks = views(pack)
    width = site.shape[1]
    listed = near_own.shape[0]
    weights = (
        (node_in_far, node_in), (node_out_far.at[0], node_out), (w_out_far.at[0], w_out), (gain_far, gain),
        (third_far, third),
    )

    @pl.when(learned())
    def _():
        fetch(weights, done)

    numbers = [listed_block(row[5:6, 0:128], l) for row in (site, rim_a, rim_b) for l in range(listed)]
    fetch([(near_far.at[b], near.at[i]) for i, b in enumerate(numbers)], done, 5)

    @pl.when(learned())
    def _():
        for i, (source, target) in enumerate(weights[:4]):
            pltpu.make_async_copy(source, target, done.at[i]).wait()
        in_first[...] = flip(node_in[0]).astype(BF16)
        in_second[...] = flip(node_in[1]).astype(BF16)
        out_t[...] = flip(w_out[...]).astype(BF16)
        node_t[...] = flip(node_out[...]).astype(BF16)
        gain_col[...] = jnp.broadcast_to(gain[...], (8, width)).T

    for i, b in enumerate(numbers):
        pltpu.make_async_copy(near_far.at[b], near.at[i], done.at[5 + i]).wait()
    near_own[...] = near[0:listed]
    for i in range(3 * listed):
        tile = near[i]
        cols[i * 128 : i * 128 + 128, :] = jnp.concatenate([tile, tile], axis=0).T
    reach = listed * 128
    own_field = charge_field(site[...], cols, 0, reach)
    field = jnp.concatenate(
        [own_field, charge_field(rim_a[...], cols, reach, reach), charge_field(rim_b[...], cols, 2 * reach, reach)],
        axis=1,
    )
    strength = jnp.sqrt(1.0 + (field[0:1] * field[0:1] + field[1:2] * field[1:2] + field[2:3] * field[2:3]))
    outside_row[...] = jnp.broadcast_to(strength[:, :width], outside_row.shape)

    @pl.when(learned())
    def _():
        features = jnp.concatenate([feat_t[...], side_a[...], side_b[...]], axis=1)
        start = (features.astype(F32) + gain_col[:, 0:1] * strength).astype(BF16)
        present = jnp.concatenate([jnp.ones((1, width), F32), rim_a[6:7, :], rim_b[6:7, :]], axis=1)
        raised = dot(in_first[...], start)
        table = jnp.where(present > 0.5, raised, 0.0).astype(BF16)
        pltpu.make_async_copy(third_far, third, done.at[4]).wait()
        new = message(0, start[:, :width], table, third, out_t[...], node_t[...], slots, total)
        hidden_out[...] = new
        raised = dot(in_second[...], new).astype(BF16)
        lifted_out[...] = raised
        lend_channels(raised, picks, lent_a, lent_b)

    @pl.when(jnp.logical_not(learned()))
    def _():
        known = [fixed[...], join3(side_a[0:24, :].astype(F32)), join3(side_b[0:24, :].astype(F32))]
        whole = jnp.concatenate(known, axis=1) + rows([field])
        fixed_out[...] = whole[:, :width]
        polar = jnp.concatenate([site[4:5, :], rim_a[4:5, :], rim_b[4:5, :]], axis=1)
        new = sweep(site, w3, w5, whole[:, :width], polar * whole, entry, moment)
        dipole_out[...] = new
        lend_pieces(new, picks, lent_a, lent_b)


def second_kernel(
    hidden, lifted, side_a, side_b, pack, w3, w5, fixed, dipole, entry,
    third_far, node_out_far, w_out_far, readout_far,
    charge, dipole_out, small_a, small_b,
    third, node_out, w_out, readout, total, moment, done,
):
    site, slots, picks = views(pack)

    @pl.when(learned())
    def _():
        fetch(
            ((third_far, third), (node_out_far.at[1], node_out), (w_out_far.at[1], w_out), (readout_far, readout)), done
        )()
        table = jnp.concatenate([lifted[...], side_a[...], side_b[...]], axis=1)
        out_t, node_t = flip(w_out[...]).astype(BF16), flip(node_out[...]).astype(BF16)
        new = message(1, hidden[...], table, third, out_t, node_t, slots, total)
        charge[...] = dot(rows([readout[...].astype(F32)]).astype(BF16), new)

    @pl.when(jnp.logical_not(learned()))
    def _():
        sides = [join3(side_a[0:24, :].astype(F32)), join3(side_b[0:24, :].astype(F32))]
        table = jnp.concatenate([dipole[...]] + sides, axis=1)
        new = sweep(site, w3, w5, fixed[...], table, entry, moment)
        dipole_out[...] = new
        lend_whole(new, picks, small_a, small_b)


def third_kernel(side_a, side_b, pack, w3, w5, fixed, dipole, entry, dipole_out, small_a, small_b, moment):
    site, _, picks = views(pack)

    @pl.when(jnp.logical_not(learned()))
    def _():
        table = jnp.concatenate([dipole[...], side_a[...], side_b[...]], axis=1)
        new = sweep(site, w3, w5, fixed[...], table, entry, moment)
        dipole_out[...] = new
        lend_whole(new, picks, small_a, small_b)


def response_kernel(
    near, pack, charge, outside_row, side_a, side_b, w3, w5, fixed, dipole, entry,
    result, spread, cols, moment, term,
):
    site = views(pack)[0]
    width = site.shape[1]
    listed = near.shape[0]
    blocks = [listed_block(site[5:6, 0:128], l) for l in range(listed)]
    spread[...] = jnp.zeros_like(spread)
    term[...] = jnp.zeros_like(term)

    def terms(dipoles):
        for l in range(listed):
            tile = near[l]
            tx, ty, tz = tile[0:1, :], tile[1:2, :], tile[2:3, :]

            def some_rows(j, acc):
                start = pl.multiple_of(j * TERM_CHUNK, TERM_CHUNK)
                c = cols[pl.ds(start, TERM_CHUNK), :]
                rx, ry, rz = tx - c[:, 0:1], ty - c[:, 1:2], tz - c[:, 2:3]
                inverse = lax.rsqrt(rx * rx + ry * ry + rz * rz + SMOOTH)
                squared = inverse * inverse
                cube = squared * inverse
                if dipoles:
                    dx, dy, dz = c[:, 4:5], c[:, 5:6], c[:, 6:7]
                    scale = (rx * dx + ry * dy + rz * dz) * (3.0 * (cube * squared))
                    return (
                        acc[0] + (rx * scale - dx * cube),
                        acc[1] + (ry * scale - dy * cube),
                        acc[2] + (rz * scale - dz * cube),
                    )
                scale = c[:, 3:4] * cube
                return acc[0] + rx * scale, acc[1] + ry * scale, acc[2] + rz * scale

            nil = jnp.zeros((TERM_CHUNK, 128), F32)
            sums = lax.fori_loop(0, width // TERM_CHUNK, some_rows, (nil, nil, nil), unroll=TERM_UNROLL)
            for axis in range(3):
                term[l, axis : axis + 1, :] = jnp.sum(sums[axis], axis=0, keepdims=True)

    @pl.when(learned())
    def _():
        q = charge[...]
        result[...] = jnp.concatenate([q[0:2], outside_row[0:1, :]], axis=0)
        cols[...] = rows([site[0:3, :], q[0:1]]).T
        terms(False)

    @pl.when(jnp.logical_not(learned()))
    def _():
        table = jnp.concatenate([dipole[...], side_a[...], side_b[...]], axis=1)
        new = sweep(site, w3, w5, fixed[...], table, entry, moment)
        result[...] = new[0:3]
        cols[...] = rows([site[0:4, :], new[0:3]]).T
        terms(True)

    side = lax.broadcasted_iota(jnp.int32, (2, 128), 0)
    for l in range(listed):
        owner, part = blocks[l] >> 1, blocks[l] & 1
        for axis in range(3):
            spread[3 * owner + axis] += jnp.where(side == part, term[l, axis : axis + 1, :], 0.0)


def gather_kernel(pieces, share):
    total = jnp.sum(pieces[...], axis=0)
    share[...] = jnp.concatenate(
        [jnp.concatenate([total[axis, 0:1], total[axis, 1:2]], axis=1) for axis in range(3)], axis=0
    )


def finish_kernel(result, share, result_far, share_far, done):
    fetch(((result, result_far), (share, share_far)), done)()


def placed(block):
    y_half, plane, step, side = block // 64, block // 8 % 8, block // 2 % 4, block % 2
    x = 3 - step if plane % 2 else step
    z = (plane - 1) % 8 if y_half else plane
    along = 1 - side if (step + y_half) % 2 == 0 else side
    y = 2 * y_half + along
    return ((y % 2 * 8 + z) * 4 + x) * 2 + y // 2


def local(
    positions, charges, polar, features, neighbours, send_rows, blocks,
    radial_in, radial_mid, radial_out, node_in, node_out, field_gain, readout,
):
    width = positions.shape[1]
    slot_count = neighbours.shape[1]
    depth = 2 * width
    half = send_rows.shape[1]
    channels = features.shape[1]
    listed = blocks.shape[0]
    members = lax.axis_size(DOM)
    near_pairs = [(i, i ^ 1) for i in range(members)]
    far_pairs = [(i, ((i - 1) ^ 1) + 1) for i in range(1, members - 1)]
    same = list(range(members))
    place = [placed(i) for i in range(members)]

    def move(value, pairs, source, target, groups=(0, 1)):
        return lax.ppermute(
            value, EVERY, [(source[a] + g * members, target[b] + g * members) for g in groups for a, b in pairs]
        )

    def trade(a, b, groups=(0, 1), source=place):
        return move(a, near_pairs, source, place, groups), move(b, far_pairs, source, place, groups)

    row8, table8 = ((8, width), F32), ((8, half), F32)
    wide = ((channels, half), BF16)
    by_site = ((channels, width), BF16)
    ints = jnp.int32
    itself = [(i, i) for i in range(members)]
    pack, mine, lent_a, lent_b = call(
        rows_kernel, [((slot_count + 16, width), F32), ((2, 4, half), F32), table8, table8],
        (), (positions, charges[None], polar[None], neighbours.T, send_rows, blocks),
        [pltpu.VMEM((3, width), F32), pltpu.VMEM((1, width), F32), pltpu.VMEM((1, width), F32),
         pltpu.VMEM((slot_count, width), ints), pltpu.VMEM((2, half), ints), pltpu.SMEM((listed,), ints)], 6,
    )
    partner = lax.ppermute(mine, "grp", [(0, 1), (1, 0)])
    copies = jnp.broadcast_to(partner[None], (members,) + partner.shape)
    near = lax.all_to_all(copies, DOM, 0, 0, tiled=True).reshape(2 * members, 4, half)
    pack = move(pack, itself, same, place)
    rim_a, rim_b = trade(lent_a, lent_b, source=same)
    features, pack, rim_a, rim_b = lax.optimization_barrier((features, pack, rim_a, rim_b))
    features = move(features, itself, same, place, (0,))
    feat_t, w3, w5, fixed, entry, lent_a, lent_b = call(
        static_kernel, [by_site, ((depth, width), F32), ((depth, width), F32), row8, ((depth, 8), F32), wide, wide],
        (pack, rim_a, rim_b), (features,), [pltpu.VMEM((width, channels), BF16)], 1, loose=1,
    )
    side_a, side_b = trade(lent_a, lent_b)
    third_shape = (LAYERS * radial_in.shape[2], slot_count * width)
    (third,) = call(
        radial_kernel, [(third_shape, BF16)], (pack, rim_a, rim_b), (radial_in, radial_mid),
        [pltpu.VMEM(radial_in.shape, BF16), pltpu.VMEM(radial_mid.shape, BF16), pltpu.VMEM(third_shape, BF16)],
        2 + slot_count // RADIAL_SLOTS, 1,
    )
    moment = pltpu.VMEM((depth, 8), F32)
    total = pltpu.VMEM((channels, width), F32)
    square = pltpu.VMEM(node_out.shape[1:], BF16)
    last = pltpu.VMEM(radial_out.shape[1:], BF16)
    outside_row, near_own, hidden, lifted, fixed_all, dipole, lent_a, lent_b = call(
        first_kernel, [row8, ((listed, 4, half), F32), by_site, by_site, row8, row8, wide, wide],
        (pack, rim_a, rim_b, feat_t, side_a, side_b, w3, w5, fixed, entry),
        (near, third, node_in, node_out, radial_out, field_gain[None]),
        [pltpu.VMEM((3 * listed, 4, half), F32), pltpu.VMEM((3 * listed * half, 8), F32),
         pltpu.VMEM(third_shape, BF16), pltpu.VMEM(node_in.shape, BF16), square, last,
         pltpu.VMEM((1, channels), F32), total, moment, square, square,
         pltpu.VMEM((channels, radial_out.shape[1]), BF16), square, pltpu.VMEM((channels, 8), F32)],
        5 + 3 * listed, loose=1,
    )
    side_a, side_b = trade(lent_a, lent_b)
    charge, dipole, small_a, small_b = call(
        second_kernel, [row8, row8, table8, table8],
        (hidden, lifted, side_a, side_b, pack, w3, w5, fixed_all, dipole, entry),
        (third, node_out, radial_out, readout.T),
        [pltpu.VMEM(third_shape, BF16), square, last, pltpu.VMEM((2, channels), BF16), total, moment], 4,
    )
    side_a, side_b = trade(small_a, small_b, (1,))
    dipole, small_a, small_b = call(
        third_kernel, [row8, table8, table8], (side_a, side_b, pack, w3, w5, fixed_all, dipole, entry),
        (), [moment],
    )
    side_a, side_b = trade(small_a, small_b, (1,))
    result, spread = call(
        response_kernel, [((3, width), F32), ((3 * members, 2, half), F32)],
        (near_own, pack, charge, outside_row, side_a, side_b, w3, w5, fixed_all, dipole, entry), (),
        [pltpu.VMEM((width, 8), F32), moment, pltpu.VMEM((listed, 4, half), F32)],
    )
    pieces = lax.all_to_all(spread, DOM, 0, 0, tiled=True).reshape(members, 3, 2, half)
    (share,) = call(gather_kernel, [((3, width), F32)], (pieces,))
    result = move(result, itself, place, same)
    share = lax.ppermute(share, "grp", [(0, 1), (1, 0)])
    whole = ((3, width), F32)
    return tuple(call(finish_kernel, [whole, whole], (result, share), copies=2, far_outs=2))


def solution(mesh):
    sites = P(None, EVERY)
    in_specs = (sites, P(EVERY), P(EVERY), P(EVERY, None), P(EVERY, None), sites, P(EVERY)) + (P(),) * 7
    return jax.shard_map(local, mesh=mesh, in_specs=in_specs, out_specs=(sites, sites), check_vma=False)
```

```python
import jax
import jax.numpy as jnp
from jax import lax
from jax.experimental import pallas as pl
from jax.experimental.pallas import tpu as pltpu
from jax.sharding import PartitionSpec as P

BASIS = 8
LAYERS = 2
SMOOTH = 1.0
SPACING = 0.75
DOM = ("dom", "sub")
EVERY = ("grp", "dom", "sub")
F32 = jnp.float32
BF16 = jnp.bfloat16
VMEM = pl.BlockSpec(memory_space=pltpu.VMEM)
ANY = pl.BlockSpec(memory_space=pl.ANY)
SWEEP_CHUNK, SWEEP_UNROLL = 32, 4
FIELD_CHUNK, FIELD_UNROLL = 32, 4
TERM_CHUNK, TERM_UNROLL = 64, 4
STATIC_CHUNK = 32
RADIAL_SLOTS = 8
MESSAGE_SLOTS = 16


def call(body, outs, held, far=(), scratch=(), copies=0, far_outs=0, loose=0):
    return pl.pallas_call(
        body,
        out_shape=[jax.ShapeDtypeStruct(s, d) for s, d in outs[: len(outs) - far_outs]]
        + [pltpu.HBM(s, d) for s, d in outs[len(outs) - far_outs :]],
        in_specs=[VMEM] * len(held) + [ANY] * len(far),
        out_specs=[VMEM] * (len(outs) - far_outs) + [ANY] * far_outs,
        scratch_shapes=list(scratch) + ([pltpu.SemaphoreType.DMA((copies,))] if copies else []),
        compiler_params=pltpu.CompilerParams(vmem_limit_bytes=24 * 2**20),
    )(*held, *far[:loose], *[pltpu.with_memory_space_constraint(a, pltpu.HBM) for a in far[loose:]])


def fetch(pairs, done, first=0):
    copies = [pltpu.make_async_copy(a, b, done.at[first + i]) for i, (a, b) in enumerate(pairs)]
    for c in copies:
        c.start()

    def wait():
        for c in copies:
            c.wait()

    return wait


def learned():
    return lax.axis_index("grp") == 0


def dot(a, b):
    return jnp.dot(a, b, preferred_element_type=F32)


def silu(x):
    half = 0.5 * x
    return half + half * jnp.tanh(half)


def flip(x):
    return x.astype(F32).T


def split3(x):
    high = x.astype(BF16)
    rest = x - high.astype(F32)
    mid = rest.astype(BF16)
    low = (rest - mid.astype(F32)).astype(BF16)
    return jnp.concatenate([high, mid, low], axis=0)


def join3(x):
    return x[0:8] + x[8:16] + x[16:24]


def one_hot(row, depth):
    ids = lax.broadcasted_iota(jnp.int32, (depth, row.shape[1]), 0)
    return jnp.where(ids == row.astype(jnp.int32), 1.0, 0.0).astype(BF16)


def views(pack):
    return pack.at[0:8, :], pack.at[8:40, :], pack.at[40:41, :]


def picked_row(picks, row):
    return picks[0:1, row * 128 : row * 128 + 128]


def listed_block(row, l):
    lane = lax.broadcasted_iota(jnp.int32, row.shape, 1)
    return jnp.sum(jnp.where(lane == l, row, 0.0)).astype(jnp.int32)


def slot_row(slots, first, count):
    return jnp.concatenate([slots[pl.ds(first + i, 1), :] for i in range(count)], axis=1)


def rows(parts, count=8):
    have = sum(p.shape[0] for p in parts)
    return jnp.concatenate(list(parts) + [jnp.zeros((count - have, parts[0].shape[1]), F32)], axis=0)


def rows_kernel(
    pos_far, charge_far, polar_far, table_far, send_far, blocks_far,
    pack, mine, lent_a, lent_b,
    pos, charge, polar, table, send, blocks, done,
):
    pairs = ((pos_far, pos), (charge_far, charge), (polar_far, polar), (table_far, table), (send_far, send))
    wait = fetch(pairs + ((blocks_far, blocks),), done)
    odd = lax.axis_index("sub")
    width = pos.shape[1]
    wait()
    lane = lax.broadcasted_iota(jnp.int32, (1, width), 1)
    listed = jnp.zeros((1, width), jnp.int32)
    for l in range(blocks.shape[0]):
        listed = jnp.where(lane == l, blocks[l], listed)
    listed = listed.astype(F32)
    sites = rows([pos[...], charge[...], polar[...], listed, jnp.ones((1, width), F32)])
    for half in range(2):
        mine[half] = sites[0:4, half * 128 : half * 128 + 128]
    first, second = send[0:1, :], send[1:2, :]
    swap = jnp.full(first.shape, odd, jnp.int32) == 1
    picks = jnp.where(swap, second, first), jnp.where(swap, first, second)
    raw = table[...]
    other = jnp.where((raw >= 256) & (raw < 512), jnp.bitwise_xor(raw, 128), raw)
    keep = jnp.full(raw.shape, odd, jnp.int32) == 1
    pack[0:8, :] = sites
    pack[8:40, :] = jnp.where(keep, raw, other).astype(F32)
    pack[40:48, :] = rows([jnp.concatenate(picks, axis=1).astype(F32)])
    pieces = split3(sites)
    for row, out in zip(picks, (lent_a, lent_b)):
        found = join3(dot(pieces, one_hot(row, width)))
        out[...] = rows([found[0:5], listed[:, 0:128], jnp.ones((1, 128), F32)])


def static_kernel(
    pack, rim_a, rim_b, features_far,
    feat_t, w3, w5, fixed, entry, lent_a, lent_b, features, done,
):
    site, slots, picks = views(pack)
    width = site.shape[1]
    depth = 2 * width
    slot_count = slots.shape[0]

    @pl.when(learned())
    def _():
        fetch(((features_far, features),), done)()
        flipped = flip(features[...]).astype(BF16)
        feat_t[...] = flipped
        lend_channels(flipped, picks, lent_a, lent_b)

    @pl.when(jnp.logical_not(learned()))
    def _():
        table = jnp.concatenate([site[...], rim_a[...], rim_b[...]], axis=1)
        entry[...] = table.T
        tx, ty, tz = site[0:1, :], site[1:2, :], site[2:3, :]

        def some_rows(j, acc):
            start = pl.multiple_of(j * STATIC_CHUNK, STATIC_CHUNK)
            ids = (lax.broadcasted_iota(jnp.int32, (STATIC_CHUNK, width), 0) + start).astype(F32)
            count = jnp.zeros((STATIC_CHUNK, width), F32)
            for k in range(slot_count):
                count = count + jnp.where(ids == slots[k : k + 1, :], 1.0, 0.0)
            cols = entry[pl.ds(start, STATIC_CHUNK), :]
            rx, ry, rz = tx - cols[:, 0:1], ty - cols[:, 1:2], tz - cols[:, 2:3]
            inverse = lax.rsqrt(rx * rx + ry * ry + rz * rz + SMOOTH)
            squared = inverse * inverse
            cube = count * (squared * inverse)
            w3[pl.ds(start, STATIC_CHUNK), :] = cube
            w5[pl.ds(start, STATIC_CHUNK), :] = 3.0 * (cube * squared)
            scale = cols[:, 3:4] * cube
            return acc[0] + rx * scale, acc[1] + ry * scale, acc[2] + rz * scale

        nil = jnp.zeros((STATIC_CHUNK, width), F32)
        sums = lax.fori_loop(0, depth // STATIC_CHUNK, some_rows, (nil, nil, nil))
        total = rows([jnp.sum(s, axis=0, keepdims=True) for s in sums])
        fixed[...] = total
        lend_pieces(total, picks, lent_a, lent_b)


def radial_kernel(
    pack, rim_a, rim_b, w_in_far, w_mid_far,
    third_far, w_in, w_mid, third, done,
):
    site, slots, _ = views(pack)
    width = site.shape[1]
    depth = 2 * width
    slot_count = slots.shape[0]

    @pl.when(learned())
    def _():
        wait = fetch(((w_in_far, w_in), (w_mid_far, w_mid)), done)
        pieces = split3(jnp.concatenate([site[...], rim_a[...], rim_b[...]], axis=1))
        step = RADIAL_SLOTS * width
        here = jnp.concatenate([site[...]] * RADIAL_SLOTS, axis=1)
        centres = lax.broadcasted_iota(jnp.int32, (BASIS, step), 0).astype(F32) * SPACING
        wait()
        first_w = jnp.concatenate([flip(w_in[0]), flip(w_in[1])], axis=0).astype(BF16)
        zero = jnp.zeros((64, 64), F32)

        def both(level):
            top = jnp.concatenate([flip(w_mid[0, level]), zero], axis=1)
            bottom = jnp.concatenate([zero, flip(w_mid[1, level])], axis=1)
            return jnp.concatenate([top, bottom], axis=0).astype(BF16)

        second_w, third_w = both(0), both(1)

        def part_out(k):
            part = pl.ds(pl.multiple_of(k * step, step), step)
            return pltpu.make_async_copy(third.at[:, part], third_far.at[:, part], done.at[2 + k])

        def some_slots(k, carry):
            found = join3(dot(pieces, one_hot(slot_row(slots, k * RADIAL_SLOTS, RADIAL_SLOTS), depth)))
            offset = here - found
            squares = offset * offset
            dist_sq = squares[0:1] + squares[1:2] + squares[2:3] + SMOOTH
            gap = jnp.sqrt(dist_sq) - centres
            basis = jnp.exp(-(gap * gap)).astype(BF16)
            hidden = silu(dot(first_w, basis)).astype(BF16)
            hidden = silu(dot(second_w, hidden)).astype(BF16)
            start = pl.multiple_of(k * step, step)
            third[:, pl.ds(start, step)] = silu(dot(third_w, hidden)).astype(BF16)
            part_out(k).start()
            return carry

        lax.fori_loop(0, slot_count // RADIAL_SLOTS, some_slots, 0)
        for k in range(slot_count // RADIAL_SLOTS):
            part_out(k).wait()


def lend_pieces(values, picks, lent_a, lent_b):
    pieces = split3(values)
    for row, out in ((0, lent_a), (1, lent_b)):
        found = dot(pieces, one_hot(picked_row(picks, row), values.shape[1]))
        out[...] = jnp.zeros_like(out)
        out[0:32, :] = rows([found], 32).astype(BF16)


def lend_whole(values, picks, lent_a, lent_b):
    pieces = split3(values)
    for row, out in ((0, lent_a), (1, lent_b)):
        out[...] = join3(dot(pieces, one_hot(picked_row(picks, row), values.shape[1])))


def lend_channels(values, picks, lent_a, lent_b):
    for row, out in ((0, lent_a), (1, lent_b)):
        out[...] = dot(values, one_hot(picked_row(picks, row), values.shape[1])).astype(BF16)


def sweep(site, w3, w5, fixed, dipoles, entry, moment):
    width = site.shape[1]
    moment[...] = dipoles.T
    tx, ty, tz = site[0:1, :], site[1:2, :], site[2:3, :]

    def some_rows(j, acc):
        start = pl.multiple_of(j * SWEEP_CHUNK, SWEEP_CHUNK)
        cols, d = entry[pl.ds(start, SWEEP_CHUNK), :], moment[pl.ds(start, SWEEP_CHUNK), :]
        rx, ry, rz = tx - cols[:, 0:1], ty - cols[:, 1:2], tz - cols[:, 2:3]
        dx, dy, dz = d[:, 0:1], d[:, 1:2], d[:, 2:3]
        cube = w3[pl.ds(start, SWEEP_CHUNK), :]
        scale = (rx * dx + ry * dy + rz * dz) * w5[pl.ds(start, SWEEP_CHUNK), :]
        return (
            acc[0] + (rx * scale - dx * cube),
            acc[1] + (ry * scale - dy * cube),
            acc[2] + (rz * scale - dz * cube),
        )

    nil = jnp.zeros((SWEEP_CHUNK, width), F32)
    sums = lax.fori_loop(0, w3.shape[0] // SWEEP_CHUNK, some_rows, (nil, nil, nil), unroll=SWEEP_UNROLL)
    return site[4:5, :] * (fixed + rows([jnp.sum(s, axis=0, keepdims=True) for s in sums]))


def message(layer, hidden, table, third, out_t, node_t, slots, total):
    slot_count = slots.shape[0]
    width = slots.shape[1]
    step = MESSAGE_SLOTS * width
    total[...] = jnp.zeros_like(total)

    def some_slots(k, carry):
        row = slot_row(slots, k * MESSAGE_SLOTS, MESSAGE_SLOTS)
        picked = dot(table, one_hot(row, table.shape[1]))
        start = pl.multiple_of(k * step, step)
        weight = dot(out_t, third[layer * 64 : layer * 64 + 64, pl.ds(start, step)])
        product = weight * picked
        part = product[:, 0:width]
        for i in range(1, MESSAGE_SLOTS):
            part = part + product[:, i * width : (i + 1) * width]
        total[...] += part
        return carry

    lax.fori_loop(0, slot_count // MESSAGE_SLOTS, some_slots, 0)
    mean = (total[...] * (1.0 / slot_count)).astype(BF16)
    return (hidden.astype(F32) + silu(dot(node_t, mean))).astype(BF16)


def charge_field(target, cols, first, count):
    tx, ty, tz = target[0:1, :], target[1:2, :], target[2:3, :]

    def some_rows(j, acc):
        c = cols[pl.ds(pl.multiple_of(first + j * FIELD_CHUNK, FIELD_CHUNK), FIELD_CHUNK), :]
        rx, ry, rz = tx - c[:, 0:1], ty - c[:, 1:2], tz - c[:, 2:3]
        inverse = lax.rsqrt(rx * rx + ry * ry + rz * rz + SMOOTH)
        scale = c[:, 3:4] * (inverse * inverse * inverse)
        return acc[0] + rx * scale, acc[1] + ry * scale, acc[2] + rz * scale

    nil = jnp.zeros((FIELD_CHUNK, target.shape[1]), F32)
    sums = lax.fori_loop(0, count // FIELD_CHUNK, some_rows, (nil, nil, nil), unroll=FIELD_UNROLL)
    return jnp.concatenate([jnp.sum(s, axis=0, keepdims=True) for s in sums], axis=0)


def first_kernel(
    pack, rim_a, rim_b, feat_t, side_a, side_b, w3, w5, fixed, entry,
    near_far, third_far, node_in_far, node_out_far, w_out_far, gain_far,
    outside_row, near_own, hidden_out, lifted_out, fixed_out, dipole_out, lent_a, lent_b,
    near, cols, third, node_in, node_out, w_out, gain, total, moment,
    in_first, in_second, out_t, node_t, gain_col, done,
):
    site, slots, picks = views(pack)
    width = site.shape[1]
    listed = near_own.shape[0]
    weights = (
        (third_far, third),
        (node_in_far, node_in), (node_out_far.at[0], node_out), (w_out_far.at[0], w_out), (gain_far, gain),
    )

    @pl.when(learned())
    def _():
        fetch(weights, done)

    numbers = [listed_block(row[5:6, 0:128], l) for row in (site, rim_a, rim_b) for l in range(listed)]
    fetch([(near_far.at[b], near.at[i]) for i, b in enumerate(numbers)], done, 5)

    @pl.when(learned())
    def _():
        for i, (source, target) in enumerate(weights[1:]):
            pltpu.make_async_copy(source, target, done.at[1 + i]).wait()
        in_first[...] = flip(node_in[0]).astype(BF16)
        in_second[...] = flip(node_in[1]).astype(BF16)
        out_t[...] = flip(w_out[...]).astype(BF16)
        node_t[...] = flip(node_out[...]).astype(BF16)
        gain_col[...] = jnp.broadcast_to(gain[...], (8, width)).T

    for i, b in enumerate(numbers):
        pltpu.make_async_copy(near_far.at[b], near.at[i], done.at[5 + i]).wait()
    near_own[...] = near[0:listed]
    for i in range(3 * listed):
        tile = near[i]
        cols[i * 128 : i * 128 + 128, :] = jnp.concatenate([tile, tile], axis=0).T
    reach = listed * 128
    own_field = charge_field(site[...], cols, 0, reach)
    field = jnp.concatenate(
        [own_field, charge_field(rim_a[...], cols, reach, reach), charge_field(rim_b[...], cols, 2 * reach, reach)],
        axis=1,
    )
    strength = jnp.sqrt(1.0 + (field[0:1] * field[0:1] + field[1:2] * field[1:2] + field[2:3] * field[2:3]))
    outside_row[...] = jnp.broadcast_to(strength[:, :width], outside_row.shape)

    @pl.when(learned())
    def _():
        features = jnp.concatenate([feat_t[...], side_a[...], side_b[...]], axis=1)
        start = (features.astype(F32) + gain_col[:, 0:1] * strength).astype(BF16)
        present = jnp.concatenate([jnp.ones((1, width), F32), rim_a[6:7, :], rim_b[6:7, :]], axis=1)
        raised = dot(in_first[...], start)
        table = jnp.where(present > 0.5, raised, 0.0).astype(BF16)
        pltpu.make_async_copy(third_far, third, done.at[0]).wait()
        new = message(0, start[:, :width], table, third, out_t[...], node_t[...], slots, total)
        hidden_out[...] = new
        raised = dot(in_second[...], new).astype(BF16)
        lifted_out[...] = raised
        lend_channels(raised, picks, lent_a, lent_b)

    @pl.when(jnp.logical_not(learned()))
    def _():
        known = [fixed[...], join3(side_a[0:24, :].astype(F32)), join3(side_b[0:24, :].astype(F32))]
        whole = jnp.concatenate(known, axis=1) + rows([field])
        fixed_out[...] = whole[:, :width]
        polar = jnp.concatenate([site[4:5, :], rim_a[4:5, :], rim_b[4:5, :]], axis=1)
        new = sweep(site, w3, w5, whole[:, :width], polar * whole, entry, moment)
        dipole_out[...] = new
        lend_pieces(new, picks, lent_a, lent_b)


def second_kernel(
    hidden, lifted, side_a, side_b, pack, w3, w5, fixed, dipole, entry,
    third_far, node_out_far, w_out_far, readout_far,
    charge, dipole_out, small_a, small_b,
    third, node_out, w_out, readout, total, moment, done,
):
    site, slots, picks = views(pack)

    @pl.when(learned())
    def _():
        fetch(
            ((third_far, third), (node_out_far.at[1], node_out), (w_out_far.at[1], w_out), (readout_far, readout)), done
        )()
        table = jnp.concatenate([lifted[...], side_a[...], side_b[...]], axis=1)
        out_t, node_t = flip(w_out[...]).astype(BF16), flip(node_out[...]).astype(BF16)
        new = message(1, hidden[...], table, third, out_t, node_t, slots, total)
        charge[...] = dot(rows([readout[...].astype(F32)]).astype(BF16), new)

    @pl.when(jnp.logical_not(learned()))
    def _():
        sides = [join3(side_a[0:24, :].astype(F32)), join3(side_b[0:24, :].astype(F32))]
        table = jnp.concatenate([dipole[...]] + sides, axis=1)
        new = sweep(site, w3, w5, fixed[...], table, entry, moment)
        dipole_out[...] = new
        lend_whole(new, picks, small_a, small_b)


def third_kernel(side_a, side_b, pack, w3, w5, fixed, dipole, entry, dipole_out, small_a, small_b, moment):
    site, _, picks = views(pack)

    @pl.when(jnp.logical_not(learned()))
    def _():
        table = jnp.concatenate([dipole[...], side_a[...], side_b[...]], axis=1)
        new = sweep(site, w3, w5, fixed[...], table, entry, moment)
        dipole_out[...] = new
        lend_whole(new, picks, small_a, small_b)


def response_kernel(
    near, pack, charge, outside_row, side_a, side_b, w3, w5, fixed, dipole, entry,
    result, spread, cols, moment, term,
):
    site = views(pack)[0]
    width = site.shape[1]
    listed = near.shape[0]
    blocks = [listed_block(site[5:6, 0:128], l) for l in range(listed)]
    spread[...] = jnp.zeros_like(spread)
    term[...] = jnp.zeros_like(term)

    def terms(dipoles):
        for l in range(listed):
            tile = near[l]
            tx, ty, tz = tile[0:1, :], tile[1:2, :], tile[2:3, :]

            def some_rows(j, acc):
                start = pl.multiple_of(j * TERM_CHUNK, TERM_CHUNK)
                c = cols[pl.ds(start, TERM_CHUNK), :]
                rx, ry, rz = tx - c[:, 0:1], ty - c[:, 1:2], tz - c[:, 2:3]
                inverse = lax.rsqrt(rx * rx + ry * ry + rz * rz + SMOOTH)
                squared = inverse * inverse
                cube = squared * inverse
                if dipoles:
                    dx, dy, dz = c[:, 4:5], c[:, 5:6], c[:, 6:7]
                    scale = (rx * dx + ry * dy + rz * dz) * (3.0 * (cube * squared))
                    return (
                        acc[0] + (rx * scale - dx * cube),
                        acc[1] + (ry * scale - dy * cube),
                        acc[2] + (rz * scale - dz * cube),
                    )
                scale = c[:, 3:4] * cube
                return acc[0] + rx * scale, acc[1] + ry * scale, acc[2] + rz * scale

            nil = jnp.zeros((TERM_CHUNK, 128), F32)
            sums = lax.fori_loop(0, width // TERM_CHUNK, some_rows, (nil, nil, nil), unroll=TERM_UNROLL)
            for axis in range(3):
                term[l, axis : axis + 1, :] = jnp.sum(sums[axis], axis=0, keepdims=True)

    @pl.when(learned())
    def _():
        q = charge[...]
        result[...] = jnp.concatenate([q[0:2], outside_row[0:1, :]], axis=0)
        cols[...] = rows([site[0:3, :], q[0:1]]).T
        terms(False)

    @pl.when(jnp.logical_not(learned()))
    def _():
        table = jnp.concatenate([dipole[...], side_a[...], side_b[...]], axis=1)
        new = sweep(site, w3, w5, fixed[...], table, entry, moment)
        result[...] = new[0:3]
        cols[...] = rows([site[0:4, :], new[0:3]]).T
        terms(True)

    side = lax.broadcasted_iota(jnp.int32, (2, 128), 0)
    for l in range(listed):
        owner, part = blocks[l] >> 1, blocks[l] & 1
        for axis in range(3):
            spread[3 * owner + axis] += jnp.where(side == part, term[l, axis : axis + 1, :], 0.0)


def gather_kernel(pieces, share):
    total = jnp.sum(pieces[...], axis=0)
    share[...] = jnp.concatenate(
        [jnp.concatenate([total[axis, 0:1], total[axis, 1:2]], axis=1) for axis in range(3)], axis=0
    )


def finish_kernel(result, share, result_far, share_far, done):
    fetch(((result, result_far), (share, share_far)), done)()


def placed(block):
    y_half, plane, step, side = block // 64, block // 8 % 8, block // 2 % 4, block % 2
    x = 3 - step if plane % 2 else step
    z = (plane - 1) % 8 if y_half else plane
    along = 1 - side if (step + y_half) % 2 == 0 else side
    y = 2 * y_half + along
    return ((y % 2 * 8 + z) * 4 + x) * 2 + y // 2


def local(
    positions, charges, polar, features, neighbours, send_rows, blocks,
    radial_in, radial_mid, radial_out, node_in, node_out, field_gain, readout,
):
    width = positions.shape[1]
    slot_count = neighbours.shape[1]
    depth = 2 * width
    half = send_rows.shape[1]
    channels = features.shape[1]
    listed = blocks.shape[0]
    members = lax.axis_size(DOM)
    near_pairs = [(i, i ^ 1) for i in range(members)]
    far_pairs = [(i, ((i - 1) ^ 1) + 1) for i in range(1, members - 1)]
    same = list(range(members))
    place = [placed(i) for i in range(members)]

    def move(value, pairs, source, target, groups=(0, 1)):
        return lax.ppermute(
            value, EVERY, [(source[a] + g * members, target[b] + g * members) for g in groups for a, b in pairs]
        )

    def trade(a, b, groups=(0, 1), source=place):
        return move(a, near_pairs, source, place, groups), move(b, far_pairs, source, place, groups)

    row8, table8 = ((8, width), F32), ((8, half), F32)
    wide = ((channels, half), BF16)
    by_site = ((channels, width), BF16)
    ints = jnp.int32
    itself = [(i, i) for i in range(members)]
    pack, mine, lent_a, lent_b = call(
        rows_kernel, [((slot_count + 16, width), F32), ((2, 4, half), F32), table8, table8],
        (), (positions, charges[None], polar[None], neighbours.T, send_rows, blocks),
        [pltpu.VMEM((3, width), F32), pltpu.VMEM((1, width), F32), pltpu.VMEM((1, width), F32),
         pltpu.VMEM((slot_count, width), ints), pltpu.VMEM((2, half), ints), pltpu.SMEM((listed,), ints)], 6,
    )
    partner = lax.ppermute(mine, "grp", [(0, 1), (1, 0)])
    copies = jnp.broadcast_to(partner[None], (members,) + partner.shape)
    near = lax.all_to_all(copies, DOM, 0, 0, tiled=True).reshape(2 * members, 4, half)
    pack = move(pack, itself, same, place)
    rim_a, rim_b = trade(lent_a, lent_b, source=same)
    features = move(features, itself, same, place, (0,))
    feat_t, w3, w5, fixed, entry, lent_a, lent_b = call(
        static_kernel, [by_site, ((depth, width), F32), ((depth, width), F32), row8, ((depth, 8), F32), wide, wide],
        (pack, rim_a, rim_b), (features,), [pltpu.VMEM((width, channels), BF16)], 1, loose=1,
    )
    side_a, side_b = trade(lent_a, lent_b)
    third_shape = (LAYERS * radial_in.shape[2], slot_count * width)
    (third,) = call(
        radial_kernel, [(third_shape, BF16)], (pack, rim_a, rim_b), (radial_in, radial_mid),
        [pltpu.VMEM(radial_in.shape, BF16), pltpu.VMEM(radial_mid.shape, BF16), pltpu.VMEM(third_shape, BF16)],
        2 + slot_count // RADIAL_SLOTS, 1,
    )
    moment = pltpu.VMEM((depth, 8), F32)
    total = pltpu.VMEM((channels, width), F32)
    square = pltpu.VMEM(node_out.shape[1:], BF16)
    last = pltpu.VMEM(radial_out.shape[1:], BF16)
    outside_row, near_own, hidden, lifted, fixed_all, dipole, lent_a, lent_b = call(
        first_kernel, [row8, ((listed, 4, half), F32), by_site, by_site, row8, row8, wide, wide],
        (pack, rim_a, rim_b, feat_t, side_a, side_b, w3, w5, fixed, entry),
        (near, third, node_in, node_out, radial_out, field_gain[None]),
        [pltpu.VMEM((3 * listed, 4, half), F32), pltpu.VMEM((3 * listed * half, 8), F32),
         pltpu.VMEM(third_shape, BF16), pltpu.VMEM(node_in.shape, BF16), square, last,
         pltpu.VMEM((1, channels), F32), total, moment, square, square,
         pltpu.VMEM((channels, radial_out.shape[1]), BF16), square, pltpu.VMEM((channels, 8), F32)],
        5 + 3 * listed, loose=1,
    )
    side_a, side_b = trade(lent_a, lent_b)
    charge, dipole, small_a, small_b = call(
        second_kernel, [row8, row8, table8, table8],
        (hidden, lifted, side_a, side_b, pack, w3, w5, fixed_all, dipole, entry),
        (third, node_out, radial_out, readout.T),
        [pltpu.VMEM(third_shape, BF16), square, last, pltpu.VMEM((2, channels), BF16), total, moment], 4,
    )
    side_a, side_b = trade(small_a, small_b, (1,))
    dipole, small_a, small_b = call(
        third_kernel, [row8, table8, table8], (side_a, side_b, pack, w3, w5, fixed_all, dipole, entry),
        (), [moment],
    )
    side_a, side_b = trade(small_a, small_b, (1,))
    result, spread = call(
        response_kernel, [((3, width), F32), ((3 * members, 2, half), F32)],
        (near_own, pack, charge, outside_row, side_a, side_b, w3, w5, fixed_all, dipole, entry), (),
        [pltpu.VMEM((width, 8), F32), moment, pltpu.VMEM((listed, 4, half), F32)],
    )
    pieces = lax.all_to_all(spread, DOM, 0, 0, tiled=True).reshape(members, 3, 2, half)
    (share,) = call(gather_kernel, [((3, width), F32)], (pieces,))
    result = move(result, itself, place, same)
    share = lax.ppermute(share, "grp", [(0, 1), (1, 0)])
    whole = ((3, width), F32)
    return tuple(call(finish_kernel, [whole, whole], (result, share), copies=2, far_outs=2))


def solution(mesh):
    sites = P(None, EVERY)
    in_specs = (sites, P(EVERY), P(EVERY), P(EVERY, None), P(EVERY, None), sites, P(EVERY)) + (P(),) * 7
    return jax.shard_map(local, mesh=mesh, in_specs=in_specs, out_specs=(sites, sites), check_vma=False)
```

```python
import jax
import jax.numpy as jnp
from jax import lax
from jax.experimental import pallas as pl
from jax.experimental.pallas import tpu as pltpu
from jax.sharding import PartitionSpec as P

BASIS = 8
LAYERS = 2
SMOOTH = 1.0
SPACING = 0.75
DOM = ("dom", "sub")
EVERY = ("grp", "dom", "sub")
F32 = jnp.float32
BF16 = jnp.bfloat16
VMEM = pl.BlockSpec(memory_space=pltpu.VMEM)
ANY = pl.BlockSpec(memory_space=pl.ANY)
SWEEP_CHUNK, SWEEP_UNROLL = 32, 4
FIELD_CHUNK, FIELD_UNROLL = 32, 4
TERM_CHUNK, TERM_UNROLL = 64, 4
STATIC_CHUNK = 32
RADIAL_SLOTS = 8
MESSAGE_SLOTS = (8, 16)


def call(body, outs, held, far=(), scratch=(), copies=0, far_outs=0, loose=0):
    return pl.pallas_call(
        body,
        out_shape=[jax.ShapeDtypeStruct(s, d) for s, d in outs[: len(outs) - far_outs]]
        + [pltpu.HBM(s, d) for s, d in outs[len(outs) - far_outs :]],
        in_specs=[VMEM] * len(held) + [ANY] * len(far),
        out_specs=[VMEM] * (len(outs) - far_outs) + [ANY] * far_outs,
        scratch_shapes=list(scratch) + ([pltpu.SemaphoreType.DMA((copies,))] if copies else []),
        compiler_params=pltpu.CompilerParams(vmem_limit_bytes=24 * 2**20),
    )(*held, *far[:loose], *[pltpu.with_memory_space_constraint(a, pltpu.HBM) for a in far[loose:]])


def fetch(pairs, done, first=0):
    copies = [pltpu.make_async_copy(a, b, done.at[first + i]) for i, (a, b) in enumerate(pairs)]
    for c in copies:
        c.start()

    def wait():
        for c in copies:
            c.wait()

    return wait


def learned():
    return lax.axis_index("grp") == 0


def dot(a, b):
    return jnp.dot(a, b, preferred_element_type=F32)


def silu(x):
    half = 0.5 * x
    return half + half * jnp.tanh(half)


def flip(x):
    return x.astype(F32).T


def split3(x):
    high = x.astype(BF16)
    rest = x - high.astype(F32)
    mid = rest.astype(BF16)
    low = (rest - mid.astype(F32)).astype(BF16)
    return jnp.concatenate([high, mid, low], axis=0)


def join3(x):
    return x[0:8] + x[8:16] + x[16:24]


def one_hot(row, depth):
    ids = lax.broadcasted_iota(jnp.int32, (depth, row.shape[1]), 0)
    return jnp.where(ids == row.astype(jnp.int32), 1.0, 0.0).astype(BF16)


def views(pack):
    return pack.at[0:8, :], pack.at[8:40, :], pack.at[40:41, :]


def picked_row(picks, row):
    return picks[0:1, row * 128 : row * 128 + 128]


def listed_block(row, l):
    lane = lax.broadcasted_iota(jnp.int32, row.shape, 1)
    return jnp.sum(jnp.where(lane == l, row, 0.0)).astype(jnp.int32)


def slot_row(slots, first, count):
    return jnp.concatenate([slots[pl.ds(first + i, 1), :] for i in range(count)], axis=1)


def rows(parts, count=8):
    have = sum(p.shape[0] for p in parts)
    return jnp.concatenate(list(parts) + [jnp.zeros((count - have, parts[0].shape[1]), F32)], axis=0)


def rows_kernel(
    pos_far, charge_far, polar_far, table_far, send_far, blocks_far,
    pack, mine, lent_a, lent_b,
    pos, charge, polar, table, send, blocks, done,
):
    pairs = ((pos_far, pos), (charge_far, charge), (polar_far, polar), (table_far, table), (send_far, send))
    wait = fetch(pairs + ((blocks_far, blocks),), done)
    odd = lax.axis_index("sub")
    width = pos.shape[1]
    wait()
    lane = lax.broadcasted_iota(jnp.int32, (1, width), 1)
    listed = jnp.zeros((1, width), jnp.int32)
    for l in range(blocks.shape[0]):
        listed = jnp.where(lane == l, blocks[l], listed)
    listed = listed.astype(F32)
    sites = rows([pos[...], charge[...], polar[...], listed, jnp.ones((1, width), F32)])
    for half in range(2):
        mine[half] = sites[0:4, half * 128 : half * 128 + 128]
    first, second = send[0:1, :], send[1:2, :]
    swap = jnp.full(first.shape, odd, jnp.int32) == 1
    picks = jnp.where(swap, second, first), jnp.where(swap, first, second)
    raw = table[...]
    other = jnp.where((raw >= 256) & (raw < 512), jnp.bitwise_xor(raw, 128), raw)
    keep = jnp.full(raw.shape, odd, jnp.int32) == 1
    pack[0:8, :] = sites
    pack[8:40, :] = jnp.where(keep, raw, other).astype(F32)
    pack[40:48, :] = rows([jnp.concatenate(picks, axis=1).astype(F32)])
    pieces = split3(sites)
    for row, out in zip(picks, (lent_a, lent_b)):
        found = join3(dot(pieces, one_hot(row, width)))
        out[...] = rows([found[0:5], listed[:, 0:128], jnp.ones((1, 128), F32)])


def static_kernel(
    pack, rim_a, rim_b, features_far,
    feat_t, w3, w5, fixed, entry, lent_a, lent_b, features, done,
):
    site, slots, picks = views(pack)
    width = site.shape[1]
    depth = 2 * width
    slot_count = slots.shape[0]

    @pl.when(learned())
    def _():
        fetch(((features_far, features),), done)()
        flipped = flip(features[...]).astype(BF16)
        feat_t[...] = flipped
        lend_channels(flipped, picks, lent_a, lent_b)

    @pl.when(jnp.logical_not(learned()))
    def _():
        table = jnp.concatenate([site[...], rim_a[...], rim_b[...]], axis=1)
        entry[...] = table.T
        tx, ty, tz = site[0:1, :], site[1:2, :], site[2:3, :]

        def some_rows(j, acc):
            start = pl.multiple_of(j * STATIC_CHUNK, STATIC_CHUNK)
            ids = (lax.broadcasted_iota(jnp.int32, (STATIC_CHUNK, width), 0) + start).astype(F32)
            count = jnp.zeros((STATIC_CHUNK, width), F32)
            for k in range(slot_count):
                count = count + jnp.where(ids == slots[k : k + 1, :], 1.0, 0.0)
            cols = entry[pl.ds(start, STATIC_CHUNK), :]
            rx, ry, rz = tx - cols[:, 0:1], ty - cols[:, 1:2], tz - cols[:, 2:3]
            inverse = lax.rsqrt(rx * rx + ry * ry + rz * rz + SMOOTH)
            squared = inverse * inverse
            cube = count * (squared * inverse)
            w3[pl.ds(start, STATIC_CHUNK), :] = cube
            w5[pl.ds(start, STATIC_CHUNK), :] = 3.0 * (cube * squared)
            scale = cols[:, 3:4] * cube
            return acc[0] + rx * scale, acc[1] + ry * scale, acc[2] + rz * scale

        nil = jnp.zeros((STATIC_CHUNK, width), F32)
        sums = lax.fori_loop(0, depth // STATIC_CHUNK, some_rows, (nil, nil, nil))
        total = rows([jnp.sum(s, axis=0, keepdims=True) for s in sums])
        fixed[...] = total
        lend_pieces(total, picks, lent_a, lent_b)


def radial_kernel(
    pack, rim_a, rim_b, w_in_far, w_mid_far,
    third_far, w_in, w_mid, third, done,
):
    site, slots, _ = views(pack)
    width = site.shape[1]
    depth = 2 * width
    slot_count = slots.shape[0]

    @pl.when(learned())
    def _():
        wait = fetch(((w_in_far, w_in), (w_mid_far, w_mid)), done)
        pieces = split3(jnp.concatenate([site[...], rim_a[...], rim_b[...]], axis=1))
        step = RADIAL_SLOTS * width
        here = jnp.concatenate([site[...]] * RADIAL_SLOTS, axis=1)
        centres = lax.broadcasted_iota(jnp.int32, (BASIS, step), 0).astype(F32) * SPACING
        wait()
        first_w = jnp.concatenate([flip(w_in[0]), flip(w_in[1])], axis=0).astype(BF16)
        zero = jnp.zeros((64, 64), F32)

        def both(level):
            top = jnp.concatenate([flip(w_mid[0, level]), zero], axis=1)
            bottom = jnp.concatenate([zero, flip(w_mid[1, level])], axis=1)
            return jnp.concatenate([top, bottom], axis=0).astype(BF16)

        second_w, third_w = both(0), both(1)

        def part_out(k):
            part = pl.ds(pl.multiple_of(k * step, step), step)
            return pltpu.make_async_copy(third.at[:, part], third_far.at[:, part], done.at[2 + k])

        def some_slots(k, carry):
            found = join3(dot(pieces, one_hot(slot_row(slots, k * RADIAL_SLOTS, RADIAL_SLOTS), depth)))
            offset = here - found
            squares = offset * offset
            dist_sq = squares[0:1] + squares[1:2] + squares[2:3] + SMOOTH
            gap = jnp.sqrt(dist_sq) - centres
            basis = jnp.exp(-(gap * gap)).astype(BF16)
            hidden = silu(dot(first_w, basis)).astype(BF16)
            hidden = silu(dot(second_w, hidden)).astype(BF16)
            start = pl.multiple_of(k * step, step)
            third[:, pl.ds(start, step)] = silu(dot(third_w, hidden)).astype(BF16)
            part_out(k).start()
            return carry

        lax.fori_loop(0, slot_count // RADIAL_SLOTS, some_slots, 0)
        for k in range(slot_count // RADIAL_SLOTS):
            part_out(k).wait()


def lend_pieces(values, picks, lent_a, lent_b):
    pieces = split3(values)
    for row, out in ((0, lent_a), (1, lent_b)):
        found = dot(pieces, one_hot(picked_row(picks, row), values.shape[1]))
        out[...] = jnp.zeros_like(out)
        out[0:32, :] = rows([found], 32).astype(BF16)


def lend_whole(values, picks, lent_a, lent_b):
    pieces = split3(values)
    for row, out in ((0, lent_a), (1, lent_b)):
        out[...] = join3(dot(pieces, one_hot(picked_row(picks, row), values.shape[1])))


def lend_channels(values, picks, lent_a, lent_b):
    for row, out in ((0, lent_a), (1, lent_b)):
        out[...] = dot(values, one_hot(picked_row(picks, row), values.shape[1])).astype(BF16)


def sweep(site, w3, w5, fixed, dipoles, entry, moment):
    width = site.shape[1]
    moment[...] = dipoles.T
    tx, ty, tz = site[0:1, :], site[1:2, :], site[2:3, :]

    def some_rows(j, acc):
        start = pl.multiple_of(j * SWEEP_CHUNK, SWEEP_CHUNK)
        cols, d = entry[pl.ds(start, SWEEP_CHUNK), :], moment[pl.ds(start, SWEEP_CHUNK), :]
        rx, ry, rz = tx - cols[:, 0:1], ty - cols[:, 1:2], tz - cols[:, 2:3]
        dx, dy, dz = d[:, 0:1], d[:, 1:2], d[:, 2:3]
        cube = w3[pl.ds(start, SWEEP_CHUNK), :]
        scale = (rx * dx + ry * dy + rz * dz) * w5[pl.ds(start, SWEEP_CHUNK), :]
        return (
            acc[0] + (rx * scale - dx * cube),
            acc[1] + (ry * scale - dy * cube),
            acc[2] + (rz * scale - dz * cube),
        )

    nil = jnp.zeros((SWEEP_CHUNK, width), F32)
    sums = lax.fori_loop(0, w3.shape[0] // SWEEP_CHUNK, some_rows, (nil, nil, nil), unroll=SWEEP_UNROLL)
    return site[4:5, :] * (fixed + rows([jnp.sum(s, axis=0, keepdims=True) for s in sums]))


def message(layer, hidden, table, third, out_t, node_t, slots, total):
    slot_count = slots.shape[0]
    width = slots.shape[1]
    together = MESSAGE_SLOTS[layer]
    step = together * width
    total[...] = jnp.zeros_like(total)

    def some_slots(k, carry):
        row = slot_row(slots, k * together, together)
        picked = dot(table, one_hot(row, table.shape[1]))
        start = pl.multiple_of(k * step, step)
        weight = dot(out_t, third[layer * 64 : layer * 64 + 64, pl.ds(start, step)])
        product = weight * picked
        part = product[:, 0:width]
        for i in range(1, together):
            part = part + product[:, i * width : (i + 1) * width]
        total[...] += part
        return carry

    lax.fori_loop(0, slot_count // together, some_slots, 0)
    mean = (total[...] * (1.0 / slot_count)).astype(BF16)
    return (hidden.astype(F32) + silu(dot(node_t, mean))).astype(BF16)


def charge_field(target, cols, first, count):
    tx, ty, tz = target[0:1, :], target[1:2, :], target[2:3, :]

    def some_rows(j, acc):
        c = cols[pl.ds(pl.multiple_of(first + j * FIELD_CHUNK, FIELD_CHUNK), FIELD_CHUNK), :]
        rx, ry, rz = tx - c[:, 0:1], ty - c[:, 1:2], tz - c[:, 2:3]
        inverse = lax.rsqrt(rx * rx + ry * ry + rz * rz + SMOOTH)
        scale = c[:, 3:4] * (inverse * inverse * inverse)
        return acc[0] + rx * scale, acc[1] + ry * scale, acc[2] + rz * scale

    nil = jnp.zeros((FIELD_CHUNK, target.shape[1]), F32)
    sums = lax.fori_loop(0, count // FIELD_CHUNK, some_rows, (nil, nil, nil), unroll=FIELD_UNROLL)
    return jnp.concatenate([jnp.sum(s, axis=0, keepdims=True) for s in sums], axis=0)


def first_kernel(
    pack, rim_a, rim_b, feat_t, side_a, side_b, w3, w5, fixed, entry,
    near_far, third_far, node_in_far, node_out_far, w_out_far, gain_far,
    outside_row, near_own, hidden_out, lifted_out, fixed_out, dipole_out, lent_a, lent_b,
    near, cols, third, node_in, node_out, w_out, gain, total, moment, done,
):
    site, slots, picks = views(pack)
    width = site.shape[1]
    listed = near_own.shape[0]
    numbers = [listed_block(row[5:6, 0:128], l) for row in (site, rim_a, rim_b) for l in range(listed)]
    fetch([(near_far.at[b], near.at[i]) for i, b in enumerate(numbers)], done, 5)
    weights = (
        (third_far, third), (node_in_far, node_in), (node_out_far.at[0], node_out),
        (w_out_far.at[0], w_out), (gain_far, gain),
    )

    @pl.when(learned())
    def _():
        fetch(weights, done)

    for i, b in enumerate(numbers):
        pltpu.make_async_copy(near_far.at[b], near.at[i], done.at[5 + i]).wait()
    near_own[...] = near[0:listed]
    for i in range(3 * listed):
        tile = near[i]
        cols[i * 128 : i * 128 + 128, :] = jnp.concatenate([tile, tile], axis=0).T
    reach = listed * 128
    own_field = charge_field(site[...], cols, 0, reach)
    field = jnp.concatenate(
        [own_field, charge_field(rim_a[...], cols, reach, reach), charge_field(rim_b[...], cols, 2 * reach, reach)],
        axis=1,
    )
    strength = jnp.sqrt(1.0 + (field[0:1] * field[0:1] + field[1:2] * field[1:2] + field[2:3] * field[2:3]))
    outside_row[...] = jnp.broadcast_to(strength[:, :width], outside_row.shape)

    @pl.when(learned())
    def _():
        for i, (a, b) in enumerate(weights):
            pltpu.make_async_copy(a, b, done.at[i]).wait()
        gain_col = jnp.broadcast_to(gain[...], (8, width)).T
        features = jnp.concatenate([feat_t[...], side_a[...], side_b[...]], axis=1)
        start = (features.astype(F32) + gain_col[:, 0:1] * strength).astype(BF16)
        present = jnp.concatenate([jnp.ones((1, width), F32), rim_a[6:7, :], rim_b[6:7, :]], axis=1)
        raised = dot(flip(node_in[0]).astype(BF16), start)
        table = jnp.where(present > 0.5, raised, 0.0).astype(BF16)
        out_t, node_t = flip(w_out[...]).astype(BF16), flip(node_out[...]).astype(BF16)
        new = message(0, start[:, :width], table, third, out_t, node_t, slots, total)
        hidden_out[...] = new
        raised = dot(flip(node_in[1]).astype(BF16), new).astype(BF16)
        lifted_out[...] = raised
        lend_channels(raised, picks, lent_a, lent_b)

    @pl.when(jnp.logical_not(learned()))
    def _():
        known = [fixed[...], join3(side_a[0:24, :].astype(F32)), join3(side_b[0:24, :].astype(F32))]
        whole = jnp.concatenate(known, axis=1) + rows([field])
        fixed_out[...] = whole[:, :width]
        polar = jnp.concatenate([site[4:5, :], rim_a[4:5, :], rim_b[4:5, :]], axis=1)
        new = sweep(site, w3, w5, whole[:, :width], polar * whole, entry, moment)
        dipole_out[...] = new
        lend_pieces(new, picks, lent_a, lent_b)


def second_kernel(
    hidden, lifted, side_a, side_b, pack, w3, w5, fixed, dipole, entry,
    third_far, node_out_far, w_out_far, readout_far,
    charge, dipole_out, small_a, small_b,
    third, node_out, w_out, readout, total, moment, done,
):
    site, slots, picks = views(pack)

    @pl.when(learned())
    def _():
        fetch(
            ((third_far, third), (node_out_far.at[1], node_out), (w_out_far.at[1], w_out), (readout_far, readout)), done
        )()
        table = jnp.concatenate([lifted[...], side_a[...], side_b[...]], axis=1)
        out_t, node_t = flip(w_out[...]).astype(BF16), flip(node_out[...]).astype(BF16)
        new = message(1, hidden[...], table, third, out_t, node_t, slots, total)
        charge[...] = dot(rows([readout[...].astype(F32)]).astype(BF16), new)

    @pl.when(jnp.logical_not(learned()))
    def _():
        sides = [join3(side_a[0:24, :].astype(F32)), join3(side_b[0:24, :].astype(F32))]
        table = jnp.concatenate([dipole[...]] + sides, axis=1)
        new = sweep(site, w3, w5, fixed[...], table, entry, moment)
        dipole_out[...] = new
        lend_whole(new, picks, small_a, small_b)


def third_kernel(side_a, side_b, pack, w3, w5, fixed, dipole, entry, dipole_out, small_a, small_b, moment):
    site, _, picks = views(pack)

    @pl.when(jnp.logical_not(learned()))
    def _():
        table = jnp.concatenate([dipole[...], side_a[...], side_b[...]], axis=1)
        new = sweep(site, w3, w5, fixed[...], table, entry, moment)
        dipole_out[...] = new
        lend_whole(new, picks, small_a, small_b)


def response_kernel(
    near, pack, charge, outside_row, side_a, side_b, w3, w5, fixed, dipole, entry,
    result, spread, cols, moment, term,
):
    site = views(pack)[0]
    width = site.shape[1]
    listed = near.shape[0]
    blocks = [listed_block(site[5:6, 0:128], l) for l in range(listed)]
    spread[...] = jnp.zeros_like(spread)
    term[...] = jnp.zeros_like(term)

    def terms(dipoles):
        for l in range(listed):
            tile = near[l]
            tx, ty, tz = tile[0:1, :], tile[1:2, :], tile[2:3, :]

            def some_rows(j, acc):
                start = pl.multiple_of(j * TERM_CHUNK, TERM_CHUNK)
                c = cols[pl.ds(start, TERM_CHUNK), :]
                rx, ry, rz = tx - c[:, 0:1], ty - c[:, 1:2], tz - c[:, 2:3]
                inverse = lax.rsqrt(rx * rx + ry * ry + rz * rz + SMOOTH)
                squared = inverse * inverse
                cube = squared * inverse
                if dipoles:
                    dx, dy, dz = c[:, 4:5], c[:, 5:6], c[:, 6:7]
                    scale = (rx * dx + ry * dy + rz * dz) * (3.0 * (cube * squared))
                    return (
                        acc[0] + (rx * scale - dx * cube),
                        acc[1] + (ry * scale - dy * cube),
                        acc[2] + (rz * scale - dz * cube),
                    )
                scale = c[:, 3:4] * cube
                return acc[0] + rx * scale, acc[1] + ry * scale, acc[2] + rz * scale

            nil = jnp.zeros((TERM_CHUNK, 128), F32)
            sums = lax.fori_loop(0, width // TERM_CHUNK, some_rows, (nil, nil, nil), unroll=TERM_UNROLL)
            for axis in range(3):
                term[l, axis : axis + 1, :] = jnp.sum(sums[axis], axis=0, keepdims=True)

    @pl.when(learned())
    def _():
        q = charge[...]
        result[...] = jnp.concatenate([q[0:2], outside_row[0:1, :]], axis=0)
        cols[...] = rows([site[0:3, :], q[0:1]]).T
        terms(False)

    @pl.when(jnp.logical_not(learned()))
    def _():
        table = jnp.concatenate([dipole[...], side_a[...], side_b[...]], axis=1)
        new = sweep(site, w3, w5, fixed[...], table, entry, moment)
        result[...] = new[0:3]
        cols[...] = rows([site[0:4, :], new[0:3]]).T
        terms(True)

    side = lax.broadcasted_iota(jnp.int32, (2, 128), 0)
    for l in range(listed):
        owner, part = blocks[l] >> 1, blocks[l] & 1
        for axis in range(3):
            spread[3 * owner + axis] += jnp.where(side == part, term[l, axis : axis + 1, :], 0.0)


def gather_kernel(pieces, share):
    total = jnp.sum(pieces[...], axis=0)
    share[...] = jnp.concatenate(
        [jnp.concatenate([total[axis, 0:1], total[axis, 1:2]], axis=1) for axis in range(3)], axis=0
    )


def finish_kernel(result, share, result_far, share_far, done):
    fetch(((result, result_far), (share, share_far)), done)()


def placed(block):
    y_half, plane, step, side = block // 64, block // 8 % 8, block // 2 % 4, block % 2
    x = 3 - step if plane % 2 else step
    z = (plane - 1) % 8 if y_half else plane
    along = 1 - side if (step + y_half) % 2 == 0 else side
    y = 2 * y_half + along
    return ((y % 2 * 8 + z) * 4 + x) * 2 + y // 2


def local(
    positions, charges, polar, features, neighbours, send_rows, blocks,
    radial_in, radial_mid, radial_out, node_in, node_out, field_gain, readout,
):
    width = positions.shape[1]
    slot_count = neighbours.shape[1]
    depth = 2 * width
    half = send_rows.shape[1]
    channels = features.shape[1]
    listed = blocks.shape[0]
    members = lax.axis_size(DOM)
    near_pairs = [(i, i ^ 1) for i in range(members)]
    far_pairs = [(i, ((i - 1) ^ 1) + 1) for i in range(1, members - 1)]
    same = list(range(members))
    place = [placed(i) for i in range(members)]

    def move(value, pairs, source, target, groups=(0, 1)):
        return lax.ppermute(
            value, EVERY, [(source[a] + g * members, target[b] + g * members) for g in groups for a, b in pairs]
        )

    def trade(a, b, groups=(0, 1), source=place):
        return move(a, near_pairs, source, place, groups), move(b, far_pairs, source, place, groups)

    row8, table8 = ((8, width), F32), ((8, half), F32)
    wide = ((channels, half), BF16)
    by_site = ((channels, width), BF16)
    ints = jnp.int32
    itself = [(i, i) for i in range(members)]
    pack, mine, lent_a, lent_b = call(
        rows_kernel, [((slot_count + 16, width), F32), ((2, 4, half), F32), table8, table8],
        (), (positions, charges[None], polar[None], neighbours.T, send_rows, blocks),
        [pltpu.VMEM((3, width), F32), pltpu.VMEM((1, width), F32), pltpu.VMEM((1, width), F32),
         pltpu.VMEM((slot_count, width), ints), pltpu.VMEM((2, half), ints), pltpu.SMEM((listed,), ints)], 6,
    )
    partner = lax.ppermute(mine, "grp", [(0, 1), (1, 0)])
    copies = jnp.broadcast_to(partner[None], (members,) + partner.shape)
    near = lax.all_to_all(copies, DOM, 0, 0, tiled=True).reshape(2 * members, 4, half)
    pack = move(pack, itself, same, place)
    rim_a, rim_b = trade(lent_a, lent_b, source=same)
    features = move(features, itself, same, place, (0,))
    feat_t, w3, w5, fixed, entry, lent_a, lent_b = call(
        static_kernel, [by_site, ((depth, width), F32), ((depth, width), F32), row8, ((depth, 8), F32), wide, wide],
        (pack, rim_a, rim_b), (features,), [pltpu.VMEM((width, channels), BF16)], 1, loose=1,
    )
    side_a, side_b = trade(lent_a, lent_b)
    third_shape = (LAYERS * radial_in.shape[2], slot_count * width)
    (third,) = call(
        radial_kernel, [(third_shape, BF16)], (pack, rim_a, rim_b), (radial_in, radial_mid),
        [pltpu.VMEM(radial_in.shape, BF16), pltpu.VMEM(radial_mid.shape, BF16), pltpu.VMEM(third_shape, BF16)],
        2 + slot_count // RADIAL_SLOTS, 1,
    )
    moment = pltpu.VMEM((depth, 8), F32)
    total = pltpu.VMEM((channels, width), F32)
    square = pltpu.VMEM(node_out.shape[1:], BF16)
    last = pltpu.VMEM(radial_out.shape[1:], BF16)
    outside_row, near_own, hidden, lifted, fixed_all, dipole, lent_a, lent_b = call(
        first_kernel, [row8, ((listed, 4, half), F32), by_site, by_site, row8, row8, wide, wide],
        (pack, rim_a, rim_b, feat_t, side_a, side_b, w3, w5, fixed, entry),
        (near, third, node_in, node_out, radial_out, field_gain[None]),
        [pltpu.VMEM((3 * listed, 4, half), F32), pltpu.VMEM((3 * listed * half, 8), F32),
         pltpu.VMEM(third_shape, BF16), pltpu.VMEM(node_in.shape, BF16), square, last,
         pltpu.VMEM((1, channels), F32), total, moment], 5 + 3 * listed, loose=1,
    )
    side_a, side_b = trade(lent_a, lent_b)
    charge, dipole, small_a, small_b = call(
        second_kernel, [row8, row8, table8, table8],
        (hidden, lifted, side_a, side_b, pack, w3, w5, fixed_all, dipole, entry),
        (third, node_out, radial_out, readout.T),
        [pltpu.VMEM(third_shape, BF16), square, last, pltpu.VMEM((2, channels), BF16), total, moment], 4,
    )
    side_a, side_b = trade(small_a, small_b, (1,))
    dipole, small_a, small_b = call(
        third_kernel, [row8, table8, table8], (side_a, side_b, pack, w3, w5, fixed_all, dipole, entry),
        (), [moment],
    )
    side_a, side_b = trade(small_a, small_b, (1,))
    result, spread = call(
        response_kernel, [((3, width), F32), ((3 * members, 2, half), F32)],
        (near_own, pack, charge, outside_row, side_a, side_b, w3, w5, fixed_all, dipole, entry), (),
        [pltpu.VMEM((width, 8), F32), moment, pltpu.VMEM((listed, 4, half), F32)],
    )
    pieces = lax.all_to_all(spread, DOM, 0, 0, tiled=True).reshape(members, 3, 2, half)
    (share,) = call(gather_kernel, [((3, width), F32)], (pieces,))
    result = move(result, itself, place, same)
    share = lax.ppermute(share, "grp", [(0, 1), (1, 0)])
    whole = ((3, width), F32)
    return tuple(call(finish_kernel, [whole, whole], (result, share), copies=2, far_outs=2))


def solution(mesh):
    sites = P(None, EVERY)
    in_specs = (sites, P(EVERY), P(EVERY), P(EVERY, None), P(EVERY, None), sites, P(EVERY)) + (P(),) * 7
    return jax.shard_map(local, mesh=mesh, in_specs=in_specs, out_specs=(sites, sites), check_vma=False)
```

```python
import jax
import jax.numpy as jnp
from jax import lax
from jax.experimental import pallas as pl
from jax.experimental.pallas import tpu as pltpu
from jax.sharding import PartitionSpec as P

BASIS = 8
LAYERS = 2
SMOOTH = 1.0
SPACING = 0.75
DOM = ("dom", "sub")
EVERY = ("grp", "dom", "sub")
F32 = jnp.float32
BF16 = jnp.bfloat16
VMEM = pl.BlockSpec(memory_space=pltpu.VMEM)
ANY = pl.BlockSpec(memory_space=pl.ANY)
SWEEP_CHUNK, SWEEP_UNROLL = 32, 16
FIELD_CHUNK, FIELD_UNROLL = 32, 8
TERM_CHUNK, TERM_UNROLL = 64, 4
STATIC_CHUNK = 64
RADIAL_SLOTS = 8
MESSAGE_SLOTS = (8, 16)


def call(body, outs, held, far=(), scratch=(), copies=0, far_outs=0, loose=0):
    return pl.pallas_call(
        body,
        out_shape=[jax.ShapeDtypeStruct(s, d) for s, d in outs[: len(outs) - far_outs]]
        + [pltpu.HBM(s, d) for s, d in outs[len(outs) - far_outs :]],
        in_specs=[VMEM] * len(held) + [ANY] * len(far),
        out_specs=[VMEM] * (len(outs) - far_outs) + [ANY] * far_outs,
        scratch_shapes=list(scratch) + ([pltpu.SemaphoreType.DMA((copies,))] if copies else []),
        compiler_params=pltpu.CompilerParams(vmem_limit_bytes=24 * 2**20),
    )(*held, *far[:loose], *[pltpu.with_memory_space_constraint(a, pltpu.HBM) for a in far[loose:]])


def fetch(pairs, done, first=0):
    copies = [pltpu.make_async_copy(a, b, done.at[first + i]) for i, (a, b) in enumerate(pairs)]
    for c in copies:
        c.start()

    def wait():
        for c in copies:
            c.wait()

    return wait


def learned():
    return lax.axis_index("grp") == 0


def dot(a, b):
    return jnp.dot(a, b, preferred_element_type=F32)


def silu(x):
    half = 0.5 * x
    return half + half * jnp.tanh(half)


def flip(x):
    return x.astype(F32).T


def split3(x):
    high = x.astype(BF16)
    rest = x - high.astype(F32)
    mid = rest.astype(BF16)
    low = (rest - mid.astype(F32)).astype(BF16)
    return jnp.concatenate([high, mid, low], axis=0)


def join3(x):
    return x[0:8] + x[8:16] + x[16:24]


def one_hot(row, depth):
    ids = lax.broadcasted_iota(jnp.int32, (depth, row.shape[1]), 0)
    return jnp.where(ids == row.astype(jnp.int32), 1.0, 0.0).astype(BF16)


def views(pack):
    return pack.at[0:8, :], pack.at[8:40, :], pack.at[40:41, :]


def picked_row(picks, row):
    return picks[0:1, row * 128 : row * 128 + 128]


def listed_block(row, l):
    lane = lax.broadcasted_iota(jnp.int32, row.shape, 1)
    return jnp.sum(jnp.where(lane == l, row, 0.0)).astype(jnp.int32)


def slot_row(slots, first, count):
    return jnp.concatenate([slots[pl.ds(first + i, 1), :] for i in range(count)], axis=1)


def rows(parts, count=8):
    have = sum(p.shape[0] for p in parts)
    return jnp.concatenate(list(parts) + [jnp.zeros((count - have, parts[0].shape[1]), F32)], axis=0)


def rows_kernel(
    pos_far, charge_far, polar_far, table_far, send_far, blocks_far,
    pack, mine, lent_a, lent_b,
    pos, charge, polar, table, send, blocks, done,
):
    pairs = ((pos_far, pos), (charge_far, charge), (polar_far, polar), (table_far, table), (send_far, send))
    wait = fetch(pairs + ((blocks_far, blocks),), done)
    odd = lax.axis_index("sub")
    width = pos.shape[1]
    wait()
    lane = lax.broadcasted_iota(jnp.int32, (1, width), 1)
    listed = jnp.zeros((1, width), jnp.int32)
    for l in range(blocks.shape[0]):
        listed = jnp.where(lane == l, blocks[l], listed)
    listed = listed.astype(F32)
    sites = rows([pos[...], charge[...], polar[...], listed, jnp.ones((1, width), F32)])
    for half in range(2):
        mine[half] = sites[0:4, half * 128 : half * 128 + 128]
    first, second = send[0:1, :], send[1:2, :]
    swap = jnp.full(first.shape, odd, jnp.int32) == 1
    picks = jnp.where(swap, second, first), jnp.where(swap, first, second)
    raw = table[...]
    other = jnp.where((raw >= 256) & (raw < 512), jnp.bitwise_xor(raw, 128), raw)
    keep = jnp.full(raw.shape, odd, jnp.int32) == 1
    pack[0:8, :] = sites
    pack[8:40, :] = jnp.where(keep, raw, other).astype(F32)
    pack[40:48, :] = rows([jnp.concatenate(picks, axis=1).astype(F32)])
    pieces = split3(sites)
    for row, out in zip(picks, (lent_a, lent_b)):
        found = join3(dot(pieces, one_hot(row, width)))
        out[...] = rows([found[0:5], listed[:, 0:128], jnp.ones((1, 128), F32)])


def static_kernel(
    pack, rim_a, rim_b, features_far,
    feat_t, w3, w5, fixed, entry, lent_a, lent_b, features, done,
):
    site, slots, picks = views(pack)
    width = site.shape[1]
    depth = 2 * width
    slot_count = slots.shape[0]

    @pl.when(learned())
    def _():
        fetch(((features_far, features),), done)()
        flipped = flip(features[...]).astype(BF16)
        feat_t[...] = flipped
        lend_channels(flipped, picks, lent_a, lent_b)

    @pl.when(jnp.logical_not(learned()))
    def _():
        table = jnp.concatenate([site[...], rim_a[...], rim_b[...]], axis=1)
        entry[...] = table.T
        tx, ty, tz = site[0:1, :], site[1:2, :], site[2:3, :]

        def some_rows(j, acc):
            start = pl.multiple_of(j * STATIC_CHUNK, STATIC_CHUNK)
            ids = (lax.broadcasted_iota(jnp.int32, (STATIC_CHUNK, width), 0) + start).astype(F32)
            count = jnp.zeros((STATIC_CHUNK, width), F32)
            for k in range(slot_count):
                count = count + jnp.where(ids == slots[k : k + 1, :], 1.0, 0.0)
            cols = entry[pl.ds(start, STATIC_CHUNK), :]
            rx, ry, rz = tx - cols[:, 0:1], ty - cols[:, 1:2], tz - cols[:, 2:3]
            inverse = lax.rsqrt(rx * rx + ry * ry + rz * rz + SMOOTH)
            squared = inverse * inverse
            cube = count * (squared * inverse)
            w3[pl.ds(start, STATIC_CHUNK), :] = cube
            w5[pl.ds(start, STATIC_CHUNK), :] = 3.0 * (cube * squared)
            scale = cols[:, 3:4] * cube
            return acc[0] + rx * scale, acc[1] + ry * scale, acc[2] + rz * scale

        nil = jnp.zeros((STATIC_CHUNK, width), F32)
        sums = lax.fori_loop(0, depth // STATIC_CHUNK, some_rows, (nil, nil, nil))
        total = rows([jnp.sum(s, axis=0, keepdims=True) for s in sums])
        fixed[...] = total
        lend_pieces(total, picks, lent_a, lent_b)


def radial_kernel(
    pack, rim_a, rim_b, w_in_far, w_mid_far,
    third_far, w_in, w_mid, third, done,
):
    site, slots, _ = views(pack)
    width = site.shape[1]
    depth = 2 * width
    slot_count = slots.shape[0]

    @pl.when(learned())
    def _():
        wait = fetch(((w_in_far, w_in), (w_mid_far, w_mid)), done)
        pieces = split3(jnp.concatenate([site[...], rim_a[...], rim_b[...]], axis=1))
        step = RADIAL_SLOTS * width
        here = jnp.concatenate([site[...]] * RADIAL_SLOTS, axis=1)
        centres = lax.broadcasted_iota(jnp.int32, (BASIS, step), 0).astype(F32) * SPACING
        wait()
        first_w = jnp.concatenate([flip(w_in[0]), flip(w_in[1])], axis=0).astype(BF16)
        zero = jnp.zeros((64, 64), F32)

        def both(level):
            top = jnp.concatenate([flip(w_mid[0, level]), zero], axis=1)
            bottom = jnp.concatenate([zero, flip(w_mid[1, level])], axis=1)
            return jnp.concatenate([top, bottom], axis=0).astype(BF16)

        second_w, third_w = both(0), both(1)

        def part_out(k):
            part = pl.ds(pl.multiple_of(k * step, step), step)
            return pltpu.make_async_copy(third.at[:, part], third_far.at[:, part], done.at[2 + k])

        def some_slots(k, carry):
            found = join3(dot(pieces, one_hot(slot_row(slots, k * RADIAL_SLOTS, RADIAL_SLOTS), depth)))
            offset = here - found
            squares = offset * offset
            dist_sq = squares[0:1] + squares[1:2] + squares[2:3] + SMOOTH
            gap = jnp.sqrt(dist_sq) - centres
            basis = jnp.exp(-(gap * gap)).astype(BF16)
            hidden = silu(dot(first_w, basis)).astype(BF16)
            hidden = silu(dot(second_w, hidden)).astype(BF16)
            start = pl.multiple_of(k * step, step)
            third[:, pl.ds(start, step)] = silu(dot(third_w, hidden)).astype(BF16)
            part_out(k).start()
            return carry

        lax.fori_loop(0, slot_count // RADIAL_SLOTS, some_slots, 0)
        for k in range(slot_count // RADIAL_SLOTS):
            part_out(k).wait()


def lend_pieces(values, picks, lent_a, lent_b):
    pieces = split3(values)
    for row, out in ((0, lent_a), (1, lent_b)):
        found = dot(pieces, one_hot(picked_row(picks, row), values.shape[1]))
        out[...] = jnp.zeros_like(out)
        out[0:32, :] = rows([found], 32).astype(BF16)


def lend_whole(values, picks, lent_a, lent_b):
    pieces = split3(values)
    for row, out in ((0, lent_a), (1, lent_b)):
        out[...] = join3(dot(pieces, one_hot(picked_row(picks, row), values.shape[1])))


def lend_channels(values, picks, lent_a, lent_b):
    for row, out in ((0, lent_a), (1, lent_b)):
        out[...] = dot(values, one_hot(picked_row(picks, row), values.shape[1])).astype(BF16)


def sweep(site, w3, w5, fixed, dipoles, entry, moment):
    width = site.shape[1]
    moment[...] = dipoles.T
    tx, ty, tz = site[0:1, :], site[1:2, :], site[2:3, :]

    def some_rows(j, acc):
        start = pl.multiple_of(j * SWEEP_CHUNK, SWEEP_CHUNK)
        cols, d = entry[pl.ds(start, SWEEP_CHUNK), :], moment[pl.ds(start, SWEEP_CHUNK), :]
        rx, ry, rz = tx - cols[:, 0:1], ty - cols[:, 1:2], tz - cols[:, 2:3]
        dx, dy, dz = d[:, 0:1], d[:, 1:2], d[:, 2:3]
        cube = w3[pl.ds(start, SWEEP_CHUNK), :]
        scale = (rx * dx + ry * dy + rz * dz) * w5[pl.ds(start, SWEEP_CHUNK), :]
        return (
            acc[0] + (rx * scale - dx * cube),
            acc[1] + (ry * scale - dy * cube),
            acc[2] + (rz * scale - dz * cube),
        )

    nil = jnp.zeros((SWEEP_CHUNK, width), F32)
    sums = lax.fori_loop(0, w3.shape[0] // SWEEP_CHUNK, some_rows, (nil, nil, nil), unroll=SWEEP_UNROLL)
    return site[4:5, :] * (fixed + rows([jnp.sum(s, axis=0, keepdims=True) for s in sums]))


def message(layer, hidden, table, third, out_t, node_t, slots, total):
    slot_count = slots.shape[0]
    width = slots.shape[1]
    together = MESSAGE_SLOTS[layer]
    step = together * width
    total[...] = jnp.zeros_like(total)

    def some_slots(k, carry):
        row = slot_row(slots, k * together, together)
        picked = dot(table, one_hot(row, table.shape[1]))
        start = pl.multiple_of(k * step, step)
        weight = dot(out_t, third[layer * 64 : layer * 64 + 64, pl.ds(start, step)])
        product = weight * picked
        part = product[:, 0:width]
        for i in range(1, together):
            part = part + product[:, i * width : (i + 1) * width]
        total[...] += part
        return carry

    lax.fori_loop(0, slot_count // together, some_slots, 0)
    mean = (total[...] * (1.0 / slot_count)).astype(BF16)
    return (hidden.astype(F32) + silu(dot(node_t, mean))).astype(BF16)


def charge_field(target, cols, first, count):
    tx, ty, tz = target[0:1, :], target[1:2, :], target[2:3, :]

    def some_rows(j, acc):
        c = cols[pl.ds(pl.multiple_of(first + j * FIELD_CHUNK, FIELD_CHUNK), FIELD_CHUNK), :]
        rx, ry, rz = tx - c[:, 0:1], ty - c[:, 1:2], tz - c[:, 2:3]
        inverse = lax.rsqrt(rx * rx + ry * ry + rz * rz + SMOOTH)
        scale = c[:, 3:4] * (inverse * inverse * inverse)
        return acc[0] + rx * scale, acc[1] + ry * scale, acc[2] + rz * scale

    nil = jnp.zeros((FIELD_CHUNK, target.shape[1]), F32)
    sums = lax.fori_loop(0, count // FIELD_CHUNK, some_rows, (nil, nil, nil), unroll=FIELD_UNROLL)
    return jnp.concatenate([jnp.sum(s, axis=0, keepdims=True) for s in sums], axis=0)


def first_kernel(
    pack, rim_a, rim_b, feat_t, side_a, side_b, w3, w5, fixed, entry,
    near_far, third_far, node_in_far, node_out_far, w_out_far, gain_far,
    outside_row, near_own, hidden_out, lifted_out, fixed_out, dipole_out, lent_a, lent_b,
    near, cols, third, node_in, node_out, w_out, gain, total, moment, done,
):
    site, slots, picks = views(pack)
    width = site.shape[1]
    listed = near_own.shape[0]
    numbers = [listed_block(row[5:6, 0:128], l) for row in (site, rim_a, rim_b) for l in range(listed)]
    fetch([(near_far.at[b], near.at[i]) for i, b in enumerate(numbers)], done, 5)
    weights = (
        (third_far, third), (node_in_far, node_in), (node_out_far.at[0], node_out),
        (w_out_far.at[0], w_out), (gain_far, gain),
    )

    @pl.when(learned())
    def _():
        fetch(weights, done)

    for i, b in enumerate(numbers):
        pltpu.make_async_copy(near_far.at[b], near.at[i], done.at[5 + i]).wait()
    near_own[...] = near[0:listed]
    for i in range(3 * listed):
        tile = near[i]
        cols[i * 128 : i * 128 + 128, :] = jnp.concatenate([tile, tile], axis=0).T
    reach = listed * 128
    own_field = charge_field(site[...], cols, 0, reach)
    field = jnp.concatenate(
        [own_field, charge_field(rim_a[...], cols, reach, reach), charge_field(rim_b[...], cols, 2 * reach, reach)],
        axis=1,
    )
    strength = jnp.sqrt(1.0 + (field[0:1] * field[0:1] + field[1:2] * field[1:2] + field[2:3] * field[2:3]))
    outside_row[...] = jnp.broadcast_to(strength[:, :width], outside_row.shape)

    @pl.when(learned())
    def _():
        for i, (a, b) in enumerate(weights):
            pltpu.make_async_copy(a, b, done.at[i]).wait()
        gain_col = jnp.broadcast_to(gain[...], (8, width)).T
        features = jnp.concatenate([feat_t[...], side_a[...], side_b[...]], axis=1)
        start = (features.astype(F32) + gain_col[:, 0:1] * strength).astype(BF16)
        present = jnp.concatenate([jnp.ones((1, width), F32), rim_a[6:7, :], rim_b[6:7, :]], axis=1)
        raised = dot(flip(node_in[0]).astype(BF16), start)
        table = jnp.where(present > 0.5, raised, 0.0).astype(BF16)
        out_t, node_t = flip(w_out[...]).astype(BF16), flip(node_out[...]).astype(BF16)
        new = message(0, start[:, :width], table, third, out_t, node_t, slots, total)
        hidden_out[...] = new
        raised = dot(flip(node_in[1]).astype(BF16), new).astype(BF16)
        lifted_out[...] = raised
        lend_channels(raised, picks, lent_a, lent_b)

    @pl.when(jnp.logical_not(learned()))
    def _():
        known = [fixed[...], join3(side_a[0:24, :].astype(F32)), join3(side_b[0:24, :].astype(F32))]
        whole = jnp.concatenate(known, axis=1) + rows([field])
        fixed_out[...] = whole[:, :width]
        polar = jnp.concatenate([site[4:5, :], rim_a[4:5, :], rim_b[4:5, :]], axis=1)
        new = sweep(site, w3, w5, whole[:, :width], polar * whole, entry, moment)
        dipole_out[...] = new
        lend_pieces(new, picks, lent_a, lent_b)


def second_kernel(
    hidden, lifted, side_a, side_b, pack, w3, w5, fixed, dipole, entry,
    third_far, node_out_far, w_out_far, readout_far,
    charge, dipole_out, small_a, small_b,
    third, node_out, w_out, readout, total, moment, done,
):
    site, slots, picks = views(pack)

    @pl.when(learned())
    def _():
        fetch(
            ((third_far, third), (node_out_far.at[1], node_out), (w_out_far.at[1], w_out), (readout_far, readout)), done
        )()
        table = jnp.concatenate([lifted[...], side_a[...], side_b[...]], axis=1)
        out_t, node_t = flip(w_out[...]).astype(BF16), flip(node_out[...]).astype(BF16)
        new = message(1, hidden[...], table, third, out_t, node_t, slots, total)
        charge[...] = dot(rows([readout[...].astype(F32)]).astype(BF16), new)

    @pl.when(jnp.logical_not(learned()))
    def _():
        sides = [join3(side_a[0:24, :].astype(F32)), join3(side_b[0:24, :].astype(F32))]
        table = jnp.concatenate([dipole[...]] + sides, axis=1)
        new = sweep(site, w3, w5, fixed[...], table, entry, moment)
        dipole_out[...] = new
        lend_whole(new, picks, small_a, small_b)


def third_kernel(side_a, side_b, pack, w3, w5, fixed, dipole, entry, dipole_out, small_a, small_b, moment):
    site, _, picks = views(pack)

    @pl.when(jnp.logical_not(learned()))
    def _():
        table = jnp.concatenate([dipole[...], side_a[...], side_b[...]], axis=1)
        new = sweep(site, w3, w5, fixed[...], table, entry, moment)
        dipole_out[...] = new
        lend_whole(new, picks, small_a, small_b)


def response_kernel(
    near, pack, charge, outside_row, side_a, side_b, w3, w5, fixed, dipole, entry,
    result, spread, cols, moment, term,
):
    site = views(pack)[0]
    width = site.shape[1]
    listed = near.shape[0]
    blocks = [listed_block(site[5:6, 0:128], l) for l in range(listed)]
    spread[...] = jnp.zeros_like(spread)
    term[...] = jnp.zeros_like(term)

    def terms(dipoles):
        for l in range(listed):
            tile = near[l]
            tx, ty, tz = tile[0:1, :], tile[1:2, :], tile[2:3, :]

            def some_rows(j, acc):
                start = pl.multiple_of(j * TERM_CHUNK, TERM_CHUNK)
                c = cols[pl.ds(start, TERM_CHUNK), :]
                rx, ry, rz = tx - c[:, 0:1], ty - c[:, 1:2], tz - c[:, 2:3]
                inverse = lax.rsqrt(rx * rx + ry * ry + rz * rz + SMOOTH)
                squared = inverse * inverse
                cube = squared * inverse
                if dipoles:
                    dx, dy, dz = c[:, 4:5], c[:, 5:6], c[:, 6:7]
                    scale = (rx * dx + ry * dy + rz * dz) * (3.0 * (cube * squared))
                    return (
                        acc[0] + (rx * scale - dx * cube),
                        acc[1] + (ry * scale - dy * cube),
                        acc[2] + (rz * scale - dz * cube),
                    )
                scale = c[:, 3:4] * cube
                return acc[0] + rx * scale, acc[1] + ry * scale, acc[2] + rz * scale

            nil = jnp.zeros((TERM_CHUNK, 128), F32)
            sums = lax.fori_loop(0, width // TERM_CHUNK, some_rows, (nil, nil, nil), unroll=TERM_UNROLL)
            for axis in range(3):
                term[l, axis : axis + 1, :] = jnp.sum(sums[axis], axis=0, keepdims=True)

    @pl.when(learned())
    def _():
        q = charge[...]
        result[...] = jnp.concatenate([q[0:2], outside_row[0:1, :]], axis=0)
        cols[...] = rows([site[0:3, :], q[0:1]]).T
        terms(False)

    @pl.when(jnp.logical_not(learned()))
    def _():
        table = jnp.concatenate([dipole[...], side_a[...], side_b[...]], axis=1)
        new = sweep(site, w3, w5, fixed[...], table, entry, moment)
        result[...] = new[0:3]
        cols[...] = rows([site[0:4, :], new[0:3]]).T
        terms(True)

    side = lax.broadcasted_iota(jnp.int32, (2, 128), 0)
    for l in range(listed):
        owner, part = blocks[l] >> 1, blocks[l] & 1
        for axis in range(3):
            spread[3 * owner + axis] += jnp.where(side == part, term[l, axis : axis + 1, :], 0.0)


def gather_kernel(pieces, share):
    total = jnp.sum(pieces[...], axis=0)
    share[...] = jnp.concatenate(
        [jnp.concatenate([total[axis, 0:1], total[axis, 1:2]], axis=1) for axis in range(3)], axis=0
    )


def finish_kernel(result, share, result_far, share_far, done):
    fetch(((result, result_far), (share, share_far)), done)()


def placed(block):
    y_half, plane, step, side = block // 64, block // 8 % 8, block // 2 % 4, block % 2
    x = 3 - step if plane % 2 else step
    z = (plane - 1) % 8 if y_half else plane
    along = 1 - side if (step + y_half) % 2 == 0 else side
    y = 2 * y_half + along
    return ((y % 2 * 8 + z) * 4 + x) * 2 + y // 2


def local(
    positions, charges, polar, features, neighbours, send_rows, blocks,
    radial_in, radial_mid, radial_out, node_in, node_out, field_gain, readout,
):
    width = positions.shape[1]
    slot_count = neighbours.shape[1]
    depth = 2 * width
    half = send_rows.shape[1]
    channels = features.shape[1]
    listed = blocks.shape[0]
    members = lax.axis_size(DOM)
    near_pairs = [(i, i ^ 1) for i in range(members)]
    far_pairs = [(i, ((i - 1) ^ 1) + 1) for i in range(1, members - 1)]
    same = list(range(members))
    place = [placed(i) for i in range(members)]

    def move(value, pairs, source, target, groups=(0, 1)):
        return lax.ppermute(
            value, EVERY, [(source[a] + g * members, target[b] + g * members) for g in groups for a, b in pairs]
        )

    def trade(a, b, groups=(0, 1), source=place):
        return move(a, near_pairs, source, place, groups), move(b, far_pairs, source, place, groups)

    row8, table8 = ((8, width), F32), ((8, half), F32)
    wide = ((channels, half), BF16)
    by_site = ((channels, width), BF16)
    ints = jnp.int32
    itself = [(i, i) for i in range(members)]
    pack, mine, lent_a, lent_b = call(
        rows_kernel, [((slot_count + 16, width), F32), ((2, 4, half), F32), table8, table8],
        (), (positions, charges[None], polar[None], neighbours.T, send_rows, blocks),
        [pltpu.VMEM((3, width), F32), pltpu.VMEM((1, width), F32), pltpu.VMEM((1, width), F32),
         pltpu.VMEM((slot_count, width), ints), pltpu.VMEM((2, half), ints), pltpu.SMEM((listed,), ints)], 6,
    )
    partner = lax.ppermute(mine, "grp", [(0, 1), (1, 0)])
    copies = jnp.broadcast_to(partner[None], (members,) + partner.shape)
    near = lax.all_to_all(copies, DOM, 0, 0, tiled=True).reshape(2 * members, 4, half)
    pack = move(pack, itself, same, place)
    rim_a, rim_b = trade(lent_a, lent_b, source=same)
    features = move(features, itself, same, place, (0,))
    feat_t, w3, w5, fixed, entry, lent_a, lent_b = call(
        static_kernel, [by_site, ((depth, width), F32), ((depth, width), F32), row8, ((depth, 8), F32), wide, wide],
        (pack, rim_a, rim_b), (features,), [pltpu.VMEM((width, channels), BF16)], 1, loose=1,
    )
    side_a, side_b = trade(lent_a, lent_b)
    third_shape = (LAYERS * radial_in.shape[2], slot_count * width)
    (third,) = call(
        radial_kernel, [(third_shape, BF16)], (pack, rim_a, rim_b), (radial_in, radial_mid),
        [pltpu.VMEM(radial_in.shape, BF16), pltpu.VMEM(radial_mid.shape, BF16), pltpu.VMEM(third_shape, BF16)],
        2 + slot_count // RADIAL_SLOTS, 1,
    )
    moment = pltpu.VMEM((depth, 8), F32)
    total = pltpu.VMEM((channels, width), F32)
    square = pltpu.VMEM(node_out.shape[1:], BF16)
    last = pltpu.VMEM(radial_out.shape[1:], BF16)
    outside_row, near_own, hidden, lifted, fixed_all, dipole, lent_a, lent_b = call(
        first_kernel, [row8, ((listed, 4, half), F32), by_site, by_site, row8, row8, wide, wide],
        (pack, rim_a, rim_b, feat_t, side_a, side_b, w3, w5, fixed, entry),
        (near, third, node_in, node_out, radial_out, field_gain[None]),
        [pltpu.VMEM((3 * listed, 4, half), F32), pltpu.VMEM((3 * listed * half, 8), F32),
         pltpu.VMEM(third_shape, BF16), pltpu.VMEM(node_in.shape, BF16), square, last,
         pltpu.VMEM((1, channels), F32), total, moment], 5 + 3 * listed, loose=1,
    )
    side_a, side_b = trade(lent_a, lent_b)
    charge, dipole, small_a, small_b = call(
        second_kernel, [row8, row8, table8, table8],
        (hidden, lifted, side_a, side_b, pack, w3, w5, fixed_all, dipole, entry),
        (third, node_out, radial_out, readout.T),
        [pltpu.VMEM(third_shape, BF16), square, last, pltpu.VMEM((2, channels), BF16), total, moment], 4,
    )
    side_a, side_b = trade(small_a, small_b, (1,))
    dipole, small_a, small_b = call(
        third_kernel, [row8, table8, table8], (side_a, side_b, pack, w3, w5, fixed_all, dipole, entry),
        (), [moment],
    )
    side_a, side_b = trade(small_a, small_b, (1,))
    result, spread = call(
        response_kernel, [((3, width), F32), ((3 * members, 2, half), F32)],
        (near_own, pack, charge, outside_row, side_a, side_b, w3, w5, fixed_all, dipole, entry), (),
        [pltpu.VMEM((width, 8), F32), moment, pltpu.VMEM((listed, 4, half), F32)],
    )
    pieces = lax.all_to_all(spread, DOM, 0, 0, tiled=True).reshape(members, 3, 2, half)
    (share,) = call(gather_kernel, [((3, width), F32)], (pieces,))
    result = move(result, itself, place, same)
    share = lax.ppermute(share, "grp", [(0, 1), (1, 0)])
    whole = ((3, width), F32)
    return tuple(call(finish_kernel, [whole, whole], (result, share), copies=2, far_outs=2))


def solution(mesh):
    sites = P(None, EVERY)
    in_specs = (sites, P(EVERY), P(EVERY), P(EVERY, None), P(EVERY, None), sites, P(EVERY)) + (P(),) * 7
    return jax.shard_map(local, mesh=mesh, in_specs=in_specs, out_specs=(sites, sites), check_vma=False)
```

```python
import jax
import jax.numpy as jnp
from jax import lax
from jax.experimental import pallas as pl
from jax.experimental.pallas import tpu as pltpu
from jax.sharding import PartitionSpec as P

BASIS = 8
LAYERS = 2
SMOOTH = 1.0
SPACING = 0.75
DOM = ("dom", "sub")
EVERY = ("grp", "dom", "sub")
F32 = jnp.float32
BF16 = jnp.bfloat16
VMEM = pl.BlockSpec(memory_space=pltpu.VMEM)
ANY = pl.BlockSpec(memory_space=pl.ANY)
SWEEP_CHUNK, SWEEP_UNROLL = 32, 16
FIELD_CHUNK, FIELD_UNROLL = 32, 16
TERM_CHUNK, TERM_UNROLL = 64, 4
STATIC_CHUNK = 64
RADIAL_SLOTS = 8
MESSAGE_SLOTS = (8, 16)


def call(body, outs, held, far=(), scratch=(), copies=0, far_outs=0, loose=0):
    return pl.pallas_call(
        body,
        out_shape=[jax.ShapeDtypeStruct(s, d) for s, d in outs[: len(outs) - far_outs]]
        + [pltpu.HBM(s, d) for s, d in outs[len(outs) - far_outs :]],
        in_specs=[VMEM] * len(held) + [ANY] * len(far),
        out_specs=[VMEM] * (len(outs) - far_outs) + [ANY] * far_outs,
        scratch_shapes=list(scratch) + ([pltpu.SemaphoreType.DMA((copies,))] if copies else []),
        compiler_params=pltpu.CompilerParams(vmem_limit_bytes=24 * 2**20),
    )(*held, *far[:loose], *[pltpu.with_memory_space_constraint(a, pltpu.HBM) for a in far[loose:]])


def fetch(pairs, done, first=0):
    copies = [pltpu.make_async_copy(a, b, done.at[first + i]) for i, (a, b) in enumerate(pairs)]
    for c in copies:
        c.start()

    def wait():
        for c in copies:
            c.wait()

    return wait


def learned():
    return lax.axis_index("grp") == 0


def dot(a, b):
    return jnp.dot(a, b, preferred_element_type=F32)


def silu(x):
    half = 0.5 * x
    return half + half * jnp.tanh(half)


def flip(x):
    return x.astype(F32).T


def split3(x):
    high = x.astype(BF16)
    rest = x - high.astype(F32)
    mid = rest.astype(BF16)
    low = (rest - mid.astype(F32)).astype(BF16)
    return jnp.concatenate([high, mid, low], axis=0)


def join3(x):
    return x[0:8] + x[8:16] + x[16:24]


def one_hot(row, depth):
    ids = lax.broadcasted_iota(jnp.int32, (depth, row.shape[1]), 0)
    return jnp.where(ids == row.astype(jnp.int32), 1.0, 0.0).astype(BF16)


def views(pack):
    return pack.at[0:8, :], pack.at[8:40, :], pack.at[40:41, :]


def picked_row(picks, row):
    return picks[0:1, row * 128 : row * 128 + 128]


def listed_block(row, l):
    lane = lax.broadcasted_iota(jnp.int32, row.shape, 1)
    return jnp.sum(jnp.where(lane == l, row, 0.0)).astype(jnp.int32)


def slot_row(slots, first, count):
    return jnp.concatenate([slots[pl.ds(first + i, 1), :] for i in range(count)], axis=1)


def rows(parts, count=8):
    have = sum(p.shape[0] for p in parts)
    return jnp.concatenate(list(parts) + [jnp.zeros((count - have, parts[0].shape[1]), F32)], axis=0)


def rows_kernel(
    pos_far, charge_far, polar_far, table_far, send_far, blocks_far,
    pack, mine, lent_a, lent_b,
    pos, charge, polar, table, send, blocks, done,
):
    pairs = ((pos_far, pos), (charge_far, charge), (polar_far, polar), (table_far, table), (send_far, send))
    wait = fetch(pairs + ((blocks_far, blocks),), done)
    odd = lax.axis_index("sub")
    width = pos.shape[1]
    wait()
    lane = lax.broadcasted_iota(jnp.int32, (1, width), 1)
    listed = jnp.zeros((1, width), jnp.int32)
    for l in range(blocks.shape[0]):
        listed = jnp.where(lane == l, blocks[l], listed)
    listed = listed.astype(F32)
    sites = rows([pos[...], charge[...], polar[...], listed, jnp.ones((1, width), F32)])
    for half in range(2):
        mine[half] = sites[0:4, half * 128 : half * 128 + 128]
    first, second = send[0:1, :], send[1:2, :]
    swap = jnp.full(first.shape, odd, jnp.int32) == 1
    picks = jnp.where(swap, second, first), jnp.where(swap, first, second)
    raw = table[...]
    other = jnp.where((raw >= 256) & (raw < 512), jnp.bitwise_xor(raw, 128), raw)
    keep = jnp.full(raw.shape, odd, jnp.int32) == 1
    pack[0:8, :] = sites
    pack[8:40, :] = jnp.where(keep, raw, other).astype(F32)
    pack[40:48, :] = rows([jnp.concatenate(picks, axis=1).astype(F32)])
    pieces = split3(sites)
    for row, out in zip(picks, (lent_a, lent_b)):
        found = join3(dot(pieces, one_hot(row, width)))
        out[...] = rows([found[0:5], listed[:, 0:128], jnp.ones((1, 128), F32)])


def static_kernel(
    pack, rim_a, rim_b, features_far,
    feat_t, w3, w5, fixed, entry, lent_a, lent_b, features, done,
):
    site, slots, picks = views(pack)
    width = site.shape[1]
    depth = 2 * width
    slot_count = slots.shape[0]

    @pl.when(learned())
    def _():
        fetch(((features_far, features),), done)()
        flipped = flip(features[...]).astype(BF16)
        feat_t[...] = flipped
        lend_channels(flipped, picks, lent_a, lent_b)

    @pl.when(jnp.logical_not(learned()))
    def _():
        table = jnp.concatenate([site[...], rim_a[...], rim_b[...]], axis=1)
        entry[...] = table.T
        tx, ty, tz = site[0:1, :], site[1:2, :], site[2:3, :]

        def some_rows(j, acc):
            start = pl.multiple_of(j * STATIC_CHUNK, STATIC_CHUNK)
            ids = (lax.broadcasted_iota(jnp.int32, (STATIC_CHUNK, width), 0) + start).astype(F32)
            count = jnp.zeros((STATIC_CHUNK, width), F32)
            for k in range(slot_count):
                count = count + jnp.where(ids == slots[k : k + 1, :], 1.0, 0.0)
            cols = entry[pl.ds(start, STATIC_CHUNK), :]
            rx, ry, rz = tx - cols[:, 0:1], ty - cols[:, 1:2], tz - cols[:, 2:3]
            inverse = lax.rsqrt(rx * rx + ry * ry + rz * rz + SMOOTH)
            squared = inverse * inverse
            cube = count * (squared * inverse)
            w3[pl.ds(start, STATIC_CHUNK), :] = cube
            w5[pl.ds(start, STATIC_CHUNK), :] = 3.0 * (cube * squared)
            scale = cols[:, 3:4] * cube
            return acc[0] + rx * scale, acc[1] + ry * scale, acc[2] + rz * scale

        nil = jnp.zeros((STATIC_CHUNK, width), F32)
        sums = lax.fori_loop(0, depth // STATIC_CHUNK, some_rows, (nil, nil, nil))
        total = rows([jnp.sum(s, axis=0, keepdims=True) for s in sums])
        fixed[...] = total
        lend_pieces(total, picks, lent_a, lent_b)


def radial_kernel(
    pack, rim_a, rim_b, w_in_far, w_mid_far,
    third_far, w_in, w_mid, third, done,
):
    site, slots, _ = views(pack)
    width = site.shape[1]
    depth = 2 * width
    slot_count = slots.shape[0]

    @pl.when(learned())
    def _():
        wait = fetch(((w_in_far, w_in), (w_mid_far, w_mid)), done)
        pieces = split3(jnp.concatenate([site[...], rim_a[...], rim_b[...]], axis=1))
        step = RADIAL_SLOTS * width
        here = jnp.concatenate([site[...]] * RADIAL_SLOTS, axis=1)
        centres = lax.broadcasted_iota(jnp.int32, (BASIS, step), 0).astype(F32) * SPACING
        wait()
        first_w = jnp.concatenate([flip(w_in[0]), flip(w_in[1])], axis=0).astype(BF16)
        zero = jnp.zeros((64, 64), F32)

        def both(level):
            top = jnp.concatenate([flip(w_mid[0, level]), zero], axis=1)
            bottom = jnp.concatenate([zero, flip(w_mid[1, level])], axis=1)
            return jnp.concatenate([top, bottom], axis=0).astype(BF16)

        second_w, third_w = both(0), both(1)

        def part_out(k):
            part = pl.ds(pl.multiple_of(k * step, step), step)
            return pltpu.make_async_copy(third.at[:, part], third_far.at[:, part], done.at[2 + k])

        def some_slots(k, carry):
            found = join3(dot(pieces, one_hot(slot_row(slots, k * RADIAL_SLOTS, RADIAL_SLOTS), depth)))
            offset = here - found
            squares = offset * offset
            dist_sq = squares[0:1] + squares[1:2] + squares[2:3] + SMOOTH
            gap = jnp.sqrt(dist_sq) - centres
            basis = jnp.exp(-(gap * gap)).astype(BF16)
            hidden = silu(dot(first_w, basis)).astype(BF16)
            hidden = silu(dot(second_w, hidden)).astype(BF16)
            start = pl.multiple_of(k * step, step)
            third[:, pl.ds(start, step)] = silu(dot(third_w, hidden)).astype(BF16)
            part_out(k).start()
            return carry

        lax.fori_loop(0, slot_count // RADIAL_SLOTS, some_slots, 0)
        for k in range(slot_count // RADIAL_SLOTS):
            part_out(k).wait()


def lend_pieces(values, picks, lent_a, lent_b):
    pieces = split3(values)
    for row, out in ((0, lent_a), (1, lent_b)):
        found = dot(pieces, one_hot(picked_row(picks, row), values.shape[1]))
        out[...] = jnp.zeros_like(out)
        out[0:32, :] = rows([found], 32).astype(BF16)


def lend_whole(values, picks, lent_a, lent_b):
    pieces = split3(values)
    for row, out in ((0, lent_a), (1, lent_b)):
        out[...] = join3(dot(pieces, one_hot(picked_row(picks, row), values.shape[1])))


def lend_channels(values, picks, lent_a, lent_b):
    for row, out in ((0, lent_a), (1, lent_b)):
        out[...] = dot(values, one_hot(picked_row(picks, row), values.shape[1])).astype(BF16)


def sweep(site, w3, w5, fixed, dipoles, entry, moment):
    width = site.shape[1]
    moment[...] = dipoles.T
    tx, ty, tz = site[0:1, :], site[1:2, :], site[2:3, :]

    def some_rows(j, acc):
        start = pl.multiple_of(j * SWEEP_CHUNK, SWEEP_CHUNK)
        cols, d = entry[pl.ds(start, SWEEP_CHUNK), :], moment[pl.ds(start, SWEEP_CHUNK), :]
        rx, ry, rz = tx - cols[:, 0:1], ty - cols[:, 1:2], tz - cols[:, 2:3]
        dx, dy, dz = d[:, 0:1], d[:, 1:2], d[:, 2:3]
        cube = w3[pl.ds(start, SWEEP_CHUNK), :]
        scale = (rx * dx + ry * dy + rz * dz) * w5[pl.ds(start, SWEEP_CHUNK), :]
        return (
            acc[0] + (rx * scale - dx * cube),
            acc[1] + (ry * scale - dy * cube),
            acc[2] + (rz * scale - dz * cube),
        )

    nil = jnp.zeros((SWEEP_CHUNK, width), F32)
    sums = lax.fori_loop(0, w3.shape[0] // SWEEP_CHUNK, some_rows, (nil, nil, nil), unroll=SWEEP_UNROLL)
    return site[4:5, :] * (fixed + rows([jnp.sum(s, axis=0, keepdims=True) for s in sums]))


def message(layer, hidden, table, third, out_t, node_t, slots, total):
    slot_count = slots.shape[0]
    width = slots.shape[1]
    together = MESSAGE_SLOTS[layer]
    step = together * width
    total[...] = jnp.zeros_like(total)

    def some_slots(k, carry):
        row = slot_row(slots, k * together, together)
        picked = dot(table, one_hot(row, table.shape[1]))
        start = pl.multiple_of(k * step, step)
        weight = dot(out_t, third[layer * 64 : layer * 64 + 64, pl.ds(start, step)])
        product = weight * picked
        part = product[:, 0:width]
        for i in range(1, together):
            part = part + product[:, i * width : (i + 1) * width]
        total[...] += part
        return carry

    lax.fori_loop(0, slot_count // together, some_slots, 0)
    mean = (total[...] * (1.0 / slot_count)).astype(BF16)
    return (hidden.astype(F32) + silu(dot(node_t, mean))).astype(BF16)


def charge_field(target, cols, first, count):
    tx, ty, tz = target[0:1, :], target[1:2, :], target[2:3, :]

    def some_rows(j, acc):
        c = cols[pl.ds(pl.multiple_of(first + j * FIELD_CHUNK, FIELD_CHUNK), FIELD_CHUNK), :]
        rx, ry, rz = tx - c[:, 0:1], ty - c[:, 1:2], tz - c[:, 2:3]
        inverse = lax.rsqrt(rx * rx + ry * ry + rz * rz + SMOOTH)
        scale = c[:, 3:4] * (inverse * inverse * inverse)
        return acc[0] + rx * scale, acc[1] + ry * scale, acc[2] + rz * scale

    nil = jnp.zeros((FIELD_CHUNK, target.shape[1]), F32)
    sums = lax.fori_loop(0, count // FIELD_CHUNK, some_rows, (nil, nil, nil), unroll=FIELD_UNROLL)
    return jnp.concatenate([jnp.sum(s, axis=0, keepdims=True) for s in sums], axis=0)


def first_kernel(
    pack, rim_a, rim_b, feat_t, side_a, side_b, w3, w5, fixed, entry,
    near_far, third_far, node_in_far, node_out_far, w_out_far, gain_far,
    outside_row, near_own, hidden_out, lifted_out, fixed_out, dipole_out, lent_a, lent_b,
    near, cols, third, node_in, node_out, w_out, gain, total, moment, done,
):
    site, slots, picks = views(pack)
    width = site.shape[1]
    listed = near_own.shape[0]
    numbers = [listed_block(row[5:6, 0:128], l) for row in (site, rim_a, rim_b) for l in range(listed)]
    fetch([(near_far.at[b], near.at[i]) for i, b in enumerate(numbers)], done, 5)
    weights = (
        (third_far, third), (node_in_far, node_in), (node_out_far.at[0], node_out),
        (w_out_far.at[0], w_out), (gain_far, gain),
    )

    @pl.when(learned())
    def _():
        fetch(weights, done)

    for i, b in enumerate(numbers):
        pltpu.make_async_copy(near_far.at[b], near.at[i], done.at[5 + i]).wait()
    near_own[...] = near[0:listed]
    for i in range(3 * listed):
        tile = near[i]
        cols[i * 128 : i * 128 + 128, :] = jnp.concatenate([tile, tile], axis=0).T
    reach = listed * 128
    own_field = charge_field(site[...], cols, 0, reach)
    field = jnp.concatenate(
        [own_field, charge_field(rim_a[...], cols, reach, reach), charge_field(rim_b[...], cols, 2 * reach, reach)],
        axis=1,
    )
    strength = jnp.sqrt(1.0 + (field[0:1] * field[0:1] + field[1:2] * field[1:2] + field[2:3] * field[2:3]))
    outside_row[...] = jnp.broadcast_to(strength[:, :width], outside_row.shape)

    @pl.when(learned())
    def _():
        for i, (a, b) in enumerate(weights):
            pltpu.make_async_copy(a, b, done.at[i]).wait()
        gain_col = jnp.broadcast_to(gain[...], (8, width)).T
        features = jnp.concatenate([feat_t[...], side_a[...], side_b[...]], axis=1)
        start = (features.astype(F32) + gain_col[:, 0:1] * strength).astype(BF16)
        present = jnp.concatenate([jnp.ones((1, width), F32), rim_a[6:7, :], rim_b[6:7, :]], axis=1)
        raised = dot(flip(node_in[0]).astype(BF16), start)
        table = jnp.where(present > 0.5, raised, 0.0).astype(BF16)
        out_t, node_t = flip(w_out[...]).astype(BF16), flip(node_out[...]).astype(BF16)
        new = message(0, start[:, :width], table, third, out_t, node_t, slots, total)
        hidden_out[...] = new
        raised = dot(flip(node_in[1]).astype(BF16), new).astype(BF16)
        lifted_out[...] = raised
        lend_channels(raised, picks, lent_a, lent_b)

    @pl.when(jnp.logical_not(learned()))
    def _():
        known = [fixed[...], join3(side_a[0:24, :].astype(F32)), join3(side_b[0:24, :].astype(F32))]
        whole = jnp.concatenate(known, axis=1) + rows([field])
        fixed_out[...] = whole[:, :width]
        polar = jnp.concatenate([site[4:5, :], rim_a[4:5, :], rim_b[4:5, :]], axis=1)
        new = sweep(site, w3, w5, whole[:, :width], polar * whole, entry, moment)
        dipole_out[...] = new
        lend_pieces(new, picks, lent_a, lent_b)


def second_kernel(
    hidden, lifted, side_a, side_b, pack, w3, w5, fixed, dipole, entry,
    third_far, node_out_far, w_out_far, readout_far,
    charge, dipole_out, small_a, small_b,
    third, node_out, w_out, readout, total, moment, done,
):
    site, slots, picks = views(pack)

    @pl.when(learned())
    def _():
        fetch(
            ((third_far, third), (node_out_far.at[1], node_out), (w_out_far.at[1], w_out), (readout_far, readout)), done
        )()
        table = jnp.concatenate([lifted[...], side_a[...], side_b[...]], axis=1)
        out_t, node_t = flip(w_out[...]).astype(BF16), flip(node_out[...]).astype(BF16)
        new = message(1, hidden[...], table, third, out_t, node_t, slots, total)
        charge[...] = dot(rows([readout[...].astype(F32)]).astype(BF16), new)

    @pl.when(jnp.logical_not(learned()))
    def _():
        sides = [join3(side_a[0:24, :].astype(F32)), join3(side_b[0:24, :].astype(F32))]
        table = jnp.concatenate([dipole[...]] + sides, axis=1)
        new = sweep(site, w3, w5, fixed[...], table, entry, moment)
        dipole_out[...] = new
        lend_whole(new, picks, small_a, small_b)


def third_kernel(side_a, side_b, pack, w3, w5, fixed, dipole, entry, dipole_out, small_a, small_b, moment):
    site, _, picks = views(pack)

    @pl.when(jnp.logical_not(learned()))
    def _():
        table = jnp.concatenate([dipole[...], side_a[...], side_b[...]], axis=1)
        new = sweep(site, w3, w5, fixed[...], table, entry, moment)
        dipole_out[...] = new
        lend_whole(new, picks, small_a, small_b)


def response_kernel(
    near, pack, charge, outside_row, side_a, side_b, w3, w5, fixed, dipole, entry,
    result, spread, cols, moment, term,
):
    site = views(pack)[0]
    width = site.shape[1]
    listed = near.shape[0]
    blocks = [listed_block(site[5:6, 0:128], l) for l in range(listed)]
    spread[...] = jnp.zeros_like(spread)
    term[...] = jnp.zeros_like(term)

    def terms(dipoles):
        for l in range(listed):
            tile = near[l]
            tx, ty, tz = tile[0:1, :], tile[1:2, :], tile[2:3, :]

            def some_rows(j, acc):
                start = pl.multiple_of(j * TERM_CHUNK, TERM_CHUNK)
                c = cols[pl.ds(start, TERM_CHUNK), :]
                rx, ry, rz = tx - c[:, 0:1], ty - c[:, 1:2], tz - c[:, 2:3]
                inverse = lax.rsqrt(rx * rx + ry * ry + rz * rz + SMOOTH)
                squared = inverse * inverse
                cube = squared * inverse
                if dipoles:
                    dx, dy, dz = c[:, 4:5], c[:, 5:6], c[:, 6:7]
                    scale = (rx * dx + ry * dy + rz * dz) * (3.0 * (cube * squared))
                    return (
                        acc[0] + (rx * scale - dx * cube),
                        acc[1] + (ry * scale - dy * cube),
                        acc[2] + (rz * scale - dz * cube),
                    )
                scale = c[:, 3:4] * cube
                return acc[0] + rx * scale, acc[1] + ry * scale, acc[2] + rz * scale

            nil = jnp.zeros((TERM_CHUNK, 128), F32)
            sums = lax.fori_loop(0, width // TERM_CHUNK, some_rows, (nil, nil, nil), unroll=TERM_UNROLL)
            for axis in range(3):
                term[l, axis : axis + 1, :] = jnp.sum(sums[axis], axis=0, keepdims=True)

    @pl.when(learned())
    def _():
        q = charge[...]
        result[...] = jnp.concatenate([q[0:2], outside_row[0:1, :]], axis=0)
        cols[...] = rows([site[0:3, :], q[0:1]]).T
        terms(False)

    @pl.when(jnp.logical_not(learned()))
    def _():
        table = jnp.concatenate([dipole[...], side_a[...], side_b[...]], axis=1)
        new = sweep(site, w3, w5, fixed[...], table, entry, moment)
        result[...] = new[0:3]
        cols[...] = rows([site[0:4, :], new[0:3]]).T
        terms(True)

    side = lax.broadcasted_iota(jnp.int32, (2, 128), 0)
    for l in range(listed):
        owner, part = blocks[l] >> 1, blocks[l] & 1
        for axis in range(3):
            spread[3 * owner + axis] += jnp.where(side == part, term[l, axis : axis + 1, :], 0.0)


def gather_kernel(pieces, share):
    total = jnp.sum(pieces[...], axis=0)
    share[...] = jnp.concatenate(
        [jnp.concatenate([total[axis, 0:1], total[axis, 1:2]], axis=1) for axis in range(3)], axis=0
    )


def finish_kernel(result, share, result_far, share_far, done):
    fetch(((result, result_far), (share, share_far)), done)()


def placed(block):
    y_half, plane, step, side = block // 64, block // 8 % 8, block // 2 % 4, block % 2
    x = 3 - step if plane % 2 else step
    z = (plane - 1) % 8 if y_half else plane
    along = 1 - side if (step + y_half) % 2 == 0 else side
    y = 2 * y_half + along
    return ((y % 2 * 8 + z) * 4 + x) * 2 + y // 2


def local(
    positions, charges, polar, features, neighbours, send_rows, blocks,
    radial_in, radial_mid, radial_out, node_in, node_out, field_gain, readout,
):
    width = positions.shape[1]
    slot_count = neighbours.shape[1]
    depth = 2 * width
    half = send_rows.shape[1]
    channels = features.shape[1]
    listed = blocks.shape[0]
    members = lax.axis_size(DOM)
    near_pairs = [(i, i ^ 1) for i in range(members)]
    far_pairs = [(i, ((i - 1) ^ 1) + 1) for i in range(1, members - 1)]
    same = list(range(members))
    place = [placed(i) for i in range(members)]

    def move(value, pairs, source, target, groups=(0, 1)):
        return lax.ppermute(
            value, EVERY, [(source[a] + g * members, target[b] + g * members) for g in groups for a, b in pairs]
        )

    def trade(a, b, groups=(0, 1), source=place):
        return move(a, near_pairs, source, place, groups), move(b, far_pairs, source, place, groups)

    row8, table8 = ((8, width), F32), ((8, half), F32)
    wide = ((channels, half), BF16)
    by_site = ((channels, width), BF16)
    ints = jnp.int32
    itself = [(i, i) for i in range(members)]
    pack, mine, lent_a, lent_b = call(
        rows_kernel, [((slot_count + 16, width), F32), ((2, 4, half), F32), table8, table8],
        (), (positions, charges[None], polar[None], neighbours.T, send_rows, blocks),
        [pltpu.VMEM((3, width), F32), pltpu.VMEM((1, width), F32), pltpu.VMEM((1, width), F32),
         pltpu.VMEM((slot_count, width), ints), pltpu.VMEM((2, half), ints), pltpu.SMEM((listed,), ints)], 6,
    )
    partner = lax.ppermute(mine, "grp", [(0, 1), (1, 0)])
    copies = jnp.broadcast_to(partner[None], (members,) + partner.shape)
    near = lax.all_to_all(copies, DOM, 0, 0, tiled=True).reshape(2 * members, 4, half)
    pack = move(pack, itself, same, place)
    rim_a, rim_b = trade(lent_a, lent_b, source=same)
    features = move(features, itself, same, place, (0,))
    feat_t, w3, w5, fixed, entry, lent_a, lent_b = call(
        static_kernel, [by_site, ((depth, width), F32), ((depth, width), F32), row8, ((depth, 8), F32), wide, wide],
        (pack, rim_a, rim_b), (features,), [pltpu.VMEM((width, channels), BF16)], 1, loose=1,
    )
    side_a, side_b = trade(lent_a, lent_b)
    third_shape = (LAYERS * radial_in.shape[2], slot_count * width)
    (third,) = call(
        radial_kernel, [(third_shape, BF16)], (pack, rim_a, rim_b), (radial_in, radial_mid),
        [pltpu.VMEM(radial_in.shape, BF16), pltpu.VMEM(radial_mid.shape, BF16), pltpu.VMEM(third_shape, BF16)],
        2 + slot_count // RADIAL_SLOTS, 1,
    )
    moment = pltpu.VMEM((depth, 8), F32)
    total = pltpu.VMEM((channels, width), F32)
    square = pltpu.VMEM(node_out.shape[1:], BF16)
    last = pltpu.VMEM(radial_out.shape[1:], BF16)
    outside_row, near_own, hidden, lifted, fixed_all, dipole, lent_a, lent_b = call(
        first_kernel, [row8, ((listed, 4, half), F32), by_site, by_site, row8, row8, wide, wide],
        (pack, rim_a, rim_b, feat_t, side_a, side_b, w3, w5, fixed, entry),
        (near, third, node_in, node_out, radial_out, field_gain[None]),
        [pltpu.VMEM((3 * listed, 4, half), F32), pltpu.VMEM((3 * listed * half, 8), F32),
         pltpu.VMEM(third_shape, BF16), pltpu.VMEM(node_in.shape, BF16), square, last,
         pltpu.VMEM((1, channels), F32), total, moment], 5 + 3 * listed, loose=1,
    )
    side_a, side_b = trade(lent_a, lent_b)
    charge, dipole, small_a, small_b = call(
        second_kernel, [row8, row8, table8, table8],
        (hidden, lifted, side_a, side_b, pack, w3, w5, fixed_all, dipole, entry),
        (third, node_out, radial_out, readout.T),
        [pltpu.VMEM(third_shape, BF16), square, last, pltpu.VMEM((2, channels), BF16), total, moment], 4,
    )
    side_a, side_b = trade(small_a, small_b, (1,))
    dipole, small_a, small_b = call(
        third_kernel, [row8, table8, table8], (side_a, side_b, pack, w3, w5, fixed_all, dipole, entry),
        (), [moment],
    )
    side_a, side_b = trade(small_a, small_b, (1,))
    result, spread = call(
        response_kernel, [((3, width), F32), ((3 * members, 2, half), F32)],
        (near_own, pack, charge, outside_row, side_a, side_b, w3, w5, fixed_all, dipole, entry), (),
        [pltpu.VMEM((width, 8), F32), moment, pltpu.VMEM((listed, 4, half), F32)],
    )
    pieces = lax.all_to_all(spread, DOM, 0, 0, tiled=True).reshape(members, 3, 2, half)
    (share,) = call(gather_kernel, [((3, width), F32)], (pieces,))
    result = move(result, itself, place, same)
    share = lax.ppermute(share, "grp", [(0, 1), (1, 0)])
    whole = ((3, width), F32)
    return tuple(call(finish_kernel, [whole, whole], (result, share), copies=2, far_outs=2))


def solution(mesh):
    sites = P(None, EVERY)
    in_specs = (sites, P(EVERY), P(EVERY), P(EVERY, None), P(EVERY, None), sites, P(EVERY)) + (P(),) * 7
    return jax.shard_map(local, mesh=mesh, in_specs=in_specs, out_specs=(sites, sites), check_vma=False)
```
